32 devices in a mesh: dp: 8 (over z, x), seq: 4 (over y, core).
Axes of the slice: x: 2, y: 2, z: 4, core: 2. Of those that a mesh axis runs over, the one named last changes fastest.
Arguments:
- hidden_in: bfloat16 [8192, 2048], P(('dp', 'seq')), may hold values from -6 to 6
- cotangent: bfloat16 [8192, 2048], P(('dp', 'seq')), may hold values from -6 to 6
- gain_attn: bfloat16 [2048], P('dp'), may hold values from 0.099609375 to 1.8984375
- w_query: bfloat16 [2048, 2048], P('dp'), may hold values from -0.125 to 0.125
- w_key: bfloat16 [2048, 256], P('dp'), may hold values from -0.125 to 0.125
- w_value: bfloat16 [2048, 256], P('dp'), may hold values from -0.125 to 0.125
- w_out: bfloat16 [2048, 2048], P(None, 'dp'), may hold values from -0.5 to 0.5
- gain_mlp: bfloat16 [2048], P('dp'), may hold values from 0.099609375 to 1.8984375
- w_gate: bfloat16 [2048, 5632], P('dp'), may hold values from -0.125 to 0.125
- w_up: bfloat16 [2048, 5632], P('dp'), may hold values from -0.125 to 0.125
- w_down: bfloat16 [5632, 2048], P(None, 'dp'), may hold values from -0.15625 to 0.15625
- doc_lengths: int32 [8, 6], P('dp'), may hold values from 0 to 1024, as said below
- valid_count: int32 [8], P('dp'), may hold values from 512 to 1024, as said below
Outputs:
- hidden_out: bfloat16 [8192, 2048], P(('dp', 'seq'))
- grad_in: bfloat16 [8192, 2048], P(('dp', 'seq'))
- grad_gain_attn: float32 [2048], P('dp')
- grad_query: float32 [2048, 2048], P('dp')
- grad_key: float32 [2048, 256], P('dp')
- grad_value: float32 [2048, 256], P('dp')
- grad_out: float32 [2048, 2048], P(None, 'dp')
- grad_gain_mlp: float32 [2048], P('dp')
- grad_gate: float32 [2048, 5632], P('dp')
- grad_up: float32 [2048, 5632], P('dp')
- grad_down: float32 [5632, 2048], P(None, 'dp')
The draws below stay inside these ranges and needn't reach their ends.
Inputs may be any that keep to these rules, and one draw needn't show every extreme that they name: `valid_count`: in every draw at least one pack has no padding. `doc_lengths`: the 6 lengths of a pack add up to 1024; a pack is either 6 documents of one token or more, or one whole document of 1024 tokens followed by empty slots, and every draw has at least one whole pack.
All inputs are finite; a program needn't handle non-finite values.
Results may differ from the reference program's by a relative error of at most 0.02.
Values may be sent and summed in bfloat16 or wider, within the bound.
No kernel may reach another device: no remote copies, remote signals or barrier semaphores. Data moves between devices by JAX's collectives and lax.ppermute only.
A program may use at most 384 MiB of HBM per device.

```python
import jax
import jax.numpy as jnp
from jax import lax

D = 2048
FF = 5632
HEADS = 32
HD = 64
KVH = 4
NSEG = 6
PACK = 1024
GROUPS = 8
TOKENS = 8192
BLOCK = 512
N_DP = 8


def draw_valid_count(key, part):
    counts_base = jax.random.randint(jax.random.fold_in(key, 11), (GROUPS,), PACK // 2, PACK + 1)
    full_pack = jax.random.randint(jax.random.fold_in(key, 12), (), 0, GROUPS)
    return counts_base.at[full_pack].set(PACK).astype(jnp.int32)


def draw_doc_lengths(key, part):

    def one_row(row_key):
        picked = jax.random.permutation(row_key, PACK - 1)[:NSEG - 1] + 1
        cuts = jnp.sort(picked).astype(jnp.int32)
        edges = jnp.concatenate([jnp.zeros((1,), jnp.int32), cuts, jnp.full((1,), PACK, jnp.int32)])
        return (edges[1:] - edges[:-1]).astype(jnp.int32)
    mixed_rows = jax.vmap(one_row)(jax.random.split(jax.random.fold_in(key, 21), GROUPS))
    whole_pick = jax.random.randint(jax.random.fold_in(key, 22), (GROUPS,), 0, 4) == 0
    forced = jax.random.randint(jax.random.fold_in(key, 23), (), 0, GROUPS)
    whole_pick = whole_pick | (jnp.arange(GROUPS, dtype=jnp.int32) == forced)
    single_row = jnp.zeros((NSEG,), jnp.int32).at[0].set(PACK)
    return jnp.where(whole_pick[:, None], single_row[None, :], mixed_rows).astype(jnp.int32)


def spiked(drawn, key, source, target, shards_of, factor):
    owner, partner = [(jnp.arange(drawn.shape[position]) // (drawn.shape[position] // shards_of)).reshape([-1 if axis == position else 1 for axis in range(drawn.ndim)]) for position in (source, target)]
    chosen = jax.random.permutation(key, shards_of)[partner]
    strong = (owner == chosen) | (owner == (partner + shards_of // 2) % shards_of)
    return jnp.where(strong, factor * drawn, drawn)


def shard_levels(key, dims, cuts, low, high):
    loudness, own = 1.0, jax.random.fold_in(key, 6)
    for position, parts in cuts:
        steps = jnp.exp(jax.random.uniform(jax.random.fold_in(own, position), (parts,), jnp.float32, low / len(cuts), high / len(cuts)))
        loudness = loudness * jnp.repeat(steps, dims[position] // parts).reshape([-1 if axis == position else 1 for axis in range(len(dims))])
    return loudness


def scatter_about(own_key, shape, deviation, limit, cuts=(), kind=jnp.bfloat16):
    drawn = jax.random.normal(own_key, shape, jnp.float32) * deviation
    if len(cuts) > 0:
        drawn = shard_levels(own_key, shape, cuts, -0.22, 0.18) * drawn
    return jnp.clip(drawn, min=-limit, max=limit).astype(kind)


def bell_draw_with(key, extent, scale, limit, cuts, heavy, held_as=jnp.bfloat16):
    entries = scale * jax.random.normal(key, extent, jnp.float32)
    if cuts:
        entries = entries * shard_levels(key, extent, cuts, -0.22, 0.18)
    return jnp.clip(spiked(entries, jax.random.fold_in(key, 3), *heavy), -limit, limit).astype(held_as)


def setup_inputs(seed: int = 0) -> dict:
    arg_keys = jax.random.split(jax.random.key(seed), 14)
    hidden_in = bell_draw_with(arg_keys[0], (TOKENS, D), 1.0, 6.0, ((0, 32),), (0, 1, 32, 2.75))
    cotangent = scatter_about(arg_keys[1], (TOKENS, D), 1.0, 6.0, ((0, 32),))
    gain_attn = jnp.clip(1.0 + 0.18 * jax.random.normal(arg_keys[2], (D,), jnp.float32), 0.099609375, 1.8984375).astype(jnp.bfloat16)
    w_query = scatter_about(arg_keys[3], (D, D), D ** -0.5, 0.125, ((0, 8),))
    w_key = scatter_about(arg_keys[4], (D, KVH * HD), D ** -0.5, 0.125, ((0, 8),))
    w_value = scatter_about(arg_keys[5], (D, KVH * HD), D ** -0.5, 0.125, ((0, 8),))
    w_out = scatter_about(arg_keys[6], (D, D), (D // 16) ** -0.5, 0.5, ((1, 8),))
    gain_mlp = jnp.clip(1.0 + 0.18 * jax.random.normal(arg_keys[7], (D,), jnp.float32), 0.099609375, 1.8984375).astype(jnp.bfloat16)
    w_gate = scatter_about(arg_keys[8], (D, FF), D ** -0.5, 0.125, ((0, 8),))
    w_up = scatter_about(arg_keys[9], (D, FF), D ** -0.5, 0.125, ((0, 8),))
    w_down = scatter_about(arg_keys[10], (FF, D), (FF // 4) ** -0.5, 0.15625, ((1, 8),))
    doc_lengths = draw_doc_lengths(jax.random.fold_in(arg_keys[13], 71), 0)
    valid_count = draw_valid_count(jax.random.fold_in(arg_keys[13], 71), 0)
    return {"hidden_in": hidden_in, "cotangent": cotangent, "gain_attn": gain_attn, "w_query": w_query, "w_key": w_key, "w_value": w_value, "w_out": w_out, "gain_mlp": gain_mlp, "w_gate": w_gate, "w_up": w_up, "w_down": w_down, "doc_lengths": doc_lengths, "valid_count": valid_count}


epsilon = 1e-05

@jax.custom_vjp
def low(v):
    return lax.optimization_barrier(v.astype(jnp.bfloat16)).astype(jnp.float32)

@jax.custom_vjp
def low_back(v):
    return v

def low_keep(v):
    return (low(v), None)

def low_pass(kept, grad):
    return (grad,)

def back_keep(v):
    return (v, None)

def back_low(kept, grad):
    return (low(grad),)
low.defvjp(low_keep, low_pass)
low_back.defvjp(back_keep, back_low)

def matmul_high(left_side, right_side):
    return jnp.dot(left_side, right_side, precision=lax.Precision.HIGHEST)

def doc_layout(lengths, pack_size):
    doc_ends = jnp.cumsum(lengths).astype(jnp.int32)
    doc_starts = (doc_ends - lengths).astype(jnp.int32)
    places = jnp.arange(pack_size, dtype=jnp.int32)
    segment = lax.optimization_barrier(jnp.sum((places[:, None] >= doc_ends[None, :]).astype(jnp.int32), axis=1)).astype(jnp.int32)
    doc_first = lax.optimization_barrier(jnp.max(jnp.where(places[:, None] >= doc_starts[None, :], doc_starts[None, :], 0), axis=1))
    return (segment, (places - doc_first).astype(jnp.int32))

def rotary_tables(positions):
    half_dim = HD // 2
    frequency = 10000.0 ** (-2.0 * jnp.arange(half_dim, dtype=jnp.float32) / HD)
    angle_table = positions.astype(jnp.float32)[:, None] * frequency[None, :]
    return (jnp.cos(angle_table), jnp.sin(angle_table))

def rotate(values, cosine, sine_part, head_count):
    row_count = values.shape[0]
    shaped = values.reshape(row_count, head_count, -1)
    half_dim = shaped.shape[2] // 2
    first_half = shaped[:, :, :half_dim]
    second = shaped[:, :, half_dim:]
    cos_rows = cosine[:, None, :]
    sin_rows = sine_part[:, None, :]
    turned = jnp.concatenate([first_half * cos_rows - second * sin_rows, second * cos_rows + first_half * sin_rows], axis=2)
    return turned.reshape(row_count, -1)

def mask_block(begin_row, block_rows, segment, live_count):
    key_ids = jnp.arange(segment.shape[0], dtype=jnp.int32)
    row_ids = begin_row + jnp.arange(block_rows, dtype=jnp.int32)
    row_seg = lax.dynamic_slice_in_dim(segment, begin_row, block_rows)
    same_doc = row_seg[:, None] == segment[None, :]
    causal = key_ids[None, :] <= row_ids[:, None]
    not_padded = (key_ids[None, :] < live_count) | (key_ids[None, :] == row_ids[:, None])
    return same_doc & causal & not_padded

def attention(queries, keys_rot, values, segment, live_count):
    pack_size = queries.shape[0]
    groups = HEADS // KVH
    query4 = queries.reshape(pack_size, KVH, groups, HD)
    key3 = keys_rot.reshape(pack_size, KVH, HD)
    value3 = values.reshape(pack_size, KVH, HD)

    def score_block(begin_row):
        query_block = lax.dynamic_slice_in_dim(query4, begin_row, BLOCK, 0)
        scores = jnp.einsum('bkgd,tkd->kgbt', query_block, key3, precision=lax.Precision.HIGHEST) * HD ** (-0.5)
        scores = low_back(scores)
        permit = mask_block(begin_row, BLOCK, segment, live_count)
        scores = jnp.where(permit[None, None], scores, -1e+30)
        row_peak = lax.optimization_barrier(jnp.max(scores, axis=-1, keepdims=True))
        exponent = jnp.exp(scores - row_peak)
        probs = exponent / lax.optimization_barrier(jnp.sum(exponent, axis=-1, keepdims=True))
        mixed = jnp.einsum('kgbt,tkd->bkgd', low(probs), value3, precision=lax.Precision.HIGHEST)
        return mixed.reshape(BLOCK, HEADS * HD)
    block_starts = jnp.arange(pack_size // BLOCK, dtype=jnp.int32) * BLOCK
    return lax.map(jax.checkpoint(score_block), block_starts).reshape(pack_size, HEADS * HD)

def residual_block(inputs, params, segment, positions, live_count):
    gain_one, query_w, key_w, value_w, out_w, gain_two, gate_w, up_w, down_w = params
    inverse_one = lax.rsqrt(lax.optimization_barrier(jnp.mean(inputs * inputs, axis=1, keepdims=True)) + epsilon)
    normed_one = low(inputs * inverse_one * gain_one)
    cosine, sine_part = rotary_tables(positions)
    queries = low_back(low(rotate(low_back(matmul_high(normed_one, query_w)), cosine, sine_part, HEADS)))
    keys_rot = low_back(low(rotate(low_back(matmul_high(normed_one, key_w)), cosine, sine_part, KVH)))
    values = low_back(low(matmul_high(normed_one, value_w)))
    mixed = low_back(low(attention(queries, keys_rot, values, segment, live_count)))
    hidden = inputs + low_back(matmul_high(mixed, out_w))
    inverse_two = lax.rsqrt(lax.optimization_barrier(jnp.mean(hidden * hidden, axis=1, keepdims=True)) + epsilon)
    normed_two = low(hidden * inverse_two * gain_two)
    gate_pre = low_back(matmul_high(normed_two, gate_w))
    up_pre = low_back(matmul_high(normed_two, up_w))
    hidden_act = low(gate_pre * jax.nn.sigmoid(gate_pre) * up_pre)
    return hidden + matmul_high(hidden_act, down_w)

def reference(hidden_in, cotangent, gain_attn, w_query, w_key, w_value, w_out, gain_mlp, w_gate, w_up, w_down, doc_lengths, valid_count):
    params = tuple((weight.astype(jnp.float32) for weight in (gain_attn, w_query, w_key, w_value, w_out, gain_mlp, w_gate, w_up, w_down)))
    packs_in = hidden_in.astype(jnp.float32).reshape(N_DP, PACK, D)
    packs_cot = cotangent.astype(jnp.float32).reshape(N_DP, PACK, D)

    def one_pack(running, pack_item):
        inputs, cot_pack, lengths, live_count = pack_item
        segment, positions = doc_layout(lengths, PACK)

        def forward(inputs_f, *weights):
            return residual_block(inputs_f, weights, segment, positions, live_count)
        result, pullback = jax.vjp(forward, inputs, *params)
        gradients = pullback(cot_pack)
        updated = tuple((total + grad_part for total, grad_part in zip(running, gradients[1:])))
        return (updated, (result.astype(jnp.bfloat16), gradients[0].astype(jnp.bfloat16)))
    zero_grads = tuple((jnp.zeros(weight.shape, jnp.float32) for weight in params))
    totals, (outputs_bf, input_grads) = lax.scan(one_pack, zero_grads, (packs_in, packs_cot, doc_lengths, valid_count))
    return (outputs_bf.reshape(TOKENS, D), input_grads.reshape(TOKENS, D), totals[0], totals[1], totals[2], totals[3], totals[4], totals[5], totals[6], totals[7], totals[8])
```

```python
import jax
import jax.numpy as jnp
from jax import lax
from jax.sharding import PartitionSpec as P

HEADS = 32
HD = 64
KVH = 4
EPS = 1e-05
BF = jnp.bfloat16
F32 = jnp.float32


class Ring:
    def __init__(self, size):
        self.size = size
        self.half = size // 2
        self.order = list(range(0, size, 2)) + list(range(size - 1, 0, -2))
        place = [0] * size
        for position, device in enumerate(self.order):
            place[device] = position
        self.place = place
        walk = [(self.order[i], self.order[(i + 1) % size]) for i in range(size)]
        self.up = walk
        self.down = [(b, a) for a, b in walk]
        self.steps = (
            [-t for t in range(self.half)] + [t for t in range(1, self.half)] + [self.half]
        )

    def slot_owners(self):
        mine = jnp.asarray(self.place, jnp.int32)[lax.axis_index("dp")]
        wanted = (mine + jnp.asarray(self.steps, jnp.int32)) % self.size
        return jnp.asarray(self.order, jnp.int32)[wanted]

    def owner_slots(self):
        mine = jnp.asarray(self.place, jnp.int32)[lax.axis_index("dp")]
        slot_of_step = [0] * self.size
        for slot, step in enumerate(self.steps):
            slot_of_step[step % self.size] = slot
        step = (jnp.asarray(self.place, jnp.int32) - mine) % self.size
        return jnp.asarray(slot_of_step, jnp.int32)[step]

    def gather(self, block):
        rows = block.shape[0] // 2
        from_down, from_up = [block], [block]
        for _ in range(1, self.half):
            from_down.append(lax.ppermute(from_down[-1], "dp", self.up))
            from_up.append(lax.ppermute(from_up[-1], "dp", self.down))
        last = jnp.concatenate(
            [
                lax.ppermute(from_down[-1][:rows], "dp", self.up),
                lax.ppermute(from_up[-1][rows:], "dp", self.down),
            ],
            axis=0,
        )
        return from_down + from_up[1:] + [last]

    def scatter(self, term, add_to):
        far = term(self.size - 1)
        rows = far.shape[0] // 2
        going_up, going_down = far[:rows].astype(BF), far[rows:].astype(BF)
        for step in range(self.half - 1, 0, -1):
            going_up = lax.ppermute(going_up, "dp", self.up)
            going_down = lax.ppermute(going_down, "dp", self.down)
            up_term = term(self.half - 1 + step)
            down_term = term(step)
            if step == self.half - 1:
                going_up = jnp.concatenate(
                    [(up_term[:rows] + going_up).astype(BF), up_term[rows:].astype(BF)], axis=0
                )
                going_down = jnp.concatenate(
                    [down_term[:rows].astype(BF), (down_term[rows:] + going_down).astype(BF)], axis=0
                )
            else:
                going_up = (up_term + going_up).astype(BF)
                going_down = (down_term + going_down).astype(BF)
        going_up = lax.ppermute(going_up, "dp", self.up)
        going_down = lax.ppermute(going_down, "dp", self.down)
        return term(0) + going_up + going_down


def swap(block, distance, size):
    return lax.ppermute(block, "seq", [(i, i ^ distance) for i in range(size)])


def seq_gather(block, size):
    blocks = [block]
    distance = size // 2
    held = {0: block}
    while distance >= 1:
        for offset in list(held):
            held[offset ^ distance] = swap(held[offset], distance, size)
        distance //= 2
    blocks = [held[offset] for offset in range(size)]
    return blocks


def seq_scatter(parts, size):
    parts = list(parts)
    distance = 1
    held = {offset: parts[offset] for offset in range(size)}
    while distance < size:
        keep = {}
        for offset in held:
            if offset & distance:
                continue
            got = swap(held[offset | distance].astype(BF), distance, size)
            keep[offset] = held[offset].astype(F32) + got.astype(F32)
        held = keep
        distance *= 2
    return held[0]


def doc_layout(lengths, pack_size):
    doc_ends = jnp.cumsum(lengths)
    doc_starts = doc_ends - lengths
    places = jnp.arange(pack_size, dtype=jnp.int32)
    segment = jnp.sum((places[:, None] >= doc_ends[None, :]).astype(jnp.int32), axis=1)
    doc_first = jnp.max(
        jnp.where(places[:, None] >= doc_starts[None, :], doc_starts[None, :], 0), axis=1
    )
    return (segment, places - doc_first)


def rotary_tables(positions):
    half_dim = HD // 2
    frequency = 10000.0 ** (-2.0 * jnp.arange(half_dim, dtype=F32) / HD)
    angle_table = positions.astype(F32)[:, None] * frequency[None, :]
    return (jnp.cos(angle_table), jnp.sin(angle_table))


def rotate(values, cosine, sine_part):
    row_count = values.shape[0]
    shaped = values.reshape(row_count, -1, HD)
    half_dim = HD // 2
    first_half = shaped[:, :, :half_dim]
    second = shaped[:, :, half_dim:]
    cos_rows = cosine[:, None, :]
    sin_rows = sine_part[:, None, :]
    turned = jnp.concatenate(
        [first_half * cos_rows - second * sin_rows, second * cos_rows + first_half * sin_rows],
        axis=2,
    )
    return turned.reshape(row_count, -1)


def mask_block(begin_row, block_rows, segment, live_count):
    key_ids = jnp.arange(segment.shape[0], dtype=jnp.int32)
    row_ids = begin_row + jnp.arange(block_rows, dtype=jnp.int32)
    row_seg = lax.dynamic_slice_in_dim(segment, begin_row, block_rows)
    same_doc = row_seg[:, None] == segment[None, :]
    causal = key_ids[None, :] <= row_ids[:, None]
    not_padded = (key_ids[None, :] < live_count) | (key_ids[None, :] == row_ids[:, None])
    return same_doc & causal & not_padded


def dot(left_side, right_side):
    return jnp.dot(left_side, right_side, preferred_element_type=F32)


def cross(left_side, right_side):
    return lax.dot_general(
        left_side, right_side, (((0,), (0,)), ((), ())), preferred_element_type=F32
    )


def against(left_side, right_side):
    return lax.dot_general(
        left_side, right_side, (((1,), (1,)), ((), ())), preferred_element_type=F32
    )


def rms_back(grad_normed, values, inverse, gain_vec):
    scaled = grad_normed * gain_vec
    return inverse * (
        scaled - values * inverse * inverse * jnp.mean(scaled * values, axis=1, keepdims=True)
    )


def masked_scores(query_block, key3, begin_row, block_rows, segment, live_count):
    scores = jnp.einsum(
        "bkgd,tkd->kgbt", query_block, key3, preferred_element_type=F32
    ) * HD ** (-0.5)
    permit = mask_block(begin_row, block_rows, segment, live_count)
    return jnp.where(permit[None, None], scores, -1e30)


def attention_forward(query4, key3, value3, segment, live_count, block_rows):
    pack_size = query4.shape[0]

    def attend(begin_row):
        query_block = lax.dynamic_slice_in_dim(query4, begin_row, block_rows, 0)
        scores = masked_scores(query_block, key3, begin_row, block_rows, segment, live_count)
        row_peak = jnp.max(scores, axis=-1, keepdims=True)
        exponent = jnp.exp(scores - row_peak)
        row_total = jnp.sum(exponent, axis=-1, keepdims=True)
        weights = (exponent / row_total).astype(BF)
        mixed = jnp.einsum("kgbt,tkd->bkgd", weights, value3, preferred_element_type=F32)
        return (mixed.reshape(block_rows, -1).astype(BF), row_peak + jnp.log(row_total))

    block_starts = jnp.arange(pack_size // block_rows, dtype=jnp.int32) * block_rows
    mixed_blocks, log_totals = lax.map(attend, block_starts)
    return (mixed_blocks.reshape(pack_size, -1), log_totals, block_starts)


def attention_backward(
    query4, key3, value3, grad4, block_starts, log_totals, segment, live_count, block_rows
):
    pack_size = query4.shape[0]
    score_scale = HD ** (-0.5)

    def attend_back(running, block_item):
        begin_row, log_total = block_item
        key_acc, value_acc = running
        query_block = lax.dynamic_slice_in_dim(query4, begin_row, block_rows, 0)
        grad_block = lax.dynamic_slice_in_dim(grad4, begin_row, block_rows, 0)
        scores = masked_scores(query_block, key3, begin_row, block_rows, segment, live_count)
        probs = jnp.exp(scores - log_total)
        weights = probs.astype(BF)
        grad_probs = jnp.einsum("bkgd,tkd->kgbt", grad_block, value3, preferred_element_type=F32)
        inner_sum = jnp.sum(probs * grad_probs, axis=-1, keepdims=True)
        grad_scores = (probs * (grad_probs - inner_sum)).astype(BF)
        grad_query_block = (
            jnp.einsum("kgbt,tkd->bkgd", grad_scores, key3, preferred_element_type=F32)
            * score_scale
        )
        key_acc = (
            key_acc
            + jnp.einsum("kgbt,bkgd->tkd", grad_scores, query_block, preferred_element_type=F32)
            * score_scale
        )
        value_acc = value_acc + jnp.einsum(
            "kgbt,bkgd->tkd", weights, grad_block, preferred_element_type=F32
        )
        return ((key_acc, value_acc), grad_query_block.reshape(block_rows, -1).astype(BF))

    zero_acc = jnp.zeros(key3.shape, F32)
    (key_acc, value_acc), grad_query_blocks = lax.scan(
        attend_back, (zero_acc, zero_acc), (block_starts, log_totals)
    )
    return (
        grad_query_blocks.reshape(pack_size, -1),
        key_acc.reshape(pack_size, -1).astype(BF),
        value_acc.reshape(pack_size, -1).astype(BF),
    )


def take_blocks(array, order, axis, size):
    width = array.shape[axis] // size
    return jnp.concatenate(
        [lax.dynamic_slice_in_dim(array, order[i] * width, width, axis) for i in range(size)],
        axis=axis,
    )


def layer(
    hidden_in,
    cotangent,
    gain_attn,
    w_query,
    w_key,
    w_value,
    w_out,
    gain_mlp,
    w_gate,
    w_up,
    w_down,
    doc_lengths,
    valid_count,
):
    seq = lax.axis_size("seq")
    n_dp = lax.axis_size("dp")
    here = lax.axis_index("seq")
    ring = Ring(n_dp)
    rows = hidden_in.shape[0]
    pack_size = rows * seq
    width = gain_attn.shape[0]
    model = width * n_dp
    q_cols = w_query.shape[1] // seq
    k_cols = w_key.shape[1] // seq
    ff = w_gate.shape[1] // seq
    block_rows = min(512, pack_size)

    owners = ring.slot_owners()
    slots = ring.owner_slots()
    seq_order = here ^ jnp.arange(seq, dtype=jnp.int32)

    def part(array, axis, cols):
        return lax.dynamic_slice_in_dim(array, here * cols, cols, axis)

    def slot(array, j):
        return lax.slice_in_dim(array, j * width, (j + 1) * width, axis=1)

    gains = jnp.concatenate(
        [gain_attn, gain_mlp, jnp.zeros((q_cols + 2 * k_cols - 2 * width,), BF)]
    )
    head_block = jnp.concatenate(
        [
            jnp.concatenate(
                [part(w_query, 1, q_cols), part(w_key, 1, k_cols), part(w_value, 1, k_cols)], axis=1
            ),
            jnp.broadcast_to(gains[None], (16, gains.shape[0])),
        ],
        axis=0,
    )
    head_blocks = ring.gather(head_block)
    w_heads = jnp.concatenate([b[:width] for b in head_blocks], axis=0)
    gain_one = jnp.concatenate([b[width, :width] for b in head_blocks]).astype(F32)
    gain_two = jnp.concatenate([b[width, width : 2 * width] for b in head_blocks]).astype(F32)
    w_out_all = jnp.concatenate(ring.gather(part(w_out, 0, q_cols)), axis=1)
    my_gate, my_up, my_down = part(w_gate, 1, ff), part(w_up, 1, ff), part(w_down, 0, ff)
    first = (ff // 2 + 127) // 128 * 128
    bounds = [(0, first), (first, ff)]
    w_gate_up, w_down_all = [], []
    for a, b in bounds:
        w_gate_up.append(
            jnp.concatenate(
                ring.gather(jnp.concatenate([my_gate[:, a:b], my_up[:, a:b]], axis=1)), axis=0
            )
        )
        w_down_all.append(jnp.concatenate(ring.gather(my_down[a:b]), axis=1))

    mine = take_blocks(hidden_in, owners, 1, n_dp)
    my_cot = take_blocks(cotangent, owners, 1, n_dp)
    inputs = jnp.concatenate(seq_gather(mine, seq), axis=0).astype(F32)
    cot = jnp.concatenate(seq_gather(my_cot, seq), axis=0)

    live_count = valid_count[0]
    segment, positions = doc_layout(doc_lengths[0], pack_size)
    cosine, sine_part = rotary_tables(take_blocks(positions, seq_order, 0, seq))

    inverse_one = lax.rsqrt(jnp.mean(inputs * inputs, axis=1, keepdims=True) + EPS)
    normed_one = (inputs * inverse_one * gain_one).astype(BF)
    heads_pre = dot(normed_one, w_heads)
    queries = rotate(heads_pre[:, :q_cols], cosine, sine_part).astype(BF)
    keys_rot = rotate(heads_pre[:, q_cols : q_cols + k_cols], cosine, sine_part).astype(BF)
    values = heads_pre[:, q_cols + k_cols :].astype(BF)

    def natural(array):
        return take_blocks(array, seq_order, 0, seq)

    kv_local = k_cols // HD
    query4 = natural(queries).reshape(pack_size, kv_local, -1, HD)
    key3 = natural(keys_rot).reshape(pack_size, kv_local, HD)
    value3 = natural(values).reshape(pack_size, kv_local, HD)
    mixed_nat, log_totals, block_starts = attention_forward(
        query4, key3, value3, segment, live_count, block_rows
    )
    mixed = natural(mixed_nat)

    def token_parts(array):
        return [array[j * rows : (j + 1) * rows] for j in range(seq)]

    branch = dot(mixed, w_out_all)
    my_inputs = mine.astype(F32)
    hidden = my_inputs + seq_scatter(token_parts(branch), seq)
    inverse_two = lax.rsqrt(jnp.mean(hidden * hidden, axis=1, keepdims=True) + EPS)
    my_normed_two = (hidden * inverse_two * gain_two).astype(BF)
    normed_two = jnp.concatenate(seq_gather(my_normed_two, seq), axis=0)

    down = 0.0
    grad_normed = 0.0
    gate_up_sums, down_sums = [], []
    for (a, b), gate_up_w, down_w in zip(bounds, w_gate_up, w_down_all):
        size = b - a
        both = dot(normed_two, gate_up_w)
        gate_pre, up_pre = both[:, :size], both[:, size:]
        sigmoid_gate = jax.nn.sigmoid(gate_pre)
        active = gate_pre * sigmoid_gate
        hidden_act = (active * up_pre).astype(BF)
        grad_act = against(cot, down_w)
        grad_up_pre = (grad_act * active).astype(BF)
        grad_gate_pre = (
            grad_act * up_pre * sigmoid_gate * (1.0 + gate_pre * (1.0 - sigmoid_gate))
        ).astype(BF)
        grad_both = jnp.concatenate([grad_gate_pre, grad_up_pre], axis=1)
        down = down + dot(hidden_act, down_w)
        grad_normed = grad_normed + against(grad_both, gate_up_w)
        gate_up_sums.append(
            ring.scatter(lambda j: cross(slot(normed_two, j), grad_both), None).astype(BF)
        )
        down_sums.append(ring.scatter(lambda j: cross(hidden_act, slot(cot, j)), None).astype(BF))

    result = (hidden + seq_scatter(token_parts(down), seq)).astype(BF)
    grad_normed_two = seq_scatter(token_parts(grad_normed), seq)
    term_gain_two = jnp.sum(grad_normed_two * hidden * inverse_two, axis=0)
    grad_hidden = my_cot.astype(F32) + rms_back(grad_normed_two, hidden, inverse_two, gain_two)
    my_grad_branch = grad_hidden.astype(BF)
    grad_branch = jnp.concatenate(seq_gather(my_grad_branch, seq), axis=0)
    out_sum = ring.scatter(lambda j: cross(mixed, slot(grad_branch, j)), None).astype(BF)
    grad_mixed = against(grad_branch, w_out_all).astype(BF)
    grad4 = natural(grad_mixed).reshape(query4.shape)
    grad_q, grad_k, grad_v = attention_backward(
        query4, key3, value3, grad4, block_starts, log_totals, segment, live_count, block_rows
    )
    grad_q_pre = rotate(natural(grad_q).astype(F32), cosine, -sine_part).astype(BF)
    grad_k_pre = rotate(natural(grad_k).astype(F32), cosine, -sine_part).astype(BF)
    grad_heads = jnp.concatenate([grad_q_pre, grad_k_pre, natural(grad_v)], axis=1)
    grad_normed_one = against(grad_heads, w_heads)
    term_gain_one = jnp.sum(grad_normed_one * inputs * inverse_one, axis=0)

    def head_term(j):
        gain_terms = jnp.concatenate(
            [
                term_gain_one[j * width : (j + 1) * width],
                term_gain_two[j * width : (j + 1) * width],
                jnp.zeros((q_cols + 2 * k_cols - 2 * width,), F32),
            ]
        )
        return jnp.concatenate(
            [
                cross(slot(normed_one, j), grad_heads),
                jnp.broadcast_to(gain_terms[None], (16, gain_terms.shape[0])),
            ],
            axis=0,
        )

    head_sum = ring.scatter(head_term, None).astype(BF)
    grad_input = (
        grad_hidden
        + rms_back(
            seq_scatter(token_parts(grad_normed_one), seq),
            my_inputs,
            inverse_one[:rows],
            gain_one,
        )
    ).astype(BF)

    def whole(array, axis):
        return take_blocks(
            jnp.concatenate(seq_gather(array, seq), axis=axis).astype(F32), seq_order, axis, seq
        )

    gate_sum = jnp.concatenate([g[:, : g.shape[1] // 2] for g in gate_up_sums], axis=1)
    up_sum = jnp.concatenate([g[:, g.shape[1] // 2 :] for g in gate_up_sums], axis=1)
    grad_gate, grad_up = whole(gate_sum, 1), whole(up_sum, 1)
    grad_down = whole(jnp.concatenate(down_sums, axis=0), 0)
    grad_out = whole(out_sum, 0)
    head_sums = seq_gather(head_sum, seq)
    gain_sum = sum(h[width, : 2 * width].astype(F32) for h in head_sums)

    def head_whole(begin, end):
        return take_blocks(
            jnp.concatenate([h[:width, begin:end] for h in head_sums], axis=1).astype(F32),
            seq_order,
            1,
            seq,
        )

    grad_query = head_whole(0, q_cols)
    grad_key = head_whole(q_cols, q_cols + k_cols)
    grad_value = head_whole(q_cols + k_cols, q_cols + 2 * k_cols)

    return (
        take_blocks(result, slots, 1, n_dp),
        take_blocks(grad_input, slots, 1, n_dp),
        gain_sum[:width],
        grad_query,
        grad_key,
        grad_value,
        grad_out,
        gain_sum[width:],
        grad_gate,
        grad_up,
        grad_down,
    )


def solution(mesh):
    return jax.shard_map(
        layer,
        mesh=mesh,
        in_specs=(
            P(("dp", "seq"), None),
            P(("dp", "seq"), None),
            P("dp"),
            P("dp", None),
            P("dp", None),
            P("dp", None),
            P(None, "dp"),
            P("dp"),
            P("dp", None),
            P("dp", None),
            P(None, "dp"),
            P("dp", None),
            P("dp"),
        ),
        out_specs=(
            P(("dp", "seq"), None),
            P(("dp", "seq"), None),
            P("dp"),
            P("dp", None),
            P("dp", None),
            P("dp", None),
            P(None, "dp"),
            P("dp"),
            P("dp", None),
            P("dp", None),
            P(None, "dp"),
        ),
        check_vma=False,
    )
```

```python
import functools

import jax
import jax.numpy as jnp
from jax import lax
from jax.experimental import pallas as pl
from jax.experimental.pallas import tpu as pltpu
from jax.sharding import PartitionSpec as P

HEADS = 32
HD = 64
KVH = 4
EPS = 1e-05
TOP = 16
BF = jnp.bfloat16
F32 = jnp.float32
NEG = -1e30
VMEM_LIMIT = 60 << 20


def dot(left_side, right_side):
    return jnp.dot(left_side, right_side, preferred_element_type=F32)


def cross(left_side, right_side):
    return lax.dot_general(
        left_side, right_side, (((0,), (0,)), ((), ())), preferred_element_type=F32
    )


def against(left_side, right_side):
    return lax.dot_general(
        left_side, right_side, (((1,), (1,)), ((), ())), preferred_element_type=F32
    )


def kernel_call(body, outs, scratch=(), flops=0, moved=0, smem=0, args=(), name=None):
    vmem = pl.BlockSpec(memory_space=pltpu.VMEM)
    return pl.pallas_call(
        body,
        out_shape=tuple(jax.ShapeDtypeStruct(s, d) for s, d in outs),
        in_specs=[pl.BlockSpec(memory_space=pltpu.SMEM)] * smem + [vmem] * (len(args) - smem),
        out_specs=tuple(vmem for _ in outs),
        scratch_shapes=list(scratch),
        compiler_params=pltpu.CompilerParams(vmem_limit_bytes=VMEM_LIMIT),
        cost_estimate=pl.CostEstimate(flops=int(flops), transcendentals=0, bytes_accessed=int(moved)),
        name=name,
    )(*args)


class Ring:
    def __init__(self, size):
        self.size = size
        self.half = size // 2
        self.order = list(range(0, size, 2)) + list(range(size - 1, 0, -2))
        place = [0] * size
        for position, device in enumerate(self.order):
            place[device] = position
        self.place = place
        walk = [(self.order[i], self.order[(i + 1) % size]) for i in range(size)]
        self.up = walk
        self.down = [(b, a) for a, b in walk]
        self.steps = (
            [-t for t in range(self.half)] + [t for t in range(1, self.half)] + [self.half]
        )

    def slot_owners(self):
        mine = jnp.asarray(self.place, jnp.int32)[lax.axis_index("dp")]
        wanted = (mine + jnp.asarray(self.steps, jnp.int32)) % self.size
        return jnp.asarray(self.order, jnp.int32)[wanted]

    def owner_slots(self):
        mine = jnp.asarray(self.place, jnp.int32)[lax.axis_index("dp")]
        slot_of_step = [0] * self.size
        for slot, step in enumerate(self.steps):
            slot_of_step[step % self.size] = slot
        step = (jnp.asarray(self.place, jnp.int32) - mine) % self.size
        return jnp.asarray(slot_of_step, jnp.int32)[step]

    def go_up(self, block):
        return lax.ppermute(block, "dp", self.up)

    def go_down(self, block):
        return lax.ppermute(block, "dp", self.down)

    def gather(self, block, cut):
        from_down, from_up = [block], [block]
        for _ in range(1, self.half):
            from_down.append(self.go_up(from_down[-1]))
            from_up.append(self.go_down(from_up[-1]))
        return (
            from_down
            + from_up[1:]
            + [self.go_up(from_down[-1][:cut]), self.go_down(from_up[-1][cut:])]
        )

    def scatter(self, far, step, last):
        up, down = far(self.size - 1)
        for t in range(self.half - 1, 0, -1):
            up, down = self.go_up(up), self.go_down(down)
            up, down = step(self.half - 1 + t, t, up, down)
        return last(self.go_up(up), self.go_down(down))


def swap(block, distance):
    return lax.ppermute(block, "seq", [(i, i ^ distance) for i in range(4)])


def seq_gather(block):
    near = jnp.concatenate([block, swap(block, 2)], axis=0)
    return near, swap(near, 1)


def seq_scatter(terms):
    half = terms.shape[0] // 2
    quarter = half // 2
    near = terms[:half].astype(F32) + swap(terms[half:], 1).astype(F32)
    return near[:quarter] + swap(near[quarter:].astype(BF), 2).astype(F32)


def fill_weights(pieces, scratch, top, width, columns):
    begin = 0
    for index, piece in enumerate(pieces):
        skip = top if index < len(pieces) - 1 else 0
        count = piece.shape[0] - skip
        scratch[begin : begin + count, :] = piece[skip:, columns]
        begin += count


def permute_features(arrays, order, size):
    rows, features = arrays[0].shape
    width = features // size
    if width % 128:
        return [
            jnp.concatenate(
                [lax.dynamic_slice_in_dim(a, order[i] * width, width, 1) for i in range(size)],
                axis=1,
            )
            for a in arrays
        ]

    def body(order_ref, *refs):
        count = len(refs) // 2
        for source, target in zip(refs[:count], refs[count:]):
            target[...] = source[...]

    return pl.pallas_call(
        body,
        out_shape=tuple(jax.ShapeDtypeStruct(a.shape, a.dtype) for a in arrays),
        grid_spec=pltpu.PrefetchScalarGridSpec(
            num_scalar_prefetch=1,
            grid=(size,),
            in_specs=[pl.BlockSpec((rows, width), lambda i, o: (0, o[i])) for _ in arrays],
            out_specs=tuple(pl.BlockSpec((rows, width), lambda i, o: (0, i)) for _ in arrays),
        ),
        name="permute_features",
    )(order, *arrays)


def pack_heads(here, w_query, w_key, w_value, w_out, gain_attn, gain_mlp, seq):
    width = w_query.shape[0]
    q_cols, k_cols = w_query.shape[1] // seq, w_key.shape[1] // seq
    total = 2 * q_cols + 2 * k_cols

    def body(here_ref, query_ref, key_ref, value_ref, out_ref, one_ref, two_ref, block_ref):
        s = here_ref[0]
        block_ref[:TOP, :] = jnp.zeros((TOP, total), BF)
        block_ref[:1, :width] = one_ref[...]
        block_ref[:1, width : 2 * width] = two_ref[...]
        block_ref[TOP:, :q_cols] = query_ref[...]

        def mine(ref):
            part = jnp.zeros((width, k_cols), F32)
            for place in range(seq):
                piece = ref[:, place * k_cols : (place + 1) * k_cols].astype(F32)
                part = jnp.where(s == place, piece, part)
            return part

        both = jnp.concatenate([mine(key_ref), mine(value_ref)], axis=1)
        block_ref[TOP:, q_cols : q_cols + 2 * k_cols] = both.astype(BF)
        block_ref[TOP:, q_cols + 2 * k_cols :] = out_ref[...].astype(F32).T.astype(BF)

    whole = lambda shape: pl.BlockSpec(shape, lambda i, o: (0, 0))
    return pl.pallas_call(
        body,
        out_shape=jax.ShapeDtypeStruct((TOP + width, total), BF),
        grid_spec=pltpu.PrefetchScalarGridSpec(
            num_scalar_prefetch=1,
            grid=(1,),
            in_specs=[
                pl.BlockSpec((width, q_cols), lambda i, o: (0, o[0])),
                whole(w_key.shape),
                whole(w_value.shape),
                pl.BlockSpec((q_cols, width), lambda i, o: (o[0], 0)),
                whole((1, width)),
                whole((1, width)),
            ],
            out_specs=whole((TOP + width, total)),
        ),
        name="pack_heads",
    )(here, w_query, w_key, w_value, w_out, gain_attn[None], gain_mlp[None])


def pack_mlp(here, w_gate, w_up, w_down, bounds, seq):
    width, ff = w_gate.shape[0], w_gate.shape[1] // seq

    def body(here_ref, gate_ref, up_ref, down_ref, *blocks):
        for (a, b), block in zip(bounds, blocks):
            size = b - a
            block[:, :size] = gate_ref[:, a:b]
            block[:, size : 2 * size] = up_ref[:, a:b]
            block[:, 2 * size :] = down_ref[a:b, :].astype(F32).T.astype(BF)

    columns = pl.BlockSpec((width, ff), lambda i, o: (0, o[0]))
    return pl.pallas_call(
        body,
        out_shape=tuple(jax.ShapeDtypeStruct((width, 3 * (b - a)), BF) for a, b in bounds),
        grid_spec=pltpu.PrefetchScalarGridSpec(
            num_scalar_prefetch=1,
            grid=(1,),
            in_specs=[columns, columns, pl.BlockSpec((ff, width), lambda i, o: (o[0], 0))],
            out_specs=tuple(
                pl.BlockSpec((width, 3 * (b - a)), lambda i, o: (0, 0)) for a, b in bounds
            ),
        ),
        name="pack_mlp",
    )(here, w_gate, w_up, w_down)


def turn(values, cosine, sine_part):
    half_dim = HD // 2
    pieces = []
    for h in range(values.shape[0] // HD):
        first = values[h * HD : h * HD + half_dim]
        second = values[h * HD + half_dim : (h + 1) * HD]
        pieces.append(first * cosine - second * sine_part)
        pieces.append(second * cosine + first * sine_part)
    return jnp.concatenate(pieces, axis=0)


def rounded(values):
    return values.astype(BF).astype(F32)


def token_block(near_ref, far_ref, place, rows):
    begin = pl.multiple_of((place % 2) * rows, rows)
    near = near_ref[pl.ds(begin, rows), :].astype(F32)
    far = far_ref[pl.ds(begin, rows), :].astype(F32)
    return jnp.where(place < 2, near, far)


def write_bias(bias_ref, lengths_ref, live, block, rows):
    keys = (block + 1) * rows
    query = lax.broadcasted_iota(jnp.int32, (1, rows), 1) + block * rows
    low = jnp.zeros((1, rows), jnp.int32)
    start = 0
    for slot in range(lengths_ref.shape[0]):
        low = jnp.where(query >= start, jnp.maximum(low, start), low)
        start = start + lengths_ref[slot]
    high = jnp.minimum(query, live - 1)
    key = lax.broadcasted_iota(jnp.int32, (keys, rows), 0)
    allowed = ((key >= low) & (key <= high)) | (key == query)
    bias_ref[:keys, :] = jnp.where(allowed, 0.0, NEG)


def attention_forward(places, lengths, live, near, far, pieces, cosine, sine_part, rows, q_cols):
    pack_size = 4 * rows
    model = near.shape[1]
    n_heads = q_cols // HD
    heads_cols = q_cols + 2 * HD
    width = pieces[0].shape[0] - TOP

    def body(places_ref, lengths_ref, live_ref, near_ref, far_ref, cos_ref, sin_ref, *refs):
        piece_refs, refs = refs[: len(pieces)], refs[len(pieces) :]
        (
            normed_ref, query_ref, kv_ref, kvt_ref, lse_ref, mixed_t_ref, mixed_ref, branch_ref,
            gains_ref, w_ref, bias_ref, query_s, mixed_s,
        ) = refs
        live_count = live_ref[0]
        fill_weights(piece_refs, w_ref, TOP, width, slice(None))
        gains_ref[...] = jnp.zeros_like(gains_ref)
        for index, piece in enumerate(piece_refs[:-1]):
            at = slice(index * width, (index + 1) * width)
            gains_ref[0:1, at] = piece[0:1, :width].astype(F32)
            gains_ref[1:2, at] = piece[0:1, width : 2 * width].astype(F32)
        ones = jnp.ones((HD, rows), BF)
        for block in range(4):
            place = places_ref[block]
            at = slice(block * rows, (block + 1) * rows)
            keys = (block + 1) * rows
            to = pl.ds(pl.multiple_of(place * rows, rows), rows)
            inputs = token_block(near_ref, far_ref, place, rows)
            inverse = lax.rsqrt(jnp.mean(inputs * inputs, axis=1, keepdims=True) + EPS)
            normed = (inputs * inverse * gains_ref[0:1, :]).astype(BF)
            normed_ref[to, :] = normed
            pre = dot(normed, w_ref[:, :heads_cols]).T
            cos_b, sin_b = cos_ref[:, at], sin_ref[:, at]
            query = (rounded(turn(pre[:q_cols], cos_b, sin_b)) * HD**-0.5).astype(BF)
            query_s[...] = query
            query_ref[:, at] = query
            key_t = rounded(turn(pre[q_cols : q_cols + HD], cos_b, sin_b))
            value_t = rounded(pre[q_cols + HD :])
            kv_t = jnp.concatenate([key_t, value_t], axis=0)
            kv_ref[at, :] = kv_t.T.astype(BF)
            kvt_ref[: 2 * HD, at] = kv_t.astype(BF)
            kvt_ref[2 * HD :, at] = ones
            write_bias(bias_ref, lengths_ref, live_count, block, rows)

            def attend(h, _):
                mine = pl.ds(pl.multiple_of(h * HD, HD), HD)
                scores = dot(kv_ref[:keys, :HD], query_s[mine, :]) + bias_ref[:keys, :]
                peak = jnp.max(scores, axis=0, keepdims=True)
                weights = jnp.exp(scores - peak).astype(BF)
                summed = dot(kvt_ref[HD:, :keys], weights)
                total = summed[HD : HD + 1]
                mixed = summed[:HD] * (1.0 / total)
                mixed_s[mine, :] = mixed
                lse_ref[pl.ds(h, 1), at] = peak + jnp.log(total)
                return 0

            lax.fori_loop(0, n_heads, attend, 0, unroll=2)
            mixed_t = mixed_s[...]
            mixed_t_ref[:, at] = mixed_t
            mixed = mixed_t.T.astype(BF)
            mixed_ref[to, :] = mixed
            branch_ref[to, :] = against(mixed, w_ref[:, heads_cols:]).astype(BF)

    args = [places, lengths, live, near, far, cosine, sine_part, *pieces]
    flops = 2 * pack_size * model * (heads_cols + q_cols) + 4 * n_heads * pack_size**2 * HD * 3
    return kernel_call(
        body,
        [
            ((pack_size, model), BF),
            ((q_cols, pack_size), BF),
            ((pack_size, 2 * HD), BF),
            ((3 * HD, pack_size), BF),
            ((n_heads, pack_size), F32),
            ((q_cols, pack_size), F32),
            ((pack_size, q_cols), BF),
            ((pack_size, model), BF),
            ((8, model), F32),
        ],
        scratch=[
            pltpu.VMEM((model, heads_cols + q_cols), BF),
            pltpu.VMEM((pack_size, rows), F32),
            pltpu.VMEM((q_cols, rows), BF),
            pltpu.VMEM((q_cols, rows), F32),
        ],
        flops=flops,
        moved=30 << 20,
        smem=3,
        args=args,
        name="attention_forward",
    )


def attention_backward(
    places, lengths, live, near, far, pieces, cosine, sine_part, query, kv, kvt, lse, mixed_t, rows
):
    q_cols, pack_size = query.shape
    model = near.shape[1]
    n_heads = q_cols // HD
    heads_cols = q_cols + 2 * HD
    width = pieces[0].shape[0] - TOP

    def body(
        places_ref, lengths_ref, live_ref, near_ref, far_ref, cos_ref, sin_ref,
        query_ref, kv_ref, kvt_ref, lse_ref, mixed_t_ref, *refs
    ):
        piece_refs, refs = refs[: len(pieces)], refs[len(pieces) :]
        grad_q_ref, grad_kv_ref, w_ref, bias_ref, grad_s, grad_q_s, key_acc, value_acc, inner_s = refs
        live_count = live_ref[0]
        fill_weights(piece_refs, w_ref, TOP, width, slice(heads_cols, heads_cols + q_cols))
        key_acc[...] = jnp.zeros_like(key_acc)
        value_acc[...] = jnp.zeros_like(value_acc)
        for block in range(4):
            place = places_ref[block]
            at = slice(block * rows, (block + 1) * rows)
            keys = (block + 1) * rows
            to = pl.ds(pl.multiple_of(place * rows, rows), rows)
            branch = token_block(near_ref, far_ref, place, rows).astype(BF)
            grad_t = rounded(dot(branch, w_ref[...]).T)
            grad_s[...] = grad_t.astype(BF)
            product = grad_t * mixed_t_ref[:, at]
            for h in range(n_heads):
                inner_s[h : h + 1, :] = jnp.sum(
                    product[h * HD : (h + 1) * HD], axis=0, keepdims=True
                )
            write_bias(bias_ref, lengths_ref, live_count, block, rows)

            def attend(h, _):
                mine = pl.ds(pl.multiple_of(h * HD, HD), HD)
                query_h = query_ref[mine, at]
                grad_h = grad_s[mine, :]
                scores = dot(kv_ref[:keys, :HD], query_h) + bias_ref[:keys, :]
                probs = jnp.exp(scores - lse_ref[pl.ds(h, 1), at])
                grad_probs = dot(kv_ref[:keys, HD:], grad_h)
                grad_scores = (probs * (grad_probs - inner_s[pl.ds(h, 1), :])).astype(BF)
                grad_q_s[mine, :] = dot(kvt_ref[:HD, :keys], grad_scores) * HD**-0.5
                key_acc[:keys, :] += against(grad_scores, query_h)
                value_acc[:keys, :] += against(probs.astype(BF), grad_h)
                return 0

            lax.fori_loop(0, n_heads, attend, 0, unroll=2)
            turned = turn(rounded(grad_q_s[...]), cos_ref[:, at], -sin_ref[:, at])
            grad_q_ref[to, :] = turned.T.astype(BF)
        for block in range(4):
            at = slice(block * rows, (block + 1) * rows)
            to = pl.ds(pl.multiple_of(places_ref[block] * rows, rows), rows)
            key_t = turn(rounded(key_acc[at, :]).T, cos_ref[:, at], -sin_ref[:, at])
            grad_kv_ref[to, :] = jnp.concatenate([key_t.T, value_acc[at, :]], axis=1).astype(BF)

    args = [
        places, lengths, live, near, far, cosine, sine_part, query, kv, kvt, lse, mixed_t, *pieces
    ]
    return kernel_call(
        body,
        [((pack_size, q_cols), BF), ((pack_size, 2 * HD), BF)],
        scratch=[
            pltpu.VMEM((model, q_cols), BF),
            pltpu.VMEM((pack_size, rows), F32),
            pltpu.VMEM((q_cols, rows), BF),
            pltpu.VMEM((q_cols, rows), F32),
            pltpu.VMEM((pack_size, HD), F32),
            pltpu.VMEM((pack_size, HD), F32),
            pltpu.VMEM((n_heads, rows), F32),
        ],
        flops=2 * pack_size * model * q_cols + 10 * n_heads * pack_size**2 * HD * 3,
        moved=20 << 20,
        smem=3,
        args=args,
        name="attention_backward",
    )


def heads_back(grad_q, grad_kv, near, far, pieces, rows):
    pack_size, q_cols = grad_q.shape
    model = near.shape[1]
    heads_cols = q_cols + 2 * HD
    width = pieces[0].shape[0] - TOP

    def body(grad_q_ref, grad_kv_ref, near_ref, far_ref, *refs):
        piece_refs, (grad_ref, gain_ref, w_ref) = refs[: len(pieces)], refs[len(pieces) :]
        fill_weights(piece_refs, w_ref, TOP, width, slice(0, heads_cols))
        total = jnp.zeros((1, model), F32)
        for block in range(4):
            at = slice(block * rows, (block + 1) * rows)
            source = near_ref if block < 2 else far_ref
            inputs = source[(block % 2) * rows : (block % 2 + 1) * rows, :].astype(F32)
            inverse = lax.rsqrt(jnp.mean(inputs * inputs, axis=1, keepdims=True) + EPS)
            grad = against(grad_q_ref[at, :], w_ref[:, :q_cols]) + against(
                grad_kv_ref[at, :], w_ref[:, q_cols:]
            )
            grad_ref[at, :] = grad.astype(BF)
            total = total + jnp.sum(grad * inputs * inverse, axis=0, keepdims=True)
        gain_ref[...] = jnp.broadcast_to(total, gain_ref.shape)

    args = [grad_q, grad_kv, near, far, *pieces]
    return kernel_call(
        body,
        [((pack_size, model), BF), ((8, model), F32)],
        scratch=[pltpu.VMEM((model, heads_cols), BF)],
        flops=2 * pack_size * model * heads_cols,
        moved=14 << 20,
        args=args,
        name="heads_back",
    )


def mlp_chunk(near, far, cot_near, cot_far, pieces, before, rows, size):
    model = near.shape[1]
    pack_size = 4 * rows
    n_in = 4 + len(pieces) + len(before)

    def body(near_ref, far_ref, cot_near_ref, cot_far_ref, *refs):
        piece_refs = refs[: len(pieces)]
        before_refs = refs[len(pieces) : n_in - 4]
        down_ref, grad_ref, both_ref, act_ref, w_ref = refs[n_in - 4 :]
        step = pl.program_id(0)

        @pl.when(step == 0)
        def _():
            fill_weights(piece_refs, w_ref, 0, model, slice(None))

        def work(normed, cot):
            both = dot(normed, w_ref[:, : 2 * size])
            grad_act = dot(cot, w_ref[:, 2 * size :])
            gate_pre, up_pre = both[:, :size], both[:, size:]
            sig = 1.0 / (1.0 + jnp.exp(-gate_pre))
            active = gate_pre * sig
            act = (active * up_pre).astype(BF)
            act_ref[...] = act
            grad_up = (grad_act * active).astype(BF)
            grad_gate = (grad_act * up_pre * (sig + active * (1.0 - sig))).astype(BF)
            both_ref[:, :size] = grad_gate
            both_ref[:, size:] = grad_up
            down = against(act, w_ref[:, 2 * size :])
            grad = against(both_ref[...], w_ref[:, : 2 * size])
            if before_refs:
                down = down + before_refs[0][...].astype(F32)
                grad = grad + before_refs[1][...].astype(F32)
            down_ref[...] = down.astype(BF)
            grad_ref[...] = grad.astype(BF)

        @pl.when(step < 2)
        def _():
            work(near_ref[...], cot_near_ref[...])

        @pl.when(step >= 2)
        def _():
            work(far_ref[...], cot_far_ref[...])

    first = pl.BlockSpec((rows, model), lambda i: (jnp.minimum(i, 1), 0))
    second = pl.BlockSpec((rows, model), lambda i: (jnp.maximum(i - 2, 0), 0))
    each = lambda cols: pl.BlockSpec((rows, cols), lambda i: (i, 0))
    return pl.pallas_call(
        body,
        grid=(4,),
        out_shape=(
            jax.ShapeDtypeStruct((pack_size, model), BF),
            jax.ShapeDtypeStruct((pack_size, model), BF),
            jax.ShapeDtypeStruct((pack_size, 2 * size), BF),
            jax.ShapeDtypeStruct((pack_size, size), BF),
        ),
        in_specs=[first, second, first, second]
        + [
            pl.BlockSpec(p.shape, lambda i: (0, 0), pipeline_mode=pl.Buffered(1)) for p in pieces
        ]
        + [each(model) for _ in before],
        out_specs=(each(model), each(model), each(2 * size), each(size)),
        scratch_shapes=[pltpu.VMEM((model, 3 * size), BF)],
        compiler_params=pltpu.CompilerParams(vmem_limit_bytes=VMEM_LIMIT),
        cost_estimate=pl.CostEstimate(
            flops=12 * pack_size * model * size,
            transcendentals=0,
            bytes_accessed=2 * (model * 3 * size + pack_size * (4 * model + 3 * size)),
        ),
        name="mlp_chunk",
    )(near, far, cot_near, cot_far, *pieces, *before)


def ring_terms(pairs, slots, width, came, top, kind):
    columns = [sum(g.shape[1] for g in gs) for _, gs in pairs]
    total = sum(columns)
    head = 0 if top is None else TOP
    cut = head + width // 2
    full = head + width

    args, specs = [], []

    def add(array, spec=None):
        args.append(array)
        specs.append(spec or pl.BlockSpec(array.shape, lambda i: (0,) * array.ndim))

    for (near, far), gs in pairs:
        for s in slots:
            for half in (near, far):
                if width % 128:
                    add(half[:, s * width : (s + 1) * width])
                else:
                    add(half, pl.BlockSpec((half.shape[0], width), lambda i, s=s: (0, s)))
        for g in gs:
            add(g)
    if top is not None:
        for s in slots:
            add(top[s])
    for c in came:
        add(c)

    if kind == "far":
        outs = [((cut, total), BF), ((width // 2, total), BF)]
    elif kind == "step":
        outs = [((full, total), BF)] * 2
    else:
        outs = [((full, total), BF)]

    def body(*refs):
        n_in = len(args)
        ins, out_refs = list(refs[:n_in]), refs[n_in:]
        sums = [[] for _ in slots]
        at = 0
        for (near, _), gs in pairs:
            halves = [(ins[at + 2 * i], ins[at + 2 * i + 1]) for i in range(len(slots))]
            at += 2 * len(slots)
            g_refs = ins[at : at + len(gs)]
            at += len(gs)
            half_rows = near.shape[0]
            for i, (near_ref, far_ref) in enumerate(halves):
                for g_ref in g_refs:
                    sums[i].append(
                        cross(near_ref[...], g_ref[:half_rows, :])
                        + cross(far_ref[...], g_ref[half_rows:, :])
                    )
        tops = [None] * len(slots)
        if top is not None:
            tops = ins[at : at + len(slots)]
            at += len(slots)
        came_refs = ins[at:]

        def put(target, row, term, lane, extra):
            value = term if extra is None else term + extra.astype(F32)
            target[row : row + term.shape[0], lane : lane + term.shape[1]] = value.astype(BF)

        for i in range(len(slots)):
            lane = 0
            pieces = ([(0, tops[i][...].astype(F32))] if head else []) + [None]
            if head:
                value = tops[i][...].astype(F32)
                if kind == "far":
                    out_refs[0][:head, :] = value.astype(BF)
                elif kind == "step":
                    extra = None
                    if i == 0 or came_refs[i].shape[0] == full:
                        extra = came_refs[i][:head, :]
                    put(out_refs[i], 0, value, 0, extra)
                else:
                    put(
                        out_refs[0],
                        0,
                        value + came_refs[0][:head, :].astype(F32),
                        0,
                        came_refs[1][:head, :],
                    )
            for term in sums[i]:
                lanes = slice(lane, lane + term.shape[1])
                middle = width // 2
                if kind == "far":
                    put(out_refs[0], head, term[:middle], lane, None)
                    put(out_refs[1], 0, term[middle:], lane, None)
                elif kind == "step":
                    if came_refs[i].shape[0] == full:
                        put(out_refs[i], head, term, lane, came_refs[i][head:, lanes])
                    elif i == 0:
                        put(out_refs[i], head, term[:middle], lane, came_refs[i][head:, lanes])
                        put(out_refs[i], cut, term[middle:], lane, None)
                    else:
                        put(out_refs[i], head, term[:middle], lane, None)
                        put(out_refs[i], cut, term[middle:], lane, came_refs[i][:, lanes])
                else:
                    put(
                        out_refs[0],
                        head,
                        term + came_refs[0][head:, lanes].astype(F32),
                        lane,
                        came_refs[1][head:, lanes],
                    )
                lane += term.shape[1]

    tokens = 2 * pairs[0][0][0].shape[0]
    return pl.pallas_call(
        body,
        grid=(1,),
        out_shape=tuple(jax.ShapeDtypeStruct(s, d) for s, d in outs),
        in_specs=specs,
        out_specs=tuple(pl.BlockSpec(s, lambda i: (0, 0)) for s, _ in outs),
        compiler_params=pltpu.CompilerParams(vmem_limit_bytes=VMEM_LIMIT),
        cost_estimate=pl.CostEstimate(
            flops=2 * len(slots) * tokens * width * total,
            transcendentals=0,
            bytes_accessed=2 * (tokens * total + len(slots) * width * (tokens + 2 * total)),
        ),
        name="ring_terms",
    )(*args)


def reduce_over_dp(ring, pairs, width, top=None):
    def far(slot):
        return ring_terms(pairs, [slot], width, [], top, "far")

    def step(up_slot, down_slot, up, down):
        return ring_terms(pairs, [up_slot, down_slot], width, [up, down], top, "step")

    def last(up, down):
        return ring_terms(pairs, [0], width, [up, down], top, "last")[0]

    return ring.scatter(far, step, last)


def unpack_mlp(places, halves, bounds, width, ff):
    count = len(bounds)
    flat = [h for pair in halves for h in pair]

    def body(places_ref, *refs):
        ins, (gate_ref, up_ref, down_ref) = refs[: 2 * count], refs[2 * count :]
        place = places_ref[pl.program_id(0)]
        begin = pl.multiple_of((place % 2) * width, width)
        for c, (a, b) in enumerate(bounds):
            size = b - a
            near = ins[2 * c][pl.ds(begin, width), :].astype(F32)
            far = ins[2 * c + 1][pl.ds(begin, width), :].astype(F32)
            block = jnp.where(place < 2, near, far)
            gate_ref[:, a:b] = block[:, :size]
            up_ref[:, a:b] = block[:, size : 2 * size]
            down_ref[a:b, :] = block[:, 2 * size :].T

    columns = pl.BlockSpec((width, ff), lambda i, p: (0, i))
    return pl.pallas_call(
        body,
        out_shape=(
            jax.ShapeDtypeStruct((width, 4 * ff), F32),
            jax.ShapeDtypeStruct((width, 4 * ff), F32),
            jax.ShapeDtypeStruct((4 * ff, width), F32),
        ),
        grid_spec=pltpu.PrefetchScalarGridSpec(
            num_scalar_prefetch=1,
            grid=(4,),
            in_specs=[pl.BlockSpec(h.shape, lambda i, p: (0, 0)) for h in flat],
            out_specs=(columns, columns, pl.BlockSpec((ff, width), lambda i, p: (i, 0))),
        ),
        compiler_params=pltpu.CompilerParams(vmem_limit_bytes=VMEM_LIMIT),
        name="unpack_mlp",
    )(places, *flat)


def unpack_heads(places, heads, outs, width, q_cols):
    full = TOP + width

    def body(places_ref, near_ref, far_ref, out_near_ref, out_far_ref, *refs):
        query_ref, key_ref, value_ref, out_ref, gain_ref = refs
        gain = jnp.zeros((8, 2 * width), F32)
        for place in range(4):
            at = places_ref[place]
            begin = pl.multiple_of((at % 2) * full, 16)
            near = near_ref[pl.ds(begin, full), :].astype(F32)
            far = far_ref[pl.ds(begin, full), :].astype(F32)
            block = jnp.where(at < 2, near, far)
            gain = gain + block[:8, : 2 * width]
            query_ref[:, place * q_cols : (place + 1) * q_cols] = block[TOP:, :q_cols]
            key_ref[:, place * HD : (place + 1) * HD] = block[TOP:, q_cols : q_cols + HD]
            value_ref[:, place * HD : (place + 1) * HD] = block[TOP:, q_cols + HD :]
            begin = pl.multiple_of((at % 2) * width, 16)
            near = out_near_ref[pl.ds(begin, width), :].astype(F32)
            far = out_far_ref[pl.ds(begin, width), :].astype(F32)
            out_ref[place * q_cols : (place + 1) * q_cols, :] = jnp.where(at < 2, near, far).T
        gain_ref[...] = gain

    args = [places, *heads, *outs]
    return kernel_call(
        body,
        [
            ((width, 4 * q_cols), F32),
            ((width, 4 * HD), F32),
            ((width, 4 * HD), F32),
            ((4 * q_cols, width), F32),
            ((8, 2 * width), F32),
        ],
        moved=8 << 20,
        smem=1,
        args=args,
        name="unpack_heads",
    )


def doc_positions(lengths, pack_size):
    doc_starts = jnp.cumsum(lengths) - lengths
    places = jnp.arange(pack_size, dtype=jnp.int32)
    doc_first = jnp.max(
        jnp.where(places[:, None] >= doc_starts[None, :], doc_starts[None, :], 0), axis=1
    )
    return places - doc_first


def rotary_tables(positions):
    half_dim = HD // 2
    frequency = 10000.0 ** (-2.0 * jnp.arange(half_dim, dtype=F32) / HD)
    angle_table = frequency[:, None] * positions.astype(F32)[None, :]
    return (jnp.cos(angle_table), jnp.sin(angle_table))


def rms_back(grad_normed, values, inverse, gain_vec):
    scaled = grad_normed * gain_vec
    return inverse * (
        scaled - values * inverse * inverse * jnp.mean(scaled * values, axis=1, keepdims=True)
    )


def layer(
    hidden_in,
    cotangent,
    gain_attn,
    w_query,
    w_key,
    w_value,
    w_out,
    gain_mlp,
    w_gate,
    w_up,
    w_down,
    doc_lengths,
    valid_count,
):
    seq = lax.axis_size("seq")
    n_dp = lax.axis_size("dp")
    here = lax.axis_index("seq").astype(jnp.int32)
    ring = Ring(n_dp)
    rows = hidden_in.shape[0]
    pack_size = rows * seq
    width = gain_attn.shape[0]
    q_cols = w_query.shape[1] // seq
    ff = w_gate.shape[1] // seq
    here_1 = here.reshape(1)
    lengths, live = doc_lengths[0], valid_count[:1]

    offset = here ^ jnp.arange(4, dtype=jnp.int32)
    places = (offset % 2) * 2 + offset // 2

    first = (ff // 2 + 127) // 128 * 128
    bounds = [(0, first), (first, ff)]
    head_block = pack_heads(here_1, w_query, w_key, w_value, w_out, gain_attn, gain_mlp, seq)
    head_pieces = ring.gather(head_block, TOP + width // 2)
    mlp_pieces = [
        ring.gather(block, width // 2)
        for block in pack_mlp(here_1, w_gate, w_up, w_down, bounds, seq)
    ]

    mine, my_cot = permute_features([hidden_in, cotangent], ring.slot_owners(), n_dp)
    near, far = seq_gather(mine)
    cot_near, cot_far = seq_gather(my_cot)
    cosine, sine_part = rotary_tables(doc_positions(lengths, pack_size))

    normed, query, kv, kvt, lse, mixed_t, mixed, branch, gains = attention_forward(
        places, lengths, live, near, far, head_pieces, cosine, sine_part, rows, q_cols
    )
    gain_one, gain_two = gains[0:1], gains[1:2]

    my_inputs = mine.astype(F32)
    hidden = my_inputs + seq_scatter(branch)
    inverse_two = lax.rsqrt(jnp.mean(hidden * hidden, axis=1, keepdims=True) + EPS)
    my_normed_two = (hidden * inverse_two * gain_two).astype(BF)
    two_near, two_far = seq_gather(my_normed_two)

    before = ()
    chunk_sums = []
    for (a, b), pieces in zip(bounds, mlp_pieces):
        down, grad_normed, grad_both, act = mlp_chunk(
            two_near, two_far, cot_near, cot_far, pieces, before, rows, b - a
        )
        before = (down, grad_normed)
        chunk_sums.append(
            reduce_over_dp(
                ring, [((two_near, two_far), [grad_both]), ((cot_near, cot_far), [act])], width
            )
        )

    grad_normed_two = seq_scatter(grad_normed)
    term_gain_two = jnp.sum(grad_normed_two * hidden * inverse_two, axis=0)
    grad_hidden = my_cot.astype(F32) + rms_back(grad_normed_two, hidden, inverse_two, gain_two)
    branch_near, branch_far = seq_gather(grad_hidden.astype(BF))
    result = (hidden + seq_scatter(down)).astype(BF)

    out_sum = reduce_over_dp(ring, [((branch_near, branch_far), [mixed])], width)
    grad_q, grad_kv = attention_backward(
        places, lengths, live, branch_near, branch_far, head_pieces, cosine, sine_part,
        query, kv, kvt, lse, mixed_t, rows
    )
    grad_normed_one, gain_terms = heads_back(grad_q, grad_kv, near, far, head_pieces, rows)
    tops = jnp.concatenate(
        [
            gain_terms[0].reshape(n_dp, width),
            term_gain_two.reshape(n_dp, width),
            jnp.zeros((n_dp, q_cols + 2 * HD - 2 * width), F32),
        ],
        axis=1,
    ).astype(BF)
    tops = [
        jnp.concatenate([tops[j : j + 1], jnp.zeros((TOP - 1, tops.shape[1]), BF)], axis=0)
        for j in range(n_dp)
    ]
    half = pack_size // 2
    head_sum = reduce_over_dp(
        ring, [((normed[:half], normed[half:]), [grad_q, grad_kv])], width, tops
    )
    inverse_one = lax.rsqrt(jnp.mean(my_inputs * my_inputs, axis=1, keepdims=True) + EPS)
    grad_input = (
        grad_hidden + rms_back(seq_scatter(grad_normed_one), my_inputs, inverse_one, gain_one)
    ).astype(BF)

    grad_gate, grad_up, grad_down = unpack_mlp(
        places, [seq_gather(c) for c in chunk_sums], bounds, width, ff
    )
    grad_query, grad_key, grad_value, grad_out, gain_sums = unpack_heads(
        places, seq_gather(head_sum), seq_gather(out_sum), width, q_cols
    )
    result, grad_input = permute_features([result, grad_input], ring.owner_slots(), n_dp)

    return (
        result,
        grad_input,
        gain_sums[0, :width],
        grad_query,
        grad_key,
        grad_value,
        grad_out,
        gain_sums[0, width:],
        grad_gate,
        grad_up,
        grad_down,
    )


def solution(mesh):
    return jax.shard_map(
        layer,
        mesh=mesh,
        in_specs=(
            P(("dp", "seq"), None),
            P(("dp", "seq"), None),
            P("dp"),
            P("dp", None),
            P("dp", None),
            P("dp", None),
            P(None, "dp"),
            P("dp"),
            P("dp", None),
            P("dp", None),
            P(None, "dp"),
            P("dp", None),
            P("dp"),
        ),
        out_specs=(
            P(("dp", "seq"), None),
            P(("dp", "seq"), None),
            P("dp"),
            P("dp", None),
            P("dp", None),
            P("dp", None),
            P(None, "dp"),
            P("dp"),
            P("dp", None),
            P("dp", None),
            P(None, "dp"),
        ),
        check_vma=False,
    )
```

```python
import functools

import jax
import jax.numpy as jnp
from jax import lax
from jax.experimental import pallas as pl
from jax.experimental.pallas import tpu as pltpu
from jax.sharding import PartitionSpec as P

HEADS = 32
HD = 64
KVH = 4
EPS = 1e-05
TOP = 16
BF = jnp.bfloat16
F32 = jnp.float32
NEG = -1e30
VMEM_LIMIT = 60 << 20
COST = pl.CostEstimate(flops=1000, transcendentals=0, bytes_accessed=1000)


def dot(left_side, right_side):
    return jnp.dot(left_side, right_side, preferred_element_type=F32)


def cross(left_side, right_side):
    return lax.dot_general(
        left_side, right_side, (((0,), (0,)), ((), ())), preferred_element_type=F32
    )


def against(left_side, right_side):
    return lax.dot_general(
        left_side, right_side, (((1,), (1,)), ((), ())), preferred_element_type=F32
    )


def kernel_call(body, outs, scratch=(), flops=0, moved=0, smem=0, args=(), name=None):
    vmem = pl.BlockSpec(memory_space=pltpu.VMEM)
    return pl.pallas_call(
        body,
        out_shape=tuple(jax.ShapeDtypeStruct(s, d) for s, d in outs),
        in_specs=[pl.BlockSpec(memory_space=pltpu.SMEM)] * smem + [vmem] * (len(args) - smem),
        out_specs=tuple(vmem for _ in outs),
        scratch_shapes=list(scratch),
        compiler_params=pltpu.CompilerParams(vmem_limit_bytes=VMEM_LIMIT),
        cost_estimate=COST,
        name=name,
    )(*args)


class Ring:
    def __init__(self, size):
        self.size = size
        self.half = size // 2
        self.order = list(range(0, size, 2)) + list(range(size - 1, 0, -2))
        place = [0] * size
        for position, device in enumerate(self.order):
            place[device] = position
        self.place = place
        walk = [(self.order[i], self.order[(i + 1) % size]) for i in range(size)]
        self.up = walk
        self.down = [(b, a) for a, b in walk]
        self.steps = (
            [-t for t in range(self.half)] + [t for t in range(1, self.half)] + [self.half]
        )

    def slot_owners(self):
        mine = jnp.asarray(self.place, jnp.int32)[lax.axis_index("dp")]
        wanted = (mine + jnp.asarray(self.steps, jnp.int32)) % self.size
        return jnp.asarray(self.order, jnp.int32)[wanted]

    def owner_slots(self):
        mine = jnp.asarray(self.place, jnp.int32)[lax.axis_index("dp")]
        slot_of_step = [0] * self.size
        for slot, step in enumerate(self.steps):
            slot_of_step[step % self.size] = slot
        step = (jnp.asarray(self.place, jnp.int32) - mine) % self.size
        return jnp.asarray(slot_of_step, jnp.int32)[step]

    def go_up(self, block):
        return lax.ppermute(block, "dp", self.up)

    def go_down(self, block):
        return lax.ppermute(block, "dp", self.down)


class Clock:
    def __init__(self):
        self.last = None

    def tie(self, *arrays):
        if self.last is None:
            out = lax.optimization_barrier(arrays)
        else:
            out = lax.optimization_barrier((*arrays, self.last))[: len(arrays)]
        self.last = out[0]
        return out if len(out) > 1 else out[0]

    def done(self, array):
        self.last = array


class Gather:
    def __init__(self, ring, block, cut):
        self.ring, self.cut = ring, cut
        self.up, self.down = [block], [block]
        self.flying = (ring.go_up(block), ring.go_down(block))
        self.left = ring.half - 1

    def land(self, clock):
        up, down = clock.tie(*self.flying)
        self.flying = None
        self.up.append(up)
        self.down.append(down)

    def go(self, clock):
        up, down = clock.tie(self.up[-1], self.down[-1])
        self.left -= 1
        if self.left == 0:
            up, down = up[: self.cut], down[self.cut :]
        self.flying = (self.ring.go_up(up), self.ring.go_down(down))

    def relay(self, clock):
        if self.left:
            self.land(clock)
            self.go(clock)

    def finish(self, clock):
        while self.left:
            self.relay(clock)
        return self.up + self.down[1:] + list(clock.tie(*self.flying))


class Scatter:
    def __init__(self, ring, terms, cut, tile):
        self.ring, self.terms, self.cut, self.tile = ring, terms, cut, tile
        self.full = terms.shape[0] // ring.size
        begin = (ring.size - 1) * self.full
        self.left = ring.half - 1
        self.flying = (
            ring.go_up(terms[begin : begin + cut]),
            ring.go_down(terms[begin + cut : begin + self.full]),
        )

    def term(self, slot, begin=0, end=None):
        end = self.full if end is None else end
        return self.terms[slot * self.full + begin : slot * self.full + end]

    def relay(self, clock):
        if self.left == 0:
            return
        up, down = clock.tie(*self.flying)
        above, below = self.ring.half - 1 + self.left, self.left
        if up.shape[0] == self.full:
            up, down = plus(self.term(above), up), plus(self.term(below), down)
        else:
            up, down = ring_add(self.terms, (above, below), up, down, self.full, self.cut, self.tile)
        self.left -= 1
        up, down = clock.tie(up, down)
        self.flying = (self.ring.go_up(up), self.ring.go_down(down))

    def finish(self, clock):
        while self.left:
            self.relay(clock)
        up, down = clock.tie(*self.flying)
        out = (self.term(0).astype(F32) + up.astype(F32) + down.astype(F32)).astype(BF)
        return clock.tie(out)


def plus(one, two):
    return (one.astype(F32) + two.astype(F32)).astype(BF)


def swap(block, distance):
    return lax.ppermute(block, "seq", [(i, i ^ distance) for i in range(4)])


def fill_weights(pieces, scratch, top, width, columns):
    begin = 0
    for index, piece in enumerate(pieces):
        skip = top if index < len(pieces) - 1 else 0
        count = piece.shape[0] - skip
        scratch[begin : begin + count, :] = piece[skip:, columns]
        begin += count


def put_features(values, order_ref, target, slots, width):
    for j in range(slots):
        to = pl.ds(pl.multiple_of(order_ref[j] * width, 128), width)
        target[:, to] = values[:, j * width : (j + 1) * width]


def blocks_in_order(array, order, size):
    width = array.shape[1] // size
    return jnp.concatenate(
        [lax.dynamic_slice_in_dim(array, order[i] * width, width, 1) for i in range(size)],
        axis=1,
    )


def permute_features(array, order, size):
    width = array.shape[1] // size
    if width % 128:
        return blocks_in_order(array, order, size)

    def body(order_ref, source, target):
        for j in range(size):
            begin = pl.ds(pl.multiple_of(order_ref[j] * width, 128), width)
            target[:, j * width : (j + 1) * width] = source[:, begin]

    return kernel_call(
        body, [(array.shape, array.dtype)], smem=1, args=[order, array], name="permute_features"
    )[0]


def pack_heads(here, w_query, w_key, w_value, w_out, gain_attn, gain_mlp, seq):
    width = w_query.shape[0]
    q_cols, k_cols = w_query.shape[1] // seq, w_key.shape[1] // seq
    total = 2 * q_cols + 2 * k_cols

    def body(here_ref, query_ref, key_ref, value_ref, out_ref, one_ref, two_ref, block_ref):
        s = here_ref[0]
        block_ref[:TOP, :] = jnp.zeros((TOP, total), BF)
        block_ref[:1, :width] = one_ref[...].reshape(1, width)
        block_ref[:1, width : 2 * width] = two_ref[...].reshape(1, width)
        block_ref[TOP:, :q_cols] = query_ref[...]

        def mine(ref):
            part = jnp.zeros((width, k_cols), F32)
            for place in range(seq):
                piece = ref[:, place * k_cols : (place + 1) * k_cols].astype(F32)
                part = jnp.where(s == place, piece, part)
            return part

        both = jnp.concatenate([mine(key_ref), mine(value_ref)], axis=1)
        block_ref[TOP:, q_cols : q_cols + 2 * k_cols] = both.astype(BF)
        block_ref[TOP:, q_cols + 2 * k_cols :] = out_ref[...].astype(F32).T.astype(BF)

    whole = lambda shape: pl.BlockSpec(shape, lambda i, o: (0, 0))
    return pl.pallas_call(
        body,
        out_shape=jax.ShapeDtypeStruct((TOP + width, total), BF),
        grid_spec=pltpu.PrefetchScalarGridSpec(
            num_scalar_prefetch=1,
            grid=(1,),
            in_specs=[
                pl.BlockSpec((width, q_cols), lambda i, o: (0, o[0])),
                whole(w_key.shape),
                whole(w_value.shape),
                pl.BlockSpec((q_cols, width), lambda i, o: (o[0], 0)),
                pl.BlockSpec((width,), lambda i, o: (0,)),
                pl.BlockSpec((width,), lambda i, o: (0,)),
            ],
            out_specs=whole((TOP + width, total)),
        ),
        name="pack_heads",
    )(here, w_query, w_key, w_value, w_out, gain_attn, gain_mlp)


def pack_mlp(here, w_gate, w_up, w_down, bounds, seq):
    width, ff = w_gate.shape[0], w_gate.shape[1] // seq

    def body(here_ref, gate_ref, up_ref, down_ref, *blocks):
        for (a, b), block in zip(bounds, blocks):
            size = b - a
            block[:, :size] = gate_ref[:, a:b]
            block[:, size : 2 * size] = up_ref[:, a:b]
            block[:, 2 * size :] = down_ref[a:b, :].astype(F32).T.astype(BF)

    columns = pl.BlockSpec((width, ff), lambda i, o: (0, o[0]))
    return pl.pallas_call(
        body,
        out_shape=tuple(jax.ShapeDtypeStruct((width, 3 * (b - a)), BF) for a, b in bounds),
        grid_spec=pltpu.PrefetchScalarGridSpec(
            num_scalar_prefetch=1,
            grid=(1,),
            in_specs=[columns, columns, pl.BlockSpec((ff, width), lambda i, o: (o[0], 0))],
            out_specs=tuple(
                pl.BlockSpec((width, 3 * (b - a)), lambda i, o: (0, 0)) for a, b in bounds
            ),
        ),
        name="pack_mlp",
    )(here, w_gate, w_up, w_down)


def turn(values, cosine, sine_part):
    half_dim = HD // 2
    pieces = []
    for h in range(values.shape[0] // HD):
        first = values[h * HD : h * HD + half_dim]
        second = values[h * HD + half_dim : (h + 1) * HD]
        pieces.append(first * cosine - second * sine_part)
        pieces.append(second * cosine + first * sine_part)
    return jnp.concatenate(pieces, axis=0)


def rounded(values):
    return values.astype(BF).astype(F32)


def pick(refs, place, target):
    for index, ref in enumerate(refs):

        @pl.when(place == index)
        def _():
            target[...] = ref[...]


def write_bias(bias_ref, lengths_ref, live, block, rows):
    keys = (block + 1) * rows
    query = lax.broadcasted_iota(jnp.int32, (1, rows), 1) + block * rows
    low = jnp.zeros((1, rows), jnp.int32)
    start = 0
    for slot in range(lengths_ref.shape[0]):
        low = jnp.where(query >= start, jnp.maximum(low, start), low)
        start = start + lengths_ref[slot]
    high = jnp.minimum(query, live - 1)
    key = lax.broadcasted_iota(jnp.int32, (keys, rows), 0)
    allowed = ((key >= low) & (key <= high)) | (key == query)
    bias_ref[:keys, :] = jnp.where(allowed, 0.0, NEG)


def attention_forward(places, lengths, live, tokens, pieces, cosine, sine_part, q_cols):
    rows, model = tokens[0].shape
    pack_size = 4 * rows
    n_heads = q_cols // HD
    heads_cols = q_cols + 2 * HD
    width = pieces[0].shape[0] - TOP

    def body(places_ref, lengths_ref, live_ref, cos_ref, sin_ref, *refs):
        token_refs, piece_refs, refs = refs[:4], refs[4 : 4 + len(pieces)], refs[4 + len(pieces) :]
        (
            normed_ref, query_ref, kv_ref, kvt_ref, lse_ref, mixed_t_ref, mixed_ref, keep_ref,
            send_ref, gains_ref, w_ref, bias_ref, query_s, mixed_s, tokens_s,
        ) = refs
        live_count = live_ref[0]
        fill_weights(piece_refs, w_ref, TOP, width, slice(None))
        gains_ref[...] = jnp.zeros_like(gains_ref)
        for index, piece in enumerate(piece_refs[:-1]):
            at = slice(index * width, (index + 1) * width)
            gains_ref[0:1, at] = piece[0:1, :width].astype(F32)
            gains_ref[1:2, at] = piece[0:1, width : 2 * width].astype(F32)
        ones = jnp.ones((HD, rows), BF)
        for block in range(4):
            place = places_ref[block]
            at = slice(block * rows, (block + 1) * rows)
            keys = (block + 1) * rows
            to = pl.ds(pl.multiple_of(place * rows, rows), rows)
            pick(token_refs, place, tokens_s)
            inputs = tokens_s[...].astype(F32)
            inverse = lax.rsqrt(jnp.mean(inputs * inputs, axis=1, keepdims=True) + EPS)
            normed = (inputs * inverse * gains_ref[0:1, :]).astype(BF)
            normed_ref[to, :] = normed
            pre = dot(normed, w_ref[:, :heads_cols]).T
            cos_b, sin_b = cos_ref[:, at], sin_ref[:, at]
            query = (rounded(turn(pre[:q_cols], cos_b, sin_b)) * HD**-0.5).astype(BF)
            query_s[...] = query
            query_ref[:, at] = query
            key_t = rounded(turn(pre[q_cols : q_cols + HD], cos_b, sin_b))
            value_t = rounded(pre[q_cols + HD :])
            kv_t = jnp.concatenate([key_t, value_t], axis=0)
            kv_ref[at, :] = kv_t.T.astype(BF)
            kvt_ref[: 2 * HD, at] = kv_t.astype(BF)
            kvt_ref[2 * HD :, at] = ones
            write_bias(bias_ref, lengths_ref, live_count, block, rows)

            def attend(h, _):
                mine = pl.ds(pl.multiple_of(h * HD, HD), HD)
                scores = dot(kv_ref[:keys, :HD], query_s[mine, :]) + bias_ref[:keys, :]
                peak = jnp.max(scores, axis=0, keepdims=True)
                weights = jnp.exp(scores - peak).astype(BF)
                summed = dot(kvt_ref[HD:, :keys], weights)
                total = summed[HD : HD + 1]
                mixed = summed[:HD] * (1.0 / total)
                mixed_s[mine, :] = mixed
                lse_ref[pl.ds(h, 1), at] = peak + jnp.log(total)
                return 0

            lax.fori_loop(0, n_heads, attend, 0, unroll=2)
            mixed_t = mixed_s[...]
            mixed_t_ref[:, at] = mixed_t
            mixed = mixed_t.T.astype(BF)
            mixed_ref[to, :] = mixed
            branch = against(mixed, w_ref[:, heads_cols:]).astype(BF)
            half_to = pl.ds(pl.multiple_of((place % 2) * rows, rows), rows)

            @pl.when(place < 2)
            def _():
                keep_ref[half_to, :] = branch

            @pl.when(place >= 2)
            def _():
                send_ref[half_to, :] = branch

    args = [places, lengths, live, cosine, sine_part, *tokens, *pieces]
    flops = 2 * pack_size * model * (heads_cols + q_cols) + 4 * n_heads * pack_size**2 * HD * 3
    return kernel_call(
        body,
        [
            ((pack_size, model), BF),
            ((q_cols, pack_size), BF),
            ((pack_size, 2 * HD), BF),
            ((3 * HD, pack_size), BF),
            ((n_heads, pack_size), F32),
            ((q_cols, pack_size), F32),
            ((pack_size, q_cols), BF),
            ((pack_size // 2, model), BF),
            ((pack_size // 2, model), BF),
            ((8, model), F32),
        ],
        scratch=[
            pltpu.VMEM((model, heads_cols + q_cols), BF),
            pltpu.VMEM((pack_size, rows), F32),
            pltpu.VMEM((q_cols, rows), BF),
            pltpu.VMEM((q_cols, rows), F32),
            pltpu.VMEM((rows, model), BF),
        ],
        flops=flops,
        moved=30 << 20,
        smem=3,
        args=args,
        name="attention_forward",
    )


def attention_backward(
    places, lengths, live, tokens, pieces, cosine, sine_part, query, kv, kvt, lse, mixed_t
):
    q_cols, pack_size = query.shape
    rows, model = tokens[0].shape
    n_heads = q_cols // HD
    heads_cols = q_cols + 2 * HD
    width = pieces[0].shape[0] - TOP

    def body(
        places_ref, lengths_ref, live_ref, cos_ref, sin_ref,
        query_ref, kv_ref, kvt_ref, lse_ref, mixed_t_ref, *refs
    ):
        token_refs, piece_refs, refs = refs[:4], refs[4 : 4 + len(pieces)], refs[4 + len(pieces) :]
        (
            grad_q_ref, grad_kv_ref, w_ref, bias_ref, grad_s, grad_q_s, key_acc, value_acc, inner_s,
            tokens_s,
        ) = refs
        live_count = live_ref[0]
        fill_weights(piece_refs, w_ref, TOP, width, slice(heads_cols, heads_cols + q_cols))
        key_acc[...] = jnp.zeros_like(key_acc)
        value_acc[...] = jnp.zeros_like(value_acc)
        for block in range(4):
            place = places_ref[block]
            at = slice(block * rows, (block + 1) * rows)
            keys = (block + 1) * rows
            to = pl.ds(pl.multiple_of(place * rows, rows), rows)
            pick(token_refs, place, tokens_s)
            grad_t = rounded(dot(tokens_s[...], w_ref[...]).T)
            grad_s[...] = grad_t.astype(BF)
            product = grad_t * mixed_t_ref[:, at]
            for h in range(n_heads):
                inner_s[h : h + 1, :] = jnp.sum(
                    product[h * HD : (h + 1) * HD], axis=0, keepdims=True
                )
            write_bias(bias_ref, lengths_ref, live_count, block, rows)

            def attend(h, _):
                mine = pl.ds(pl.multiple_of(h * HD, HD), HD)
                query_h = query_ref[mine, at]
                grad_h = grad_s[mine, :]
                scores = dot(kv_ref[:keys, :HD], query_h) + bias_ref[:keys, :]
                probs = jnp.exp(scores - lse_ref[pl.ds(h, 1), at])
                grad_probs = dot(kv_ref[:keys, HD:], grad_h)
                grad_scores = (probs * (grad_probs - inner_s[pl.ds(h, 1), :])).astype(BF)
                grad_q_s[mine, :] = dot(kvt_ref[:HD, :keys], grad_scores) * HD**-0.5
                key_acc[:keys, :] += against(grad_scores, query_h)
                value_acc[:keys, :] += against(probs.astype(BF), grad_h)
                return 0

            lax.fori_loop(0, n_heads, attend, 0, unroll=2)
            turned = turn(rounded(grad_q_s[...]), cos_ref[:, at], -sin_ref[:, at])
            grad_q_ref[to, :] = turned.T.astype(BF)
        for block in range(4):
            at = slice(block * rows, (block + 1) * rows)
            to = pl.ds(pl.multiple_of(places_ref[block] * rows, rows), rows)
            key_t = turn(rounded(key_acc[at, :]).T, cos_ref[:, at], -sin_ref[:, at])
            grad_kv_ref[to, :] = jnp.concatenate([key_t.T, value_acc[at, :]], axis=1).astype(BF)

    args = [
        places, lengths, live, cosine, sine_part, query, kv, kvt, lse, mixed_t, *tokens, *pieces
    ]
    return kernel_call(
        body,
        [((pack_size, q_cols), BF), ((pack_size, 2 * HD), BF)],
        scratch=[
            pltpu.VMEM((model, q_cols), BF),
            pltpu.VMEM((pack_size, rows), F32),
            pltpu.VMEM((q_cols, rows), BF),
            pltpu.VMEM((q_cols, rows), F32),
            pltpu.VMEM((pack_size, HD), F32),
            pltpu.VMEM((pack_size, HD), F32),
            pltpu.VMEM((n_heads, rows), F32),
            pltpu.VMEM((rows, model), BF),
        ],
        flops=2 * pack_size * model * q_cols + 10 * n_heads * pack_size**2 * HD * 3,
        moved=20 << 20,
        smem=3,
        args=args,
        name="attention_backward",
    )


def heads_back(grad_q, grad_kv, tokens, pieces):
    pack_size, q_cols = grad_q.shape
    rows, model = tokens[0].shape
    heads_cols = q_cols + 2 * HD
    width = pieces[0].shape[0] - TOP

    def body(grad_q_ref, grad_kv_ref, *refs):
        token_refs, piece_refs = refs[:4], refs[4 : 4 + len(pieces)]
        keep_ref, send_ref, gain_ref, w_ref, tokens_s = refs[4 + len(pieces) :]
        step = pl.program_id(0)

        @pl.when(step == 0)
        def _():
            fill_weights(piece_refs, w_ref, TOP, width, slice(0, heads_cols))
            gain_ref[...] = jnp.zeros_like(gain_ref)

        pick(token_refs, step, tokens_s)
        inputs = tokens_s[...].astype(F32)
        inverse = lax.rsqrt(jnp.mean(inputs * inputs, axis=1, keepdims=True) + EPS)
        grad = against(grad_q_ref[...], w_ref[:, :q_cols]) + against(
            grad_kv_ref[...], w_ref[:, q_cols:]
        )

        @pl.when(step < 2)
        def _():
            keep_ref[...] = grad.astype(BF)

        @pl.when(step >= 2)
        def _():
            send_ref[...] = grad.astype(BF)

        total = jnp.sum(grad * inputs * inverse, axis=0, keepdims=True)
        gain_ref[...] += jnp.broadcast_to(total, gain_ref.shape)

    first = pl.BlockSpec((rows, model), lambda i: (jnp.minimum(i, 1), 0))
    second = pl.BlockSpec((rows, model), lambda i: (jnp.maximum(i - 2, 0), 0))
    fixed = lambda a: pl.BlockSpec(a.shape, lambda i: (0, 0), pipeline_mode=pl.Buffered(1))
    half = jax.ShapeDtypeStruct((pack_size // 2, model), BF)
    return pl.pallas_call(
        body,
        grid=(4,),
        out_shape=(half, half, jax.ShapeDtypeStruct((8, model), F32)),
        in_specs=[
            pl.BlockSpec((rows, q_cols), lambda i: (i, 0)),
            pl.BlockSpec((rows, 2 * HD), lambda i: (i, 0)),
        ]
        + [fixed(a) for a in (*tokens, *pieces)],
        out_specs=(first, second, pl.BlockSpec((8, model), lambda i: (0, 0))),
        scratch_shapes=[pltpu.VMEM((model, heads_cols), BF), pltpu.VMEM((rows, model), BF)],
        compiler_params=pltpu.CompilerParams(vmem_limit_bytes=VMEM_LIMIT),
        cost_estimate=COST,
        name="heads_back",
    )(grad_q, grad_kv, *tokens, *pieces)


def mlp_half(tokens, cots, pieces, before, size):
    rows, model = tokens[0].shape

    def body(*refs):
        token_refs, cot_refs, refs = refs[:2], refs[2:4], refs[4:]
        piece_refs, refs = refs[: len(pieces)], refs[len(pieces) :]
        before_refs, refs = refs[: len(before)], refs[len(before) :]
        down_ref, grad_ref, both_ref, w_ref, tokens_s, cot_s = refs
        step = pl.program_id(0)

        @pl.when(step == 0)
        def _():
            fill_weights(piece_refs, w_ref, 0, model, slice(None))

        pick(token_refs, step, tokens_s)
        pick(cot_refs, step, cot_s)
        both = dot(tokens_s[...], w_ref[:, : 2 * size])
        grad_act = dot(cot_s[...], w_ref[:, 2 * size :])
        gate_pre, up_pre = both[:, :size], both[:, size:]
        sig = 1.0 / (1.0 + jnp.exp(-gate_pre))
        active = gate_pre * sig
        both_ref[:, 2 * size :] = (active * up_pre).astype(BF)
        both_ref[:, size : 2 * size] = (grad_act * active).astype(BF)
        both_ref[:, :size] = (grad_act * up_pre * (sig + active * (1.0 - sig))).astype(BF)
        down = against(both_ref[:, 2 * size :], w_ref[:, 2 * size :])
        grad = against(both_ref[:, : 2 * size], w_ref[:, : 2 * size])
        if before_refs:
            down = down + before_refs[0][...].astype(F32)
            grad = grad + before_refs[1][...].astype(F32)
        down_ref[...] = down.astype(BF)
        grad_ref[...] = grad.astype(BF)

    by_rows = lambda cols: pl.BlockSpec((rows, cols), lambda i: (i, 0))
    fixed = lambda array: pl.BlockSpec(
        array.shape, lambda i: (0, 0), pipeline_mode=pl.Buffered(1)
    )
    half = jax.ShapeDtypeStruct((2 * rows, model), BF)
    return pl.pallas_call(
        body,
        grid=(2,),
        out_shape=(half, half, jax.ShapeDtypeStruct((2 * rows, 3 * size), BF)),
        in_specs=[fixed(a) for a in (*tokens, *cots, *pieces)] + [by_rows(model)] * len(before),
        out_specs=(by_rows(model), by_rows(model), by_rows(3 * size)),
        scratch_shapes=[
            pltpu.VMEM((model, 3 * size), BF),
            pltpu.VMEM((rows, model), BF),
            pltpu.VMEM((rows, model), BF),
        ],
        compiler_params=pltpu.CompilerParams(vmem_limit_bytes=VMEM_LIMIT),
        cost_estimate=COST,
        name="mlp_half",
    )(*tokens, *cots, *pieces, *before)


def weight_terms(pairs, width, n_slots, group, tops=None):
    tokens = sum(x.shape[0] for x in pairs[0][0])
    total = sum(cols.stop - cols.start for _, _, cols in pairs)
    head = 0 if tops is None else TOP

    def distinct(lists):
        out = []
        for one in lists:
            if not any(one is other for other in out):
                out.append(one)
        return out

    x_lists = distinct(x for x, _, _ in pairs)
    g_lists = distinct(g for _, g, _ in pairs)
    while (width * group) % 128:
        group *= 2
    wide = width * group
    args, specs = [], []
    for x in [x for xs in x_lists for x in xs]:
        args.append(x)
        specs.append(pl.BlockSpec((x.shape[0], wide), lambda i: (0, i)))
    for g in [g for gs in g_lists for g in gs]:
        args.append(g)
        specs.append(pl.BlockSpec(g.shape, lambda i: (0, 0), pipeline_mode=pl.Buffered(1)))
    if head:
        args.append(tops)
        specs.append(pl.BlockSpec((group * TOP, total), lambda i: (i, 0)))

    def body(*refs):
        def take(lists):
            nonlocal refs
            out = []
            for one in lists:
                out.append((one, refs[: len(one)]))
                refs = refs[len(one) :]
            return out

        x_refs, g_refs = take(x_lists), take(g_lists)
        out_ref, x_s = refs[-2:]
        lane = 0
        filled = None
        for xs, gs, cols in pairs:
            parts = next(r for other, r in x_refs if other is xs)
            g_parts = next(r for other, r in g_refs if other is gs)
            if len(parts) > 1 and filled is not xs:
                at = 0
                for part in parts:
                    x_s[at : at + part.shape[0], :] = part[...]
                    at += part.shape[0]
                filled = xs
            product, at = None, 0
            for g in g_parts:
                rows = g.shape[0]
                x = (x_s if len(parts) > 1 else parts[0])[at : at + rows, :]
                at += rows
                more = cross(x, g[:, cols])
                product = more if product is None else product + more
            product = product.astype(BF)
            count = cols.stop - cols.start
            for j in range(group):
                at = j * (head + width) + head
                out_ref[at : at + width, lane : lane + count] = product[
                    j * width : (j + 1) * width
                ]
            lane += count
        if head:
            for j in range(group):
                at = j * (head + width)
                out_ref[at : at + head, :] = refs[0][j * TOP : (j + 1) * TOP, :]

    return pl.pallas_call(
        body,
        grid=(n_slots // group,),
        out_shape=jax.ShapeDtypeStruct((n_slots * (head + width), total), BF),
        in_specs=specs,
        out_specs=pl.BlockSpec((group * (head + width), total), lambda i: (i, 0)),
        scratch_shapes=[pltpu.VMEM((tokens, wide), BF)],
        compiler_params=pltpu.CompilerParams(vmem_limit_bytes=VMEM_LIMIT),
        cost_estimate=COST,
        name="weight_terms",
    )(*args)


def ring_add(terms, slots, up, down, full, cut, tile):
    total = terms.shape[1]

    def body(up_term, down_term, up_ref, down_ref, up_out, down_out):
        if up_ref.shape[0] == full:
            up_out[...] = (up_term[...].astype(F32) + up_ref[...].astype(F32)).astype(BF)
            down_out[...] = (down_term[...].astype(F32) + down_ref[...].astype(F32)).astype(BF)
        else:
            up_out[:cut, :] = (up_term[:cut, :].astype(F32) + up_ref[...].astype(F32)).astype(BF)
            up_out[cut:, :] = up_term[cut:, :]
            down_out[:cut, :] = down_term[:cut, :]
            down_out[cut:, :] = (
                down_term[cut:, :].astype(F32) + down_ref[...].astype(F32)
            ).astype(BF)

    columns = lambda array: pl.BlockSpec((array.shape[0], tile), lambda i: (0, i))
    out = jax.ShapeDtypeStruct((full, total), BF)
    return pl.pallas_call(
        body,
        grid=(total // tile,),
        out_shape=(out, out),
        in_specs=[
            pl.BlockSpec((full, tile), lambda i: (slots[0], i)),
            pl.BlockSpec((full, tile), lambda i: (slots[1], i)),
            columns(up),
            columns(down),
        ],
        out_specs=(columns(out), columns(out)),
        cost_estimate=COST,
        name="ring_add",
    )(terms, terms, up, down)


def row_call(body, outs, row_args, fixed_args, steps, smem=(), name=None):
    rows = outs[0][0][0] if outs[0][2] else row_args[0][0].shape[0]
    tile = rows // steps
    n_smem = len(smem)
    by_rows = lambda cols, at: pl.BlockSpec((tile, cols), lambda i, *_: (i + at, 0))
    return pl.pallas_call(
        body,
        out_shape=tuple(jax.ShapeDtypeStruct(s, d) for s, d, _ in outs),
        grid_spec=pltpu.PrefetchScalarGridSpec(
            num_scalar_prefetch=n_smem,
            grid=(steps,),
            in_specs=[by_rows(a.shape[1], at * steps) for a, at in row_args]
            + [pl.BlockSpec(a.shape, lambda i, *_: (0, 0)) for a in fixed_args],
            out_specs=tuple(
                by_rows(s[1], 0) if split else pl.BlockSpec(s, lambda i, *_: (0, 0))
                for s, _, split in outs
            ),
        ),
        cost_estimate=COST,
        name=name,
    )(*smem, *[a for a, _ in row_args], *fixed_args)


STEPS = 2


def second_norm(inputs, keep, came, last, gains):
    def body(inputs_ref, keep_ref, came_ref, last_ref, gains_ref, hidden_ref, normed_ref):
        branch = keep_ref[...].astype(F32) + came_ref[...].astype(F32) + last_ref[...].astype(F32)
        hidden = inputs_ref[...].astype(F32) + branch
        inverse = lax.rsqrt(jnp.mean(hidden * hidden, axis=1, keepdims=True) + EPS)
        hidden_ref[...] = hidden
        normed_ref[...] = (hidden * inverse * gains_ref[1:2, :]).astype(BF)

    return row_call(
        body,
        [(inputs.shape, F32, True), (inputs.shape, BF, True)],
        [(inputs, 0), (keep, 0), (came, 0), (last, 0)],
        [gains],
        STEPS,
        name="second_norm",
    )


def norm_back(grad, values, gain):
    inverse = lax.rsqrt(jnp.mean(values * values, axis=1, keepdims=True) + EPS)
    scaled = grad * gain
    mean = jnp.mean(scaled * values, axis=1, keepdims=True)
    return inverse, inverse * (scaled - values * (inverse * inverse * mean))


def second_norm_back(cot, hidden, keep, came, last, gains):
    rows, model = hidden.shape

    def body(cot_ref, hidden_ref, keep_ref, came_ref, last_ref, gains_ref, grad_ref, low_ref, gain_ref):
        @pl.when(pl.program_id(0) == 0)
        def _():
            gain_ref[...] = jnp.zeros_like(gain_ref)

        grad = keep_ref[...].astype(F32) + came_ref[...].astype(F32) + last_ref[...].astype(F32)
        hidden_v = hidden_ref[...]
        inverse, back = norm_back(grad, hidden_v, gains_ref[1:2, :])
        total = jnp.sum(grad * hidden_v * inverse, axis=0, keepdims=True)
        gain_ref[...] += jnp.broadcast_to(total, gain_ref.shape)
        out = cot_ref[...].astype(F32) + back
        grad_ref[...] = out
        low_ref[...] = out.astype(BF)

    return row_call(
        body,
        [((rows, model), F32, True), ((rows, model), BF, True), ((8, model), F32, False)],
        [(cot, 0), (hidden, 0), (keep, 0), (came, 0), (last, 0)],
        [gains],
        STEPS,
        name="second_norm_back",
    )


def first_norm_back(grad_hidden, inputs, keep, came, last, gains, order, n_slots):
    width = inputs.shape[1] // n_slots

    def body(order_ref, grad_ref, inputs_ref, keep_ref, came_ref, last_ref, gains_ref, out_ref):
        grad = keep_ref[...].astype(F32) + came_ref[...].astype(F32) + last_ref[...].astype(F32)
        _, back = norm_back(grad, inputs_ref[...].astype(F32), gains_ref[0:1, :])
        out = (grad_ref[...] + back).astype(BF)
        if width % 128:
            out_ref[...] = out
        else:
            put_features(out, order_ref, out_ref, n_slots, width)

    return row_call(
        body,
        [(inputs.shape, BF, True)],
        [(grad_hidden, 0), (inputs, 0), (keep, 0), (came, 0), (last, 0)],
        [gains],
        STEPS,
        smem=(order,),
        name="first_norm_back",
    )[0]


def layer_output(hidden, keep, came, last, order, n_slots):
    width = hidden.shape[1] // n_slots

    def body(order_ref, hidden_ref, keep_ref, came_ref, last_ref, out_ref):
        down = keep_ref[...].astype(F32) + came_ref[...].astype(F32) + last_ref[...].astype(F32)
        out = (hidden_ref[...] + down).astype(BF)
        if width % 128:
            out_ref[...] = out
        else:
            put_features(out, order_ref, out_ref, n_slots, width)

    return row_call(
        body,
        [(hidden.shape, BF, True)],
        [(hidden, 0), (keep, 0), (came, 0), (last, 0)],
        [],
        STEPS,
        smem=(order,),
        name="layer_output",
    )[0]


def unpack_mlp(places, chunks, bounds, width, ff):
    flat = [block for blocks in chunks for block in blocks]

    def body(places_ref, *refs):
        ins = refs[: len(flat)]
        gate_ref, up_ref, down_ref = refs[len(flat) : len(flat) + 3]
        scratches = refs[len(flat) + 3 :]
        place = places_ref[pl.program_id(0)]
        for c, (a, b) in enumerate(bounds):
            size = b - a
            block_s = scratches[c]
            pick(ins[4 * c : 4 * c + 4], place, block_s)
            gate_ref[:, a:b] = block_s[:, :size].astype(F32)
            up_ref[:, a:b] = block_s[:, size : 2 * size].astype(F32)
            down_ref[a:b, :] = block_s[:, 2 * size :].astype(F32).T

    columns = pl.BlockSpec((width, ff), lambda i, p: (0, i))
    return pl.pallas_call(
        body,
        out_shape=(
            jax.ShapeDtypeStruct((width, 4 * ff), F32),
            jax.ShapeDtypeStruct((width, 4 * ff), F32),
            jax.ShapeDtypeStruct((4 * ff, width), F32),
        ),
        grid_spec=pltpu.PrefetchScalarGridSpec(
            num_scalar_prefetch=1,
            grid=(4,),
            in_specs=[
                pl.BlockSpec(h.shape, lambda i, p: (0, 0), pipeline_mode=pl.Buffered(1))
                for h in flat
            ],
            out_specs=(columns, columns, pl.BlockSpec((ff, width), lambda i, p: (i, 0))),
            scratch_shapes=[pltpu.VMEM((width, 3 * (b - a)), BF) for a, b in bounds],
        ),
        compiler_params=pltpu.CompilerParams(vmem_limit_bytes=VMEM_LIMIT),
        cost_estimate=COST,
        name="unpack_mlp",
    )(places, *flat)


def unpack_heads(places, heads, width, q_cols):
    kv = q_cols + 2 * HD

    def body(places_ref, *refs):
        head_refs = refs[:4]
        query_ref, key_ref, value_ref, out_ref, gain_ref, head_s = refs[4:]
        gain = jnp.zeros((8, 2 * width), F32)
        for place in range(4):
            pick(head_refs, places_ref[place], head_s)
            gain = gain + head_s[:TOP, : 2 * width].astype(F32)[:8]
            at = slice(place * q_cols, (place + 1) * q_cols)
            query_ref[:, at] = head_s[TOP:, :q_cols].astype(F32)
            both = head_s[TOP:, q_cols:kv].astype(F32)
            key_ref[:, place * HD : (place + 1) * HD] = both[:, :HD]
            value_ref[:, place * HD : (place + 1) * HD] = both[:, HD:]
            out_ref[at, :] = head_s[TOP:, kv:].astype(F32).T
        gain_ref[...] = gain

    args = [places, *heads]
    return kernel_call(
        body,
        [
            ((width, 4 * q_cols), F32),
            ((width, 4 * HD), F32),
            ((width, 4 * HD), F32),
            ((4 * q_cols, width), F32),
            ((8, 2 * width), F32),
        ],
        scratch=[pltpu.VMEM(heads[0].shape, BF)],
        smem=1,
        args=args,
        name="unpack_heads",
    )


def doc_positions(lengths, pack_size):
    doc_starts = jnp.cumsum(lengths) - lengths
    places = jnp.arange(pack_size, dtype=jnp.int32)
    doc_first = jnp.max(
        jnp.where(places[:, None] >= doc_starts[None, :], doc_starts[None, :], 0), axis=1
    )
    return places - doc_first


def rotary_tables(positions):
    half_dim = HD // 2
    frequency = 10000.0 ** (-2.0 * jnp.arange(half_dim, dtype=F32) / HD)
    angle_table = frequency[:, None] * positions.astype(F32)[None, :]
    return (jnp.cos(angle_table), jnp.sin(angle_table))


def layer(
    hidden_in,
    cotangent,
    gain_attn,
    w_query,
    w_key,
    w_value,
    w_out,
    gain_mlp,
    w_gate,
    w_up,
    w_down,
    doc_lengths,
    valid_count,
):
    seq = lax.axis_size("seq")
    n_dp = lax.axis_size("dp")
    here = lax.axis_index("seq").astype(jnp.int32)
    ring = Ring(n_dp)
    rows, model = hidden_in.shape
    pack_size = rows * seq
    width = gain_attn.shape[0]
    q_cols = w_query.shape[1] // seq
    ff = w_gate.shape[1] // seq
    here_1 = here.reshape(1)
    lengths, live = doc_lengths[0], valid_count[:1]
    middle = width // 2

    offset = here ^ jnp.arange(4, dtype=jnp.int32)
    places = (offset % 2) * 2 + offset // 2

    first = (ff // 2 + 127) // 128 * 128
    bounds = [(0, first), (first, ff)]
    sizes = [b - a for a, b in bounds]

    def other_half(keep, came):
        return plus(keep[rows:], came[rows:])

    def four(block, across, beside):
        return [block, across, beside, swap(across, 1)]

    clock = Clock()
    head_block = pack_heads(here_1, w_query, w_key, w_value, w_out, gain_attn, gain_mlp, seq)
    clock.done(head_block)
    heads = Gather(ring, head_block, TOP + middle)
    hidden_in, cotangent = clock.tie(hidden_in, cotangent)
    mine = permute_features(hidden_in, ring.slot_owners(), n_dp)
    clock.done(mine)
    across, beside = swap(mine, 2), swap(mine, 1)
    w_gate, w_up, w_down, cotangent = clock.tie(w_gate, w_up, w_down, cotangent)
    blocks = pack_mlp(here_1, w_gate, w_up, w_down, bounds, seq)
    clock.done(blocks[0])
    heads.relay(clock)
    cotangent = clock.tie(cotangent)
    my_cot = permute_features(cotangent, ring.slot_owners(), n_dp)
    cosine, sine_part = rotary_tables(doc_positions(lengths, pack_size))
    cosine, sine_part, my_cot = clock.tie(cosine, sine_part, my_cot)
    heads.relay(clock)
    across, my_cot = clock.tie(across, my_cot)
    tokens = four(mine, across, beside)
    cot_across, cot_beside = swap(my_cot, 2), swap(my_cot, 1)
    heads.relay(clock)
    head_pieces = heads.finish(clock)
    tokens = list(clock.tie(*tokens))
    blocks = clock.tie(*blocks)
    chunks = [Gather(ring, block, middle) for block in blocks]
    normed, query, kv, kvt, lse, mixed_t, mixed, keep, send, gains = attention_forward(
        places, lengths, live, tokens, head_pieces, cosine, sine_part, q_cols
    )
    clock.done(lse)
    chunks[0].relay(clock)
    chunks[1].land(clock)
    cot_across, send = clock.tie(cot_across, send)
    came = clock.tie(swap(send, 1))
    last = swap(clock.tie(other_half(keep, came)), 2)
    cots = four(my_cot, cot_across, cot_beside)
    chunks[0].relay(clock)
    last = clock.tie(last)
    hidden, my_normed = second_norm(mine, keep, came, last, gains)
    clock.done(my_normed)
    across, beside = swap(my_normed, 2), swap(my_normed, 1)
    chunks[0].relay(clock)
    across = clock.tie(across)
    seconds = four(my_normed, across, beside)
    pieces = chunks[0].finish(clock)
    chunks[1].go(clock)
    seconds = list(clock.tie(*seconds))
    cots = list(clock.tie(*cots))

    def terms_of(both, size):
        return weight_terms(
            [(seconds, both, slice(0, 2 * size)), (cots, both, slice(2 * size, 3 * size))],
            width,
            n_dp,
            2,
        )

    down_send, grad_send, both_send = mlp_half(seconds[2:], cots[2:], pieces, (), sizes[0])
    clock.done(both_send)
    chunks[1].relay(clock)
    first_two = clock.tie(*seconds[:2])
    down_keep, grad_keep, both_keep = mlp_half(first_two, cots[:2], pieces, (), sizes[0])
    clock.done(both_keep)
    chunks[1].relay(clock)
    both = list(clock.tie(both_keep, both_send))
    terms = terms_of(both, sizes[0])
    clock.done(terms)
    pieces = chunks[1].finish(clock)
    sums = [Scatter(ring, clock.tie(terms), middle, sizes[0])]
    down_send, grad_send, both_send = mlp_half(
        seconds[2:], cots[2:], clock.tie(*pieces), (down_send, grad_send), sizes[1]
    )
    clock.done(both_send)
    sums[0].relay(clock)
    grad_send, down_send = clock.tie(grad_send, down_send)
    came, down_came = swap(grad_send, 1), swap(down_send, 1)
    first_two = clock.tie(*seconds[:2])
    down_keep, grad_keep, both_keep = mlp_half(
        first_two, cots[:2], pieces, (down_keep, grad_keep), sizes[1]
    )
    clock.done(both_keep)
    came, down_came = clock.tie(came, down_came)
    last = swap(clock.tie(other_half(grad_keep, came)), 2)
    sums[0].relay(clock)
    both = list(clock.tie(both_keep, both_send))
    terms = terms_of(both, sizes[1])
    clock.done(terms)
    sums.append(Scatter(ring, clock.tie(terms), middle, sizes[1]))
    last = clock.tie(last)
    grad_hidden, my_branch, gain_two_terms = second_norm_back(
        my_cot, hidden, grad_keep, came, last, gains
    )
    clock.done(my_branch)
    across, beside = swap(my_branch, 2), swap(my_branch, 1)
    down_other = clock.tie(other_half(down_keep, down_came))
    sums[0].relay(clock)
    sums[1].relay(clock)
    across = clock.tie(across)
    branches = four(my_branch, across, beside)
    down_last = swap(clock.tie(down_other), 2)
    branches = list(clock.tie(*branches))
    grad_q, grad_kv = attention_backward(
        places, lengths, live, branches, head_pieces, cosine, sine_part,
        query, kv, kvt, lse, mixed_t
    )
    clock.done(grad_kv)
    sums[1].relay(clock)
    chunk_sum = sums[0].finish(clock)
    down_last = clock.tie(down_last)
    chunk_across, chunk_beside = swap(clock.tie(chunk_sum), 2), swap(chunk_sum, 1)
    tokens = clock.tie(*tokens)
    grad_keep, grad_send, gain_one_terms = heads_back(grad_q, grad_kv, tokens, head_pieces)
    clock.done(gain_one_terms)
    columns = head_block.shape[1]
    tops = jnp.concatenate(
        [
            gain_one_terms[0].reshape(n_dp, width),
            gain_two_terms[0].reshape(n_dp, width),
            jnp.zeros((n_dp, columns - 2 * width), F32),
        ],
        axis=1,
    ).astype(BF)
    tops = jnp.pad(tops[:, None], ((0, 0), (0, TOP - 1), (0, 0))).reshape(n_dp * TOP, -1)
    normed, tops = clock.tie(normed, tops)
    normed = [normed]
    head_terms = weight_terms(
        [
            (normed, [grad_q], slice(0, q_cols)),
            (normed, [grad_kv], slice(0, 2 * HD)),
            (branches, [mixed], slice(0, q_cols)),
        ],
        width,
        n_dp,
        2,
        tops,
    )
    clock.done(head_terms)
    chunk_across = clock.tie(chunk_across)
    firsts = four(chunk_sum, chunk_across, chunk_beside)
    head_ring = Scatter(ring, clock.tie(head_terms), TOP + middle, columns)
    sums[1].relay(clock)
    came = clock.tie(swap(clock.tie(grad_send), 1))
    last = swap(clock.tie(other_half(grad_keep, came)), 2)
    head_ring.relay(clock)
    last = clock.tie(last)
    firsts = list(clock.tie(*firsts))
    grad_input = first_norm_back(
        grad_hidden, mine, grad_keep, came, last, gains, ring.slot_owners(), n_dp
    )
    clock.done(grad_input)
    second_sum = sums[1].finish(clock)
    second_across, second_beside = swap(second_sum, 2), swap(second_sum, 1)
    head_ring.relay(clock)
    down_came = clock.tie(down_came)
    result = layer_output(hidden, down_keep, down_came, down_last, ring.slot_owners(), n_dp)
    clock.done(result)
    head_ring.relay(clock)
    second_across = clock.tie(second_across)
    others = four(second_sum, second_across, second_beside)
    head_sum = head_ring.finish(clock)
    head_across, head_beside = swap(head_sum, 2), swap(head_sum, 1)
    firsts, others = list(clock.tie(*firsts)), list(clock.tie(*others))
    grad_gate, grad_up, grad_down = unpack_mlp(places, [firsts, others], bounds, width, ff)
    clock.done(grad_gate)
    head_across = clock.tie(head_across)
    head_blocks = four(head_sum, head_across, head_beside)
    grad_query, grad_key, grad_value, grad_out, gain_sums = unpack_heads(
        places, list(clock.tie(*head_blocks)), width, q_cols
    )
    if width % 128:
        slots = ring.owner_slots()
        result = blocks_in_order(result, slots, n_dp)
        grad_input = blocks_in_order(grad_input, slots, n_dp)

    return (
        result,
        grad_input,
        gain_sums[0, :width],
        grad_query,
        grad_key,
        grad_value,
        grad_out,
        gain_sums[0, width:],
        grad_gate,
        grad_up,
        grad_down,
    )


def solution(mesh):
    return jax.shard_map(
        layer,
        mesh=mesh,
        in_specs=(
            P(("dp", "seq"), None),
            P(("dp", "seq"), None),
            P("dp"),
            P("dp", None),
            P("dp", None),
            P("dp", None),
            P(None, "dp"),
            P("dp"),
            P("dp", None),
            P("dp", None),
            P(None, "dp"),
            P("dp", None),
            P("dp"),
        ),
        out_specs=(
            P(("dp", "seq"), None),
            P(("dp", "seq"), None),
            P("dp"),
            P("dp", None),
            P("dp", None),
            P("dp", None),
            P(None, "dp"),
            P("dp"),
            P("dp", None),
            P("dp", None),
            P(None, "dp"),
        ),
        check_vma=False,
    )
```

```python
import functools

import jax
import jax.numpy as jnp
from jax import lax
from jax.experimental import pallas as pl
from jax.experimental.pallas import tpu as pltpu
from jax.sharding import PartitionSpec as P

HEADS = 32
HD = 64
KVH = 4
EPS = 1e-05
TOP = 16
BF = jnp.bfloat16
F32 = jnp.float32
NEG = -1e30
LIMITS = {
    "attention_forward": 20,
    "attention_backward": 16,
    "heads_back": 14,
    "mlp_half": 26,
    "mlp_half_far": 44,
    "weight_terms": 14,
    "unpack_mlp": 28,
    "unpack_heads": 12,
    "permute_features": 56,
    "pack_heads": 56,
    "pack_mlp": 56,
}


def limits(name):
    return pltpu.CompilerParams(vmem_limit_bytes=LIMITS.get(name, 12) << 20)


COST = pl.CostEstimate(flops=1000, transcendentals=0, bytes_accessed=1000)


def dot(left_side, right_side):
    return jnp.dot(left_side, right_side, preferred_element_type=F32)


def cross(left_side, right_side):
    return lax.dot_general(
        left_side, right_side, (((0,), (0,)), ((), ())), preferred_element_type=F32
    )


def against(left_side, right_side):
    return lax.dot_general(
        left_side, right_side, (((1,), (1,)), ((), ())), preferred_element_type=F32
    )


def kernel_call(body, outs, scratch=(), flops=0, moved=0, smem=0, args=(), name=None):
    vmem = pl.BlockSpec(memory_space=pltpu.VMEM)
    return pl.pallas_call(
        body,
        out_shape=tuple(jax.ShapeDtypeStruct(s, d) for s, d in outs),
        in_specs=[pl.BlockSpec(memory_space=pltpu.SMEM)] * smem + [vmem] * (len(args) - smem),
        out_specs=tuple(vmem for _ in outs),
        scratch_shapes=list(scratch),
        compiler_params=limits(name),
        cost_estimate=COST,
        name=name,
    )(*args)


class Ring:
    def __init__(self, size):
        self.size = size
        self.half = size // 2
        self.order = list(range(0, size, 2)) + list(range(size - 1, 0, -2))
        place = [0] * size
        for position, device in enumerate(self.order):
            place[device] = position
        self.place = place
        walk = [(self.order[i], self.order[(i + 1) % size]) for i in range(size)]
        self.up = walk
        self.down = [(b, a) for a, b in walk]
        self.steps = (
            [-t for t in range(self.half)] + [t for t in range(1, self.half)] + [self.half]
        )

    def slot_owners(self):
        mine = jnp.asarray(self.place, jnp.int32)[lax.axis_index("dp")]
        wanted = (mine + jnp.asarray(self.steps, jnp.int32)) % self.size
        return jnp.asarray(self.order, jnp.int32)[wanted]

    def owner_slots(self):
        mine = jnp.asarray(self.place, jnp.int32)[lax.axis_index("dp")]
        slot_of_step = [0] * self.size
        for slot, step in enumerate(self.steps):
            slot_of_step[step % self.size] = slot
        step = (jnp.asarray(self.place, jnp.int32) - mine) % self.size
        return jnp.asarray(slot_of_step, jnp.int32)[step]

    def go_up(self, block):
        return lax.ppermute(block, "dp", self.up)

    def go_down(self, block):
        return lax.ppermute(block, "dp", self.down)


class Clock:
    def __init__(self):
        self.last = None

    def tie(self, *arrays):
        if self.last is None:
            out = lax.optimization_barrier(arrays)
        else:
            out = lax.optimization_barrier((*arrays, self.last))[: len(arrays)]
        self.last = out[0]
        return out if len(out) > 1 else out[0]

    def done(self, array):
        self.last = array


class Gather:
    def __init__(self, ring, block, cut):
        self.ring, self.cut = ring, cut
        self.up, self.down = [block], [block]
        self.flying = (ring.go_up(block), ring.go_down(block))
        self.left = ring.half - 1

    def land(self, clock):
        up, down = clock.tie(*self.flying)
        self.flying = None
        self.up.append(up)
        self.down.append(down)

    def go(self, clock):
        up, down = clock.tie(self.up[-1], self.down[-1])
        self.left -= 1
        if self.left == 0:
            up, down = up[: self.cut], down[self.cut :]
        self.flying = (self.ring.go_up(up), self.ring.go_down(down))

    def relay(self, clock):
        if self.left:
            self.land(clock)
            self.go(clock)

    def finish(self, clock):
        while self.left:
            self.relay(clock)
        return self.up + self.down[1:] + list(clock.tie(*self.flying))


class Scatter:
    def __init__(self, ring, terms, cut, tile):
        self.ring, self.cut, self.tile = ring, cut, tile
        self.terms, up, down = terms
        self.full = self.terms.shape[0] // ring.size
        self.left = ring.half - 1
        self.flying = (ring.go_up(up), ring.go_down(down))

    def term(self, slot, begin=0, end=None):
        end = self.full if end is None else end
        return self.terms[slot * self.full + begin : slot * self.full + end]

    def relay(self, clock):
        if self.left == 0:
            return
        up, down = clock.tie(*self.flying)
        above, below = self.ring.half - 1 + self.left, self.left
        if up.shape[0] == self.full:
            up, down = plus(self.term(above), up), plus(self.term(below), down)
        else:
            up, down = ring_add(self.terms, (above, below), up, down, self.full, self.cut, self.tile)
        self.left -= 1
        up, down = clock.tie(up, down)
        self.flying = (self.ring.go_up(up), self.ring.go_down(down))

    def finish(self, clock):
        while self.left:
            self.relay(clock)
        up, down = clock.tie(*self.flying)
        out = (self.term(0).astype(F32) + up.astype(F32) + down.astype(F32)).astype(BF)
        return clock.tie(out)


def plus(one, two):
    return (one.astype(F32) + two.astype(F32)).astype(BF)


def swap(block, distance):
    return lax.ppermute(block, "seq", [(i, i ^ distance) for i in range(4)])


def fill_weights(pieces, scratch, top, width, columns):
    begin = 0
    for index, piece in enumerate(pieces):
        skip = top if index < len(pieces) - 1 else 0
        count = piece.shape[0] - skip
        scratch[begin : begin + count, :] = piece[skip:, columns]
        begin += count


def put_features(values, order_ref, target, slots, width):
    for j in range(slots):
        to = pl.ds(pl.multiple_of(order_ref[j] * width, 128), width)
        target[:, to] = values[:, j * width : (j + 1) * width]


def blocks_in_order(array, order, size):
    width = array.shape[1] // size
    return jnp.concatenate(
        [lax.dynamic_slice_in_dim(array, order[i] * width, width, 1) for i in range(size)],
        axis=1,
    )


def permute_features(array, order, size):
    width = array.shape[1] // size
    if width % 128:
        return blocks_in_order(array, order, size)

    def body(order_ref, source, target):
        for j in range(size):
            begin = pl.ds(pl.multiple_of(order_ref[j] * width, 128), width)
            target[:, j * width : (j + 1) * width] = source[:, begin]

    return kernel_call(
        body, [(array.shape, array.dtype)], smem=1, args=[order, array], name="permute_features"
    )[0]


def pack_heads(here, w_query, w_key, w_value, w_out, gain_attn, gain_mlp, seq):
    width = w_query.shape[0]
    q_cols, k_cols = w_query.shape[1] // seq, w_key.shape[1] // seq
    total = 2 * q_cols + 2 * k_cols

    def body(here_ref, query_ref, key_ref, value_ref, out_ref, one_ref, two_ref, block_ref):
        s = here_ref[0]
        block_ref[:TOP, :] = jnp.zeros((TOP, total), BF)
        block_ref[:1, :width] = one_ref[...].reshape(1, width)
        block_ref[:1, width : 2 * width] = two_ref[...].reshape(1, width)
        block_ref[TOP:, :q_cols] = query_ref[...]

        def mine(ref):
            part = jnp.zeros((width, k_cols), F32)
            for place in range(seq):
                piece = ref[:, place * k_cols : (place + 1) * k_cols].astype(F32)
                part = jnp.where(s == place, piece, part)
            return part

        both = jnp.concatenate([mine(key_ref), mine(value_ref)], axis=1)
        block_ref[TOP:, q_cols : q_cols + 2 * k_cols] = both.astype(BF)
        block_ref[TOP:, q_cols + 2 * k_cols :] = out_ref[...].astype(F32).T.astype(BF)

    whole = lambda shape: pl.BlockSpec(shape, lambda i, o: (0, 0))
    return pl.pallas_call(
        body,
        out_shape=jax.ShapeDtypeStruct((TOP + width, total), BF),
        grid_spec=pltpu.PrefetchScalarGridSpec(
            num_scalar_prefetch=1,
            grid=(1,),
            in_specs=[
                pl.BlockSpec((width, q_cols), lambda i, o: (0, o[0])),
                whole(w_key.shape),
                whole(w_value.shape),
                pl.BlockSpec((q_cols, width), lambda i, o: (o[0], 0)),
                pl.BlockSpec((width,), lambda i, o: (0,)),
                pl.BlockSpec((width,), lambda i, o: (0,)),
            ],
            out_specs=whole((TOP + width, total)),
        ),
        compiler_params=limits("pack_heads"),
        name="pack_heads",
    )(here, w_query, w_key, w_value, w_out, gain_attn, gain_mlp)


def pack_mlp(here, w_gate, w_up, w_down, bounds, seq):
    width, ff = w_gate.shape[0], w_gate.shape[1] // seq

    def body(here_ref, gate_ref, up_ref, down_ref, *blocks):
        for (a, b), block in zip(bounds, blocks):
            size = b - a
            block[:, :size] = gate_ref[:, a:b]
            block[:, size : 2 * size] = up_ref[:, a:b]
            block[:, 2 * size :] = down_ref[a:b, :].astype(F32).T.astype(BF)

    columns = pl.BlockSpec((width, ff), lambda i, o: (0, o[0]))
    return pl.pallas_call(
        body,
        out_shape=tuple(jax.ShapeDtypeStruct((width, 3 * (b - a)), BF) for a, b in bounds),
        grid_spec=pltpu.PrefetchScalarGridSpec(
            num_scalar_prefetch=1,
            grid=(1,),
            in_specs=[columns, columns, pl.BlockSpec((ff, width), lambda i, o: (o[0], 0))],
            out_specs=tuple(
                pl.BlockSpec((width, 3 * (b - a)), lambda i, o: (0, 0)) for a, b in bounds
            ),
        ),
        compiler_params=limits("pack_mlp"),
        name="pack_mlp",
    )(here, w_gate, w_up, w_down)


def turn(values, cosine, sine_part):
    half_dim = HD // 2
    pieces = []
    for h in range(values.shape[0] // HD):
        first = values[h * HD : h * HD + half_dim]
        second = values[h * HD + half_dim : (h + 1) * HD]
        pieces.append(first * cosine - second * sine_part)
        pieces.append(second * cosine + first * sine_part)
    return jnp.concatenate(pieces, axis=0)


def rounded(values):
    return values.astype(BF).astype(F32)


def pick(refs, place, target):
    for index, ref in enumerate(refs):

        @pl.when(place == index)
        def _():
            target[...] = ref[...]


def write_bias(bias_ref, lengths_ref, live, block, rows):
    keys = (block + 1) * rows
    query = lax.broadcasted_iota(jnp.int32, (1, rows), 1) + block * rows
    low = jnp.zeros((1, rows), jnp.int32)
    start = 0
    for slot in range(lengths_ref.shape[0]):
        low = jnp.where(query >= start, jnp.maximum(low, start), low)
        start = start + lengths_ref[slot]
    high = jnp.minimum(query, live - 1)
    key = lax.broadcasted_iota(jnp.int32, (keys, rows), 0)
    allowed = ((key >= low) & (key <= high)) | (key == query)
    bias_ref[:keys, :] = jnp.where(allowed, 0.0, NEG)


def attention_forward(places, lengths, live, tokens, pieces, cosine, sine_part, q_cols):
    rows, model = tokens[0].shape
    pack_size = 4 * rows
    n_heads = q_cols // HD
    heads_cols = q_cols + 2 * HD
    width = pieces[0].shape[0] - TOP

    def body(places_ref, lengths_ref, live_ref, cos_ref, sin_ref, *refs):
        token_refs, piece_refs, refs = refs[:4], refs[4 : 4 + len(pieces)], refs[4 + len(pieces) :]
        (
            normed_ref, query_ref, kv_ref, kvt_ref, lse_ref, mixed_t_ref, mixed_ref, keep_ref,
            send_ref, gains_ref, w_ref, bias_ref, query_s, mixed_s, tokens_s,
        ) = refs
        live_count = live_ref[0]
        fill_weights(piece_refs, w_ref, TOP, width, slice(None))
        gains_ref[...] = jnp.zeros_like(gains_ref)
        for index, piece in enumerate(piece_refs[:-1]):
            at = slice(index * width, (index + 1) * width)
            gains_ref[0:1, at] = piece[0:1, :width].astype(F32)
            gains_ref[1:2, at] = piece[0:1, width : 2 * width].astype(F32)
        ones = jnp.ones((HD, rows), BF)
        for block in range(4):
            place = places_ref[block]
            at = slice(block * rows, (block + 1) * rows)
            keys = (block + 1) * rows
            to = pl.ds(pl.multiple_of(place * rows, rows), rows)
            pick(token_refs, place, tokens_s)
            inputs = tokens_s[...].astype(F32)
            inverse = lax.rsqrt(jnp.mean(inputs * inputs, axis=1, keepdims=True) + EPS)
            normed = (inputs * inverse * gains_ref[0:1, :]).astype(BF)
            normed_ref[to, :] = normed
            pre = dot(normed, w_ref[:, :heads_cols]).T
            cos_b, sin_b = cos_ref[:, at], sin_ref[:, at]
            query = (rounded(turn(pre[:q_cols], cos_b, sin_b)) * HD**-0.5).astype(BF)
            query_s[...] = query
            query_ref[:, at] = query
            key_t = rounded(turn(pre[q_cols : q_cols + HD], cos_b, sin_b))
            value_t = rounded(pre[q_cols + HD :])
            kv_t = jnp.concatenate([key_t, value_t], axis=0)
            kv_ref[at, :] = kv_t.T.astype(BF)
            kvt_ref[: 2 * HD, at] = kv_t.astype(BF)
            kvt_ref[2 * HD :, at] = ones
            write_bias(bias_ref, lengths_ref, live_count, block, rows)

            def attend(h, _):
                mine = pl.ds(pl.multiple_of(h * HD, HD), HD)
                scores = dot(kv_ref[:keys, :HD], query_s[mine, :]) + bias_ref[:keys, :]
                peak = jnp.max(scores, axis=0, keepdims=True)
                weights = jnp.exp(scores - peak).astype(BF)
                summed = dot(kvt_ref[HD:, :keys], weights)
                total = summed[HD : HD + 1]
                mixed = summed[:HD] * (1.0 / total)
                mixed_s[mine, :] = mixed
                lse_ref[pl.ds(h, 1), at] = peak + jnp.log(total)
                return 0

            lax.fori_loop(0, n_heads, attend, 0, unroll=2)
            mixed_t = mixed_s[...]
            mixed_t_ref[:, at] = mixed_t
            mixed = mixed_t.T.astype(BF)
            mixed_ref[to, :] = mixed
            branch = against(mixed, w_ref[:, heads_cols:]).astype(BF)
            half_to = pl.ds(pl.multiple_of((place % 2) * rows, rows), rows)

            @pl.when(place < 2)
            def _():
                keep_ref[half_to, :] = branch

            @pl.when(place >= 2)
            def _():
                send_ref[half_to, :] = branch

    args = [places, lengths, live, cosine, sine_part, *tokens, *pieces]
    flops = 2 * pack_size * model * (heads_cols + q_cols) + 4 * n_heads * pack_size**2 * HD * 3
    return kernel_call(
        body,
        [
            ((pack_size, model), BF),
            ((q_cols, pack_size), BF),
            ((pack_size, 2 * HD), BF),
            ((3 * HD, pack_size), BF),
            ((n_heads, pack_size), F32),
            ((q_cols, pack_size), F32),
            ((pack_size, q_cols), BF),
            ((pack_size // 2, model), BF),
            ((pack_size // 2, model), BF),
            ((8, model), F32),
        ],
        scratch=[
            pltpu.VMEM((model, heads_cols + q_cols), BF),
            pltpu.VMEM((pack_size, rows), F32),
            pltpu.VMEM((q_cols, rows), BF),
            pltpu.VMEM((q_cols, rows), F32),
            pltpu.VMEM((rows, model), BF),
        ],
        flops=flops,
        moved=30 << 20,
        smem=3,
        args=args,
        name="attention_forward",
    )


def attention_backward(
    places, lengths, live, tokens, pieces, cosine, sine_part, query, kv, kvt, lse, mixed_t
):
    q_cols, pack_size = query.shape
    rows, model = tokens[0].shape
    n_heads = q_cols // HD
    heads_cols = q_cols + 2 * HD
    width = pieces[0].shape[0] - TOP

    def body(
        places_ref, lengths_ref, live_ref, cos_ref, sin_ref,
        query_ref, kv_ref, kvt_ref, lse_ref, mixed_t_ref, *refs
    ):
        token_refs, piece_refs, refs = refs[:4], refs[4 : 4 + len(pieces)], refs[4 + len(pieces) :]
        (
            grad_q_ref, grad_kv_ref, w_ref, bias_ref, grad_s, grad_q_s, key_acc, value_acc, inner_s,
            tokens_s,
        ) = refs
        live_count = live_ref[0]
        fill_weights(piece_refs, w_ref, TOP, width, slice(heads_cols, heads_cols + q_cols))
        key_acc[...] = jnp.zeros_like(key_acc)
        value_acc[...] = jnp.zeros_like(value_acc)
        for block in range(4):
            place = places_ref[block]
            at = slice(block * rows, (block + 1) * rows)
            keys = (block + 1) * rows
            to = pl.ds(pl.multiple_of(place * rows, rows), rows)
            pick(token_refs, place, tokens_s)
            grad_t = rounded(dot(tokens_s[...], w_ref[...]).T)
            grad_s[...] = grad_t.astype(BF)
            product = grad_t * mixed_t_ref[:, at]
            for h in range(n_heads):
                inner_s[h : h + 1, :] = jnp.sum(
                    product[h * HD : (h + 1) * HD], axis=0, keepdims=True
                )
            write_bias(bias_ref, lengths_ref, live_count, block, rows)

            def attend(h, _):
                mine = pl.ds(pl.multiple_of(h * HD, HD), HD)
                query_h = query_ref[mine, at]
                grad_h = grad_s[mine, :]
                scores = dot(kv_ref[:keys, :HD], query_h) + bias_ref[:keys, :]
                probs = jnp.exp(scores - lse_ref[pl.ds(h, 1), at])
                grad_probs = dot(kv_ref[:keys, HD:], grad_h)
                grad_scores = (probs * (grad_probs - inner_s[pl.ds(h, 1), :])).astype(BF)
                grad_q_s[mine, :] = dot(kvt_ref[:HD, :keys], grad_scores) * HD**-0.5
                key_acc[:keys, :] += against(grad_scores, query_h)
                value_acc[:keys, :] += against(probs.astype(BF), grad_h)
                return 0

            lax.fori_loop(0, n_heads, attend, 0, unroll=8)
            turned = turn(rounded(grad_q_s[...]), cos_ref[:, at], -sin_ref[:, at])
            grad_q_ref[to, :] = turned.T.astype(BF)
        for block in range(4):
            at = slice(block * rows, (block + 1) * rows)
            to = pl.ds(pl.multiple_of(places_ref[block] * rows, rows), rows)
            key_t = turn(rounded(key_acc[at, :]).T, cos_ref[:, at], -sin_ref[:, at])
            grad_kv_ref[to, :] = jnp.concatenate([key_t.T, value_acc[at, :]], axis=1).astype(BF)

    args = [
        places, lengths, live, cosine, sine_part, query, kv, kvt, lse, mixed_t, *tokens, *pieces
    ]
    return kernel_call(
        body,
        [((pack_size, q_cols), BF), ((pack_size, 2 * HD), BF)],
        scratch=[
            pltpu.VMEM((model, q_cols), BF),
            pltpu.VMEM((pack_size, rows), F32),
            pltpu.VMEM((q_cols, rows), BF),
            pltpu.VMEM((q_cols, rows), F32),
            pltpu.VMEM((pack_size, HD), F32),
            pltpu.VMEM((pack_size, HD), F32),
            pltpu.VMEM((n_heads, rows), F32),
            pltpu.VMEM((rows, model), BF),
        ],
        flops=2 * pack_size * model * q_cols + 10 * n_heads * pack_size**2 * HD * 3,
        moved=20 << 20,
        smem=3,
        args=args,
        name="attention_backward",
    )


def heads_back(grad_q, grad_kv, tokens, pieces):
    pack_size, q_cols = grad_q.shape
    rows, model = tokens[0].shape
    heads_cols = q_cols + 2 * HD
    width = pieces[0].shape[0] - TOP

    def body(grad_q_ref, grad_kv_ref, *refs):
        token_refs, piece_refs = refs[:4], refs[4 : 4 + len(pieces)]
        keep_ref, send_ref, gain_ref, w_ref, tokens_s = refs[4 + len(pieces) :]
        step = pl.program_id(0)

        @pl.when(step == 0)
        def _():
            fill_weights(piece_refs, w_ref, TOP, width, slice(0, heads_cols))
            gain_ref[...] = jnp.zeros_like(gain_ref)

        pick(token_refs, step, tokens_s)
        inputs = tokens_s[...].astype(F32)
        inverse = lax.rsqrt(jnp.mean(inputs * inputs, axis=1, keepdims=True) + EPS)
        grad = against(grad_q_ref[...], w_ref[:, :q_cols]) + against(
            grad_kv_ref[...], w_ref[:, q_cols:]
        )

        @pl.when(step < 2)
        def _():
            keep_ref[...] = grad.astype(BF)

        @pl.when(step >= 2)
        def _():
            send_ref[...] = grad.astype(BF)

        total = jnp.sum(grad * inputs * inverse, axis=0, keepdims=True)
        gain_ref[...] += jnp.broadcast_to(total, gain_ref.shape)

    first = pl.BlockSpec((rows, model), lambda i: (jnp.minimum(i, 1), 0))
    second = pl.BlockSpec((rows, model), lambda i: (jnp.maximum(i - 2, 0), 0))
    fixed = lambda a: pl.BlockSpec(memory_space=pltpu.VMEM)
    half = jax.ShapeDtypeStruct((pack_size // 2, model), BF)
    return pl.pallas_call(
        body,
        grid=(4,),
        out_shape=(half, half, jax.ShapeDtypeStruct((8, model), F32)),
        in_specs=[
            pl.BlockSpec((rows, q_cols), lambda i: (i, 0)),
            pl.BlockSpec((rows, 2 * HD), lambda i: (i, 0)),
        ]
        + [fixed(a) for a in (*tokens, *pieces)],
        out_specs=(first, second, pl.BlockSpec((8, model), lambda i: (0, 0))),
        scratch_shapes=[pltpu.VMEM((model, heads_cols), BF), pltpu.VMEM((rows, model), BF)],
        compiler_params=limits("heads_back"),
        cost_estimate=COST,
        name="heads_back",
    )(grad_q, grad_kv, *tokens, *pieces)


def mlp_half(tokens, cots, pieces, before, size, room="mlp_half"):
    rows, model = tokens[0].shape

    def body(*refs):
        token_refs, cot_refs, refs = refs[:2], refs[2:4], refs[4:]
        piece_refs, refs = refs[: len(pieces)], refs[len(pieces) :]
        before_refs, refs = refs[: len(before)], refs[len(before) :]
        down_ref, grad_ref, both_ref, w_ref, tokens_s, cot_s = refs
        step = pl.program_id(0)

        @pl.when(step == 0)
        def _():
            fill_weights(piece_refs, w_ref, 0, model, slice(None))

        pick(token_refs, step, tokens_s)
        pick(cot_refs, step, cot_s)
        both = dot(tokens_s[...], w_ref[:, : 2 * size])
        grad_act = dot(cot_s[...], w_ref[:, 2 * size :])
        gate_pre, up_pre = both[:, :size], both[:, size:]
        sig = 1.0 / (1.0 + jnp.exp(-gate_pre))
        active = gate_pre * sig
        both_ref[:, 2 * size :] = (active * up_pre).astype(BF)
        both_ref[:, size : 2 * size] = (grad_act * active).astype(BF)
        both_ref[:, :size] = (grad_act * up_pre * (sig + active * (1.0 - sig))).astype(BF)
        down = against(both_ref[:, 2 * size :], w_ref[:, 2 * size :])
        grad = against(both_ref[:, : 2 * size], w_ref[:, : 2 * size])
        if before_refs:
            down = down + before_refs[0][...].astype(F32)
            grad = grad + before_refs[1][...].astype(F32)
        down_ref[...] = down.astype(BF)
        grad_ref[...] = grad.astype(BF)

    by_rows = lambda cols: pl.BlockSpec((rows, cols), lambda i: (i, 0))
    fixed = lambda array: pl.BlockSpec(memory_space=pltpu.VMEM)
    half = jax.ShapeDtypeStruct((2 * rows, model), BF)
    return pl.pallas_call(
        body,
        grid=(2,),
        out_shape=(half, half, jax.ShapeDtypeStruct((2 * rows, 3 * size), BF)),
        in_specs=[fixed(a) for a in (*tokens, *cots, *pieces)] + [by_rows(model)] * len(before),
        out_specs=(by_rows(model), by_rows(model), by_rows(3 * size)),
        scratch_shapes=[
            pltpu.VMEM((model, 3 * size), BF),
            pltpu.VMEM((rows, model), BF),
            pltpu.VMEM((rows, model), BF),
        ],
        compiler_params=limits(room),
        cost_estimate=COST,
        name="mlp_half",
    )(*tokens, *cots, *pieces, *before)


def weight_terms(pairs, width, n_slots, group, cut, tops=None):
    tokens = sum(x.shape[0] for x in pairs[0][0])
    total = sum(cols.stop - cols.start for _, _, cols in pairs)
    head = 0 if tops is None else TOP

    def distinct(lists):
        out = []
        for one in lists:
            if not any(one is other for other in out):
                out.append(one)
        return out

    x_lists = distinct(x for x, _, _ in pairs)
    g_lists = distinct(g for _, g, _ in pairs)
    while (width * group) % 128:
        group *= 2
    wide = width * group
    args, specs = [], []
    for x in [x for xs in x_lists for x in xs]:
        args.append(x)
        specs.append(pl.BlockSpec((x.shape[0], wide), lambda i: (0, i)))
    for g in [g for gs in g_lists for g in gs]:
        args.append(g)
        specs.append(pl.BlockSpec(memory_space=pltpu.VMEM))
    if head:
        args.append(tops)
        specs.append(pl.BlockSpec((group * TOP, total), lambda i: (i, 0)))

    def body(*refs):
        def take(lists):
            nonlocal refs
            out = []
            for one in lists:
                out.append((one, refs[: len(one)]))
                refs = refs[len(one) :]
            return out

        x_refs, g_refs = take(x_lists), take(g_lists)
        out_ref, up_ref, down_ref, x_s = refs[-4:]
        lane = 0
        filled = None
        for xs, gs, cols in pairs:
            parts = next(r for other, r in x_refs if other is xs)
            g_parts = next(r for other, r in g_refs if other is gs)
            if len(parts) > 1 and filled is not xs:
                at = 0
                for part in parts:
                    x_s[at : at + part.shape[0], :] = part[...]
                    at += part.shape[0]
                filled = xs
            product, at = None, 0
            for g in g_parts:
                rows = g.shape[0]
                x = (x_s if len(parts) > 1 else parts[0])[at : at + rows, :]
                at += rows
                more = cross(x, g[:, cols])
                product = more if product is None else product + more
            product = product.astype(BF)
            count = cols.stop - cols.start
            for j in range(group):
                at = j * (head + width) + head
                out_ref[at : at + width, lane : lane + count] = product[
                    j * width : (j + 1) * width
                ]
            lane += count
        if head:
            for j in range(group):
                at = j * (head + width)
                out_ref[at : at + head, :] = refs[0][j * TOP : (j + 1) * TOP, :]

        @pl.when(pl.program_id(0) == n_slots // group - 1)
        def _():
            begin = (group - 1) * (head + width)
            up_ref[...] = out_ref[begin : begin + cut, :]
            down_ref[...] = out_ref[begin + cut : begin + head + width, :]

    far = [(cut, total), (head + width - cut, total)]
    return pl.pallas_call(
        body,
        grid=(n_slots // group,),
        out_shape=(
            jax.ShapeDtypeStruct((n_slots * (head + width), total), BF),
            *[jax.ShapeDtypeStruct(shape, BF) for shape in far],
        ),
        in_specs=specs,
        out_specs=(
            pl.BlockSpec((group * (head + width), total), lambda i: (i, 0)),
            *[pl.BlockSpec(shape, lambda i: (0, 0)) for shape in far],
        ),
        scratch_shapes=[pltpu.VMEM((tokens, wide), BF)],
        compiler_params=limits("weight_terms"),
        cost_estimate=COST,
        name="weight_terms",
    )(*args)


def ring_add(terms, slots, up, down, full, cut, tile):
    total = terms.shape[1]

    def body(up_term, down_term, up_ref, down_ref, up_out, down_out):
        if up_ref.shape[0] == full:
            up_out[...] = (up_term[...].astype(F32) + up_ref[...].astype(F32)).astype(BF)
            down_out[...] = (down_term[...].astype(F32) + down_ref[...].astype(F32)).astype(BF)
        else:
            up_out[:cut, :] = (up_term[:cut, :].astype(F32) + up_ref[...].astype(F32)).astype(BF)
            up_out[cut:, :] = up_term[cut:, :]
            down_out[:cut, :] = down_term[:cut, :]
            down_out[cut:, :] = (
                down_term[cut:, :].astype(F32) + down_ref[...].astype(F32)
            ).astype(BF)

    columns = lambda array: pl.BlockSpec((array.shape[0], tile), lambda i: (0, i))
    out = jax.ShapeDtypeStruct((full, total), BF)
    return pl.pallas_call(
        body,
        grid=(total // tile,),
        out_shape=(out, out),
        in_specs=[
            pl.BlockSpec((full, tile), lambda i: (slots[0], i)),
            pl.BlockSpec((full, tile), lambda i: (slots[1], i)),
            columns(up),
            columns(down),
        ],
        out_specs=(columns(out), columns(out)),
        compiler_params=limits("ring_add"),
        cost_estimate=COST,
        name="ring_add",
    )(terms, terms, up, down)


def row_call(body, outs, row_args, fixed_args, steps, smem=(), name=None):
    rows = outs[0][0][0] if outs[0][2] else row_args[0][0].shape[0]
    tile = rows // steps
    n_smem = len(smem)
    by_rows = lambda cols, at: pl.BlockSpec((tile, cols), lambda i, *_: (i + at, 0))
    return pl.pallas_call(
        body,
        out_shape=tuple(jax.ShapeDtypeStruct(s, d) for s, d, _ in outs),
        grid_spec=pltpu.PrefetchScalarGridSpec(
            num_scalar_prefetch=n_smem,
            grid=(steps,),
            in_specs=[by_rows(a.shape[1], at * steps) for a, at in row_args]
            + [pl.BlockSpec(a.shape, lambda i, *_: (0, 0)) for a in fixed_args],
            out_specs=tuple(
                by_rows(s[1], 0) if split else pl.BlockSpec(s, lambda i, *_: (0, 0))
                for s, _, split in outs
            ),
        ),
        compiler_params=limits(name),
        cost_estimate=COST,
        name=name,
    )(*smem, *[a for a, _ in row_args], *fixed_args)


STEPS = 2


def second_norm(inputs, keep, came, last, gains):
    def body(inputs_ref, keep_ref, came_ref, last_ref, gains_ref, hidden_ref, normed_ref):
        branch = keep_ref[...].astype(F32) + came_ref[...].astype(F32) + last_ref[...].astype(F32)
        hidden = inputs_ref[...].astype(F32) + branch
        inverse = lax.rsqrt(jnp.mean(hidden * hidden, axis=1, keepdims=True) + EPS)
        hidden_ref[...] = hidden
        normed_ref[...] = (hidden * inverse * gains_ref[1:2, :]).astype(BF)

    return row_call(
        body,
        [(inputs.shape, F32, True), (inputs.shape, BF, True)],
        [(inputs, 0), (keep, 0), (came, 0), (last, 0)],
        [gains],
        STEPS,
        name="second_norm",
    )


def norm_back(grad, values, gain):
    inverse = lax.rsqrt(jnp.mean(values * values, axis=1, keepdims=True) + EPS)
    scaled = grad * gain
    mean = jnp.mean(scaled * values, axis=1, keepdims=True)
    return inverse, inverse * (scaled - values * (inverse * inverse * mean))


def second_norm_back(cot, hidden, keep, came, last, gains):
    rows, model = hidden.shape

    def body(cot_ref, hidden_ref, keep_ref, came_ref, last_ref, gains_ref, grad_ref, low_ref, gain_ref):
        @pl.when(pl.program_id(0) == 0)
        def _():
            gain_ref[...] = jnp.zeros_like(gain_ref)

        grad = keep_ref[...].astype(F32) + came_ref[...].astype(F32) + last_ref[...].astype(F32)
        hidden_v = hidden_ref[...]
        inverse, back = norm_back(grad, hidden_v, gains_ref[1:2, :])
        total = jnp.sum(grad * hidden_v * inverse, axis=0, keepdims=True)
        gain_ref[...] += jnp.broadcast_to(total, gain_ref.shape)
        out = cot_ref[...].astype(F32) + back
        grad_ref[...] = out
        low_ref[...] = out.astype(BF)

    return row_call(
        body,
        [((rows, model), F32, True), ((rows, model), BF, True), ((8, model), F32, False)],
        [(cot, 0), (hidden, 0), (keep, 0), (came, 0), (last, 0)],
        [gains],
        STEPS,
        name="second_norm_back",
    )


def first_norm_back(grad_hidden, inputs, keep, came, last, gains, order, n_slots):
    width = inputs.shape[1] // n_slots

    def body(order_ref, grad_ref, inputs_ref, keep_ref, came_ref, last_ref, gains_ref, out_ref):
        grad = keep_ref[...].astype(F32) + came_ref[...].astype(F32) + last_ref[...].astype(F32)
        _, back = norm_back(grad, inputs_ref[...].astype(F32), gains_ref[0:1, :])
        out = (grad_ref[...] + back).astype(BF)
        if width % 128:
            out_ref[...] = out
        else:
            put_features(out, order_ref, out_ref, n_slots, width)

    return row_call(
        body,
        [(inputs.shape, BF, True)],
        [(grad_hidden, 0), (inputs, 0), (keep, 0), (came, 0), (last, 0)],
        [gains],
        STEPS,
        smem=(order,),
        name="first_norm_back",
    )[0]


def layer_output(hidden, keep, came, last, order, n_slots):
    width = hidden.shape[1] // n_slots

    def body(order_ref, hidden_ref, keep_ref, came_ref, last_ref, out_ref):
        down = keep_ref[...].astype(F32) + came_ref[...].astype(F32) + last_ref[...].astype(F32)
        out = (hidden_ref[...] + down).astype(BF)
        if width % 128:
            out_ref[...] = out
        else:
            put_features(out, order_ref, out_ref, n_slots, width)

    return row_call(
        body,
        [(hidden.shape, BF, True)],
        [(hidden, 0), (keep, 0), (came, 0), (last, 0)],
        [],
        STEPS,
        smem=(order,),
        name="layer_output",
    )[0]


def unpack_mlp(places, chunks, bounds, width, ff):
    flat = [block for blocks in chunks for block in blocks]

    def body(places_ref, *refs):
        ins = refs[: len(flat)]
        gate_ref, up_ref, down_ref = refs[len(flat) : len(flat) + 3]
        scratches = refs[len(flat) + 3 :]
        place = places_ref[pl.program_id(0)]
        for c, (a, b) in enumerate(bounds):
            size = b - a
            block_s = scratches[c]
            pick(ins[4 * c : 4 * c + 4], place, block_s)
            gate_ref[:, a:b] = block_s[:, :size].astype(F32)
            up_ref[:, a:b] = block_s[:, size : 2 * size].astype(F32)
            down_ref[a:b, :] = block_s[:, 2 * size :].astype(F32).T

    columns = pl.BlockSpec((width, ff), lambda i, p: (0, i))
    return pl.pallas_call(
        body,
        out_shape=(
            jax.ShapeDtypeStruct((width, 4 * ff), F32),
            jax.ShapeDtypeStruct((width, 4 * ff), F32),
            jax.ShapeDtypeStruct((4 * ff, width), F32),
        ),
        grid_spec=pltpu.PrefetchScalarGridSpec(
            num_scalar_prefetch=1,
            grid=(4,),
            in_specs=[
                pl.BlockSpec(h.shape, lambda i, p: (0, 0), pipeline_mode=pl.Buffered(1))
                for h in flat
            ],
            out_specs=(columns, columns, pl.BlockSpec((ff, width), lambda i, p: (i, 0))),
            scratch_shapes=[pltpu.VMEM((width, 3 * (b - a)), BF) for a, b in bounds],
        ),
        compiler_params=limits("unpack_mlp"),
        cost_estimate=COST,
        name="unpack_mlp",
    )(places, *flat)


def unpack_heads(places, heads, width, q_cols):
    kv = q_cols + 2 * HD

    def body(places_ref, *refs):
        head_refs = refs[:4]
        query_ref, key_ref, value_ref, out_ref, gain_ref, head_s = refs[4:]
        gain = jnp.zeros((8, 2 * width), F32)
        for place in range(4):
            pick(head_refs, places_ref[place], head_s)
            gain = gain + head_s[:TOP, : 2 * width].astype(F32)[:8]
            at = slice(place * q_cols, (place + 1) * q_cols)
            query_ref[:, at] = head_s[TOP:, :q_cols].astype(F32)
            both = head_s[TOP:, q_cols:kv].astype(F32)
            key_ref[:, place * HD : (place + 1) * HD] = both[:, :HD]
            value_ref[:, place * HD : (place + 1) * HD] = both[:, HD:]
            out_ref[at, :] = head_s[TOP:, kv:].astype(F32).T
        gain_ref[...] = gain

    args = [places, *heads]
    return kernel_call(
        body,
        [
            ((width, 4 * q_cols), F32),
            ((width, 4 * HD), F32),
            ((width, 4 * HD), F32),
            ((4 * q_cols, width), F32),
            ((8, 2 * width), F32),
        ],
        scratch=[pltpu.VMEM(heads[0].shape, BF)],
        smem=1,
        args=args,
        name="unpack_heads",
    )


def doc_positions(lengths, pack_size):
    doc_starts = jnp.cumsum(lengths) - lengths
    places = jnp.arange(pack_size, dtype=jnp.int32)
    doc_first = jnp.max(
        jnp.where(places[:, None] >= doc_starts[None, :], doc_starts[None, :], 0), axis=1
    )
    return places - doc_first


def rotary_tables(positions):
    half_dim = HD // 2
    frequency = 10000.0 ** (-2.0 * jnp.arange(half_dim, dtype=F32) / HD)
    angle_table = frequency[:, None] * positions.astype(F32)[None, :]
    return (jnp.cos(angle_table), jnp.sin(angle_table))


def layer(
    hidden_in,
    cotangent,
    gain_attn,
    w_query,
    w_key,
    w_value,
    w_out,
    gain_mlp,
    w_gate,
    w_up,
    w_down,
    doc_lengths,
    valid_count,
):
    seq = lax.axis_size("seq")
    n_dp = lax.axis_size("dp")
    here = lax.axis_index("seq").astype(jnp.int32)
    ring = Ring(n_dp)
    rows, model = hidden_in.shape
    pack_size = rows * seq
    width = gain_attn.shape[0]
    q_cols = w_query.shape[1] // seq
    ff = w_gate.shape[1] // seq
    here_1 = here.reshape(1)
    lengths, live = doc_lengths[0], valid_count[:1]
    middle = width // 2

    offset = here ^ jnp.arange(4, dtype=jnp.int32)
    places = (offset % 2) * 2 + offset // 2

    first = (ff // 2 + 127) // 128 * 128
    bounds = [(0, first), (first, ff)]
    sizes = [b - a for a, b in bounds]

    def other_half(keep, came):
        return plus(keep[rows:], came[rows:])

    def far_memory(*arrays):
        return [pltpu.with_memory_space_constraint(a, pltpu.HBM) for a in arrays]

    def four(block, across, beside):
        return [block, across, beside, swap(across, 1)]

    clock = Clock()
    head_block = pack_heads(here_1, w_query, w_key, w_value, w_out, gain_attn, gain_mlp, seq)
    clock.done(head_block)
    heads = Gather(ring, head_block, TOP + middle)
    hidden_in, cotangent = clock.tie(hidden_in, cotangent)
    mine = permute_features(hidden_in, ring.slot_owners(), n_dp)
    clock.done(mine)
    across, beside = swap(mine, 2), swap(mine, 1)
    w_gate, w_up, w_down, cotangent = clock.tie(w_gate, w_up, w_down, cotangent)
    blocks = pack_mlp(here_1, w_gate, w_up, w_down, bounds, seq)
    clock.done(blocks[0])
    heads.relay(clock)
    cotangent = clock.tie(cotangent)
    my_cot = permute_features(cotangent, ring.slot_owners(), n_dp)
    cosine, sine_part = rotary_tables(doc_positions(lengths, pack_size))
    cosine, sine_part, my_cot = clock.tie(cosine, sine_part, my_cot)
    heads.relay(clock)
    across, my_cot = clock.tie(across, my_cot)
    tokens = four(mine, across, beside)
    cot_across, cot_beside = swap(my_cot, 2), swap(my_cot, 1)
    heads.relay(clock)
    head_pieces = heads.finish(clock)
    tokens = list(clock.tie(*tokens))
    blocks = clock.tie(*blocks)
    chunks = [Gather(ring, block, middle) for block in blocks]
    normed, query, kv, kvt, lse, mixed_t, mixed, keep, send, gains = attention_forward(
        places, lengths, live, tokens, head_pieces, cosine, sine_part, q_cols
    )
    normed, query, kv, kvt, mixed_t, mixed = far_memory(normed, query, kv, kvt, mixed_t, mixed)
    clock.done(lse)
    chunks[0].relay(clock)
    chunks[1].land(clock)
    cot_across, send = clock.tie(cot_across, send)
    came = clock.tie(swap(send, 1))
    last = swap(clock.tie(other_half(keep, came)), 2)
    cots = four(my_cot, cot_across, cot_beside)
    chunks[0].relay(clock)
    last = clock.tie(last)
    hidden, my_normed = second_norm(mine, keep, came, last, gains)
    clock.done(my_normed)
    across, beside = swap(my_normed, 2), swap(my_normed, 1)
    beside = clock.tie(beside)
    chunks[0].relay(clock)
    across = clock.tie(across)
    seconds = four(my_normed, across, beside)
    pieces = chunks[0].finish(clock)
    chunks[1].go(clock)
    seconds = list(clock.tie(*seconds))
    cots = list(clock.tie(*cots))

    def terms_of(both, size):
        return weight_terms(
            [(seconds, both, slice(0, 2 * size)), (cots, both, slice(2 * size, 3 * size))],
            width,
            n_dp,
            2,
            middle,
        )

    down_send, grad_send, both_send = far_memory(
        *mlp_half(seconds[2:], cots[2:], pieces, (), sizes[0])
    )
    clock.done(both_send)
    first_two = clock.tie(*seconds[:2])
    down_keep, grad_keep, both_keep = far_memory(
        *mlp_half(first_two, cots[:2], pieces, (), sizes[0])
    )
    clock.done(both_keep)
    chunks[1].relay(clock)
    both = list(clock.tie(both_keep, both_send))
    terms = terms_of(both, sizes[0])
    clock.done(terms[0])
    chunks[1].relay(clock)
    pieces = far_memory(*chunks[1].finish(clock))
    sums = [Scatter(ring, clock.tie(*terms), middle, sizes[0])]
    down_send, grad_send, both_send = mlp_half(
        seconds[2:], cots[2:], clock.tie(*pieces), (down_send, grad_send), sizes[1], "mlp_half_far"
    )
    clock.done(both_send)
    both_send = far_memory(both_send)[0]
    sums[0].relay(clock)
    grad_send, down_send = clock.tie(grad_send, down_send)
    came, down_came = swap(grad_send, 1), swap(down_send, 1)
    first_two = clock.tie(*seconds[:2])
    down_keep, grad_keep, both_keep = mlp_half(
        first_two, cots[:2], pieces, (down_keep, grad_keep), sizes[1], "mlp_half_far"
    )
    both_keep = far_memory(both_keep)[0]
    clock.done(both_keep)
    came, down_came = clock.tie(came, down_came)
    last = swap(clock.tie(other_half(grad_keep, came)), 2)
    sums[0].relay(clock)
    both = list(clock.tie(both_keep, both_send))
    terms = terms_of(both, sizes[1])
    clock.done(terms[0])
    sums.append(Scatter(ring, clock.tie(*terms), middle, sizes[1]))
    last = clock.tie(last)
    grad_hidden, my_branch, gain_two_terms = second_norm_back(
        my_cot, hidden, grad_keep, came, last, gains
    )
    clock.done(my_branch)
    across, beside = swap(my_branch, 2), swap(my_branch, 1)
    down_other = clock.tie(other_half(down_keep, down_came))
    beside = clock.tie(beside)
    sums[0].relay(clock)
    sums[1].relay(clock)
    across = clock.tie(across)
    branches = four(my_branch, across, beside)
    branches = list(clock.tie(*branches))
    down_last = swap(clock.tie(down_other), 2)
    grad_q, grad_kv = attention_backward(
        places, lengths, live, branches, head_pieces, cosine, sine_part,
        query, kv, kvt, lse, mixed_t
    )
    clock.done(grad_kv)
    down_last, *tokens = clock.tie(down_last, *tokens)
    grad_keep, grad_send, gain_one_terms = heads_back(grad_q, grad_kv, tokens, head_pieces)
    clock.done(gain_one_terms)
    columns = head_block.shape[1]
    tops = jnp.concatenate(
        [
            gain_one_terms[0].reshape(n_dp, width),
            gain_two_terms[0].reshape(n_dp, width),
            jnp.zeros((n_dp, columns - 2 * width), F32),
        ],
        axis=1,
    ).astype(BF)
    tops = jnp.pad(tops[:, None], ((0, 0), (0, TOP - 1), (0, 0))).reshape(n_dp * TOP, -1)
    normed, tops = clock.tie(normed, tops)
    normed = [normed]
    head_terms = weight_terms(
        [
            (normed, [grad_q], slice(0, q_cols)),
            (normed, [grad_kv], slice(0, 2 * HD)),
            (branches, [mixed], slice(0, q_cols)),
        ],
        width,
        n_dp,
        2,
        TOP + middle,
        tops,
    )
    clock.done(head_terms[0])
    head_ring = Scatter(ring, head_terms, TOP + middle, columns)
    sums[1].relay(clock)
    chunk_sum = sums[0].finish(clock)
    chunk_across, chunk_beside = swap(chunk_sum, 2), swap(chunk_sum, 1)
    head_ring.relay(clock)
    came = clock.tie(swap(clock.tie(grad_send), 1))
    last = swap(clock.tie(other_half(grad_keep, came)), 2)
    chunk_beside = clock.tie(chunk_beside)
    sums[1].relay(clock)
    chunk_across = clock.tie(chunk_across)
    firsts = four(chunk_sum, chunk_across, chunk_beside)
    head_ring.relay(clock)
    firsts = list(clock.tie(*firsts))
    last = clock.tie(last)
    grad_input = first_norm_back(
        grad_hidden, mine, grad_keep, came, last, gains, ring.slot_owners(), n_dp
    )
    clock.done(grad_input)
    down_came = clock.tie(down_came)
    result = layer_output(hidden, down_keep, down_came, down_last, ring.slot_owners(), n_dp)
    clock.done(result)
    second_sum = sums[1].finish(clock)
    second_across, second_beside = swap(second_sum, 2), swap(second_sum, 1)
    second_beside = clock.tie(second_beside)
    head_ring.relay(clock)
    head_sum = head_ring.finish(clock)
    head_across, head_beside = swap(head_sum, 2), swap(head_sum, 1)
    second_across = clock.tie(second_across)
    others = four(second_sum, second_across, second_beside)
    others = list(clock.tie(*others))
    grad_gate, grad_up, grad_down = unpack_mlp(places, [firsts, others], bounds, width, ff)
    clock.done(grad_gate)
    head_across = clock.tie(head_across)
    head_blocks = four(head_sum, head_across, head_beside)
    grad_query, grad_key, grad_value, grad_out, gain_sums = unpack_heads(
        places, list(clock.tie(*head_blocks)), width, q_cols
    )
    if width % 128:
        slots = ring.owner_slots()
        result = blocks_in_order(result, slots, n_dp)
        grad_input = blocks_in_order(grad_input, slots, n_dp)

    return (
        result,
        grad_input,
        gain_sums[0, :width],
        grad_query,
        grad_key,
        grad_value,
        grad_out,
        gain_sums[0, width:],
        grad_gate,
        grad_up,
        grad_down,
    )


def solution(mesh):
    return jax.shard_map(
        layer,
        mesh=mesh,
        in_specs=(
            P(("dp", "seq"), None),
            P(("dp", "seq"), None),
            P("dp"),
            P("dp", None),
            P("dp", None),
            P("dp", None),
            P(None, "dp"),
            P("dp"),
            P("dp", None),
            P("dp", None),
            P(None, "dp"),
            P("dp", None),
            P("dp"),
        ),
        out_specs=(
            P(("dp", "seq"), None),
            P(("dp", "seq"), None),
            P("dp"),
            P("dp", None),
            P("dp", None),
            P("dp", None),
            P(None, "dp"),
            P("dp"),
            P("dp", None),
            P("dp", None),
            P(None, "dp"),
        ),
        check_vma=False,
    )
```

```python
import functools

import jax
import jax.numpy as jnp
from jax import lax
from jax.experimental import pallas as pl
from jax.experimental.pallas import tpu as pltpu
from jax.sharding import PartitionSpec as P

HEADS = 32
HD = 64
KVH = 4
EPS = 1e-05
TOP = 16
BF = jnp.bfloat16
F32 = jnp.float32
NEG = -1e30
LIMITS = {
    "attention_forward": 20,
    "attention_backward": 16,
    "heads_back": 14,
    "mlp_chunk": 26,
    "mlp_chunk_far": 44,
    "weight_terms": 14,
    "unpack_mlp": 28,
    "unpack_heads": 12,
    "permute_features": 56,
    "pack_heads": 56,
    "pack_mlp": 56,
}


def limits(name):
    return pltpu.CompilerParams(vmem_limit_bytes=LIMITS.get(name, 12) << 20)


COST = pl.CostEstimate(flops=1000, transcendentals=0, bytes_accessed=1000)


def dot(left_side, right_side):
    return jnp.dot(left_side, right_side, preferred_element_type=F32)


def cross(left_side, right_side):
    return lax.dot_general(
        left_side, right_side, (((0,), (0,)), ((), ())), preferred_element_type=F32
    )


def against(left_side, right_side):
    return lax.dot_general(
        left_side, right_side, (((1,), (1,)), ((), ())), preferred_element_type=F32
    )


def kernel_call(body, outs, scratch=(), flops=0, moved=0, smem=0, args=(), name=None):
    vmem = pl.BlockSpec(memory_space=pltpu.VMEM)
    return pl.pallas_call(
        body,
        out_shape=tuple(jax.ShapeDtypeStruct(s, d) for s, d in outs),
        in_specs=[pl.BlockSpec(memory_space=pltpu.SMEM)] * smem + [vmem] * (len(args) - smem),
        out_specs=tuple(vmem for _ in outs),
        scratch_shapes=list(scratch),
        compiler_params=limits(name),
        cost_estimate=COST,
        name=name,
    )(*args)


class Ring:
    def __init__(self, size):
        self.size = size
        self.half = size // 2
        self.order = list(range(0, size, 2)) + list(range(size - 1, 0, -2))
        place = [0] * size
        for position, device in enumerate(self.order):
            place[device] = position
        self.place = place
        walk = [(self.order[i], self.order[(i + 1) % size]) for i in range(size)]
        self.up = walk
        self.down = [(b, a) for a, b in walk]
        self.steps = (
            [-t for t in range(self.half)] + [t for t in range(1, self.half)] + [self.half]
        )

    def slot_owners(self):
        mine = jnp.asarray(self.place, jnp.int32)[lax.axis_index("dp")]
        wanted = (mine + jnp.asarray(self.steps, jnp.int32)) % self.size
        return jnp.asarray(self.order, jnp.int32)[wanted]

    def owner_slots(self):
        mine = jnp.asarray(self.place, jnp.int32)[lax.axis_index("dp")]
        slot_of_step = [0] * self.size
        for slot, step in enumerate(self.steps):
            slot_of_step[step % self.size] = slot
        step = (jnp.asarray(self.place, jnp.int32) - mine) % self.size
        return jnp.asarray(slot_of_step, jnp.int32)[step]

    def go_up(self, block):
        return lax.ppermute(block, "dp", self.up)

    def go_down(self, block):
        return lax.ppermute(block, "dp", self.down)


class Clock:
    def __init__(self):
        self.last = None

    def tie(self, *arrays):
        if self.last is None:
            out = lax.optimization_barrier(arrays)
        else:
            out = lax.optimization_barrier((*arrays, self.last))[: len(arrays)]
        self.last = out[0]
        return out if len(out) > 1 else out[0]

    def done(self, array):
        self.last = array


class Gather:
    def __init__(self, ring, block, cut):
        self.ring, self.cut = ring, cut
        self.up, self.down = [block], [block]
        self.flying = (ring.go_up(block), ring.go_down(block))
        self.left = ring.half - 1

    def land(self, clock):
        up, down = clock.tie(*self.flying)
        self.flying = None
        self.up.append(up)
        self.down.append(down)

    def go(self, clock):
        up, down = clock.tie(self.up[-1], self.down[-1])
        self.left -= 1
        if self.left == 0:
            up, down = up[: self.cut], down[self.cut :]
        self.flying = (self.ring.go_up(up), self.ring.go_down(down))

    def relay(self, clock):
        if self.left:
            self.land(clock)
            self.go(clock)

    def finish(self, clock):
        while self.left:
            self.relay(clock)
        return self.up + self.down[1:] + list(clock.tie(*self.flying))


class Scatter:
    def __init__(self, ring, terms, cut, tile):
        self.ring, self.cut, self.tile = ring, cut, tile
        self.terms, up, down = terms
        self.full = self.terms.shape[0] // ring.size
        self.left = ring.half - 1
        self.flying = (ring.go_up(up), ring.go_down(down))

    def term(self, slot, begin=0, end=None):
        end = self.full if end is None else end
        return self.terms[slot * self.full + begin : slot * self.full + end]

    def relay(self, clock):
        if self.left == 0:
            return
        up, down = clock.tie(*self.flying)
        above, below = self.ring.half - 1 + self.left, self.left
        if up.shape[0] == self.full:
            up, down = plus(self.term(above), up), plus(self.term(below), down)
        else:
            up, down = ring_add(self.terms, (above, below), up, down, self.full, self.cut, self.tile)
        self.left -= 1
        up, down = clock.tie(up, down)
        self.flying = (self.ring.go_up(up), self.ring.go_down(down))

    def finish(self, clock):
        while self.left:
            self.relay(clock)
        up, down = clock.tie(*self.flying)
        out = (self.term(0).astype(F32) + up.astype(F32) + down.astype(F32)).astype(BF)
        return clock.tie(out)


def plus(one, two):
    return (one.astype(F32) + two.astype(F32)).astype(BF)


def swap(block, distance):
    return lax.ppermute(block, "seq", [(i, i ^ distance) for i in range(4)])


def fill_weights(pieces, scratch, top, width, columns):
    begin = 0
    for index, piece in enumerate(pieces):
        skip = top if index < len(pieces) - 1 else 0
        count = piece.shape[0] - skip
        scratch[begin : begin + count, :] = piece[skip:, columns]
        begin += count


def put_features(values, order_ref, target, slots, width):
    for j in range(slots):
        to = pl.ds(pl.multiple_of(order_ref[j] * width, 128), width)
        target[:, to] = values[:, j * width : (j + 1) * width]


def blocks_in_order(array, order, size):
    width = array.shape[1] // size
    return jnp.concatenate(
        [lax.dynamic_slice_in_dim(array, order[i] * width, width, 1) for i in range(size)],
        axis=1,
    )


def permute_features(array, order, size):
    width = array.shape[1] // size
    if width % 128:
        return blocks_in_order(array, order, size)

    def body(order_ref, source, target):
        for j in range(size):
            begin = pl.ds(pl.multiple_of(order_ref[j] * width, 128), width)
            target[:, j * width : (j + 1) * width] = source[:, begin]

    return kernel_call(
        body, [(array.shape, array.dtype)], smem=1, args=[order, array], name="permute_features"
    )[0]


def pack_heads(here, w_query, w_key, w_value, w_out, gain_attn, gain_mlp, seq):
    width = w_query.shape[0]
    q_cols, k_cols = w_query.shape[1] // seq, w_key.shape[1] // seq
    total = 2 * q_cols + 2 * k_cols

    def body(here_ref, query_ref, key_ref, value_ref, out_ref, one_ref, two_ref, block_ref):
        s = here_ref[0]
        block_ref[:TOP, :] = jnp.zeros((TOP, total), BF)
        block_ref[:1, :width] = one_ref[...].reshape(1, width)
        block_ref[:1, width : 2 * width] = two_ref[...].reshape(1, width)
        block_ref[TOP:, :q_cols] = query_ref[...]

        def mine(ref):
            part = jnp.zeros((width, k_cols), F32)
            for place in range(seq):
                piece = ref[:, place * k_cols : (place + 1) * k_cols].astype(F32)
                part = jnp.where(s == place, piece, part)
            return part

        both = jnp.concatenate([mine(key_ref), mine(value_ref)], axis=1)
        block_ref[TOP:, q_cols : q_cols + 2 * k_cols] = both.astype(BF)
        block_ref[TOP:, q_cols + 2 * k_cols :] = out_ref[...].astype(F32).T.astype(BF)

    whole = lambda shape: pl.BlockSpec(shape, lambda i, o: (0, 0))
    return pl.pallas_call(
        body,
        out_shape=jax.ShapeDtypeStruct((TOP + width, total), BF),
        grid_spec=pltpu.PrefetchScalarGridSpec(
            num_scalar_prefetch=1,
            grid=(1,),
            in_specs=[
                pl.BlockSpec((width, q_cols), lambda i, o: (0, o[0])),
                whole(w_key.shape),
                whole(w_value.shape),
                pl.BlockSpec((q_cols, width), lambda i, o: (o[0], 0)),
                pl.BlockSpec((width,), lambda i, o: (0,)),
                pl.BlockSpec((width,), lambda i, o: (0,)),
            ],
            out_specs=whole((TOP + width, total)),
        ),
        compiler_params=limits("pack_heads"),
        name="pack_heads",
    )(here, w_query, w_key, w_value, w_out, gain_attn, gain_mlp)


def pack_mlp(here, w_gate, w_up, w_down, bounds, seq):
    width, ff = w_gate.shape[0], w_gate.shape[1] // seq

    def body(here_ref, gate_ref, up_ref, down_ref, *blocks):
        for (a, b), block in zip(bounds, blocks):
            size = b - a
            block[:, :size] = gate_ref[:, a:b]
            block[:, size : 2 * size] = up_ref[:, a:b]
            block[:, 2 * size :] = down_ref[a:b, :].astype(F32).T.astype(BF)

    columns = pl.BlockSpec((width, ff), lambda i, o: (0, o[0]))
    return pl.pallas_call(
        body,
        out_shape=tuple(jax.ShapeDtypeStruct((width, 3 * (b - a)), BF) for a, b in bounds),
        grid_spec=pltpu.PrefetchScalarGridSpec(
            num_scalar_prefetch=1,
            grid=(1,),
            in_specs=[columns, columns, pl.BlockSpec((ff, width), lambda i, o: (o[0], 0))],
            out_specs=tuple(
                pl.BlockSpec((width, 3 * (b - a)), lambda i, o: (0, 0)) for a, b in bounds
            ),
        ),
        compiler_params=limits("pack_mlp"),
        name="pack_mlp",
    )(here, w_gate, w_up, w_down)


def turn(values, cosine, sine_part):
    half_dim = HD // 2
    pieces = []
    for h in range(values.shape[0] // HD):
        first = values[h * HD : h * HD + half_dim]
        second = values[h * HD + half_dim : (h + 1) * HD]
        pieces.append(first * cosine - second * sine_part)
        pieces.append(second * cosine + first * sine_part)
    return jnp.concatenate(pieces, axis=0)


def rounded(values):
    return values.astype(BF).astype(F32)


def pick(refs, place, target):
    for index, ref in enumerate(refs):

        @pl.when(place == index)
        def _():
            target[...] = ref[...]


def write_bias(bias_ref, lengths_ref, live, block, rows):
    keys = (block + 1) * rows
    query = lax.broadcasted_iota(jnp.int32, (1, rows), 1) + block * rows
    low = jnp.zeros((1, rows), jnp.int32)
    start = 0
    for slot in range(lengths_ref.shape[0]):
        low = jnp.where(query >= start, jnp.maximum(low, start), low)
        start = start + lengths_ref[slot]
    high = jnp.minimum(query, live - 1)
    key = lax.broadcasted_iota(jnp.int32, (keys, rows), 0)
    allowed = ((key >= low) & (key <= high)) | (key == query)
    bias_ref[:keys, :] = jnp.where(allowed, 0.0, NEG)


def attention_forward(places, lengths, live, tokens, pieces, cosine, sine_part, q_cols):
    rows, model = tokens[0].shape
    pack_size = 4 * rows
    n_heads = q_cols // HD
    heads_cols = q_cols + 2 * HD
    width = pieces[0].shape[0] - TOP

    def body(places_ref, lengths_ref, live_ref, cos_ref, sin_ref, *refs):
        token_refs, piece_refs, refs = refs[:4], refs[4 : 4 + len(pieces)], refs[4 + len(pieces) :]
        (
            normed_ref, query_ref, kv_ref, kvt_ref, lse_ref, mixed_t_ref, mixed_ref, keep_ref,
            send_ref, gains_ref, w_ref, bias_ref, query_s, mixed_s, tokens_s,
        ) = refs
        live_count = live_ref[0]
        fill_weights(piece_refs, w_ref, TOP, width, slice(None))
        gains_ref[...] = jnp.zeros_like(gains_ref)
        for index, piece in enumerate(piece_refs[:-1]):
            at = slice(index * width, (index + 1) * width)
            gains_ref[0:1, at] = piece[0:1, :width].astype(F32)
            gains_ref[1:2, at] = piece[0:1, width : 2 * width].astype(F32)
        ones = jnp.ones((HD, rows), BF)
        for block in range(4):
            place = places_ref[block]
            at = slice(block * rows, (block + 1) * rows)
            keys = (block + 1) * rows
            to = pl.ds(pl.multiple_of(place * rows, rows), rows)
            pick(token_refs, place, tokens_s)
            inputs = tokens_s[...].astype(F32)
            inverse = lax.rsqrt(jnp.mean(inputs * inputs, axis=1, keepdims=True) + EPS)
            normed = (inputs * inverse * gains_ref[0:1, :]).astype(BF)
            normed_ref[to, :] = normed
            pre = dot(normed, w_ref[:, :heads_cols]).T
            cos_b, sin_b = cos_ref[:, at], sin_ref[:, at]
            query = (rounded(turn(pre[:q_cols], cos_b, sin_b)) * HD**-0.5).astype(BF)
            query_s[...] = query
            query_ref[:, at] = query
            key_t = rounded(turn(pre[q_cols : q_cols + HD], cos_b, sin_b))
            value_t = rounded(pre[q_cols + HD :])
            kv_t = jnp.concatenate([key_t, value_t], axis=0)
            kv_ref[at, :] = kv_t.T.astype(BF)
            kvt_ref[: 2 * HD, at] = kv_t.astype(BF)
            kvt_ref[2 * HD :, at] = ones
            write_bias(bias_ref, lengths_ref, live_count, block, rows)

            def attend(h, _):
                mine = pl.ds(pl.multiple_of(h * HD, HD), HD)
                scores = dot(kv_ref[:keys, :HD], query_s[mine, :]) + bias_ref[:keys, :]
                peak = jnp.max(scores, axis=0, keepdims=True)
                weights = jnp.exp(scores - peak).astype(BF)
                summed = dot(kvt_ref[HD:, :keys], weights)
                total = summed[HD : HD + 1]
                mixed = summed[:HD] * (1.0 / total)
                mixed_s[mine, :] = mixed
                lse_ref[pl.ds(h, 1), at] = peak + jnp.log(total)
                return 0

            lax.fori_loop(0, n_heads, attend, 0, unroll=2)
            mixed_t = mixed_s[...]
            mixed_t_ref[:, at] = mixed_t
            mixed = mixed_t.T.astype(BF)
            mixed_ref[to, :] = mixed
            branch = against(mixed, w_ref[:, heads_cols:]).astype(BF)
            half_to = pl.ds(pl.multiple_of((place % 2) * rows, rows), rows)

            @pl.when(place < 2)
            def _():
                keep_ref[half_to, :] = branch

            @pl.when(place >= 2)
            def _():
                send_ref[half_to, :] = branch

    args = [places, lengths, live, cosine, sine_part, *tokens, *pieces]
    flops = 2 * pack_size * model * (heads_cols + q_cols) + 4 * n_heads * pack_size**2 * HD * 3
    return kernel_call(
        body,
        [
            ((pack_size, model), BF),
            ((q_cols, pack_size), BF),
            ((pack_size, 2 * HD), BF),
            ((3 * HD, pack_size), BF),
            ((n_heads, pack_size), F32),
            ((q_cols, pack_size), F32),
            ((pack_size, q_cols), BF),
            ((pack_size // 2, model), BF),
            ((pack_size // 2, model), BF),
            ((8, model), F32),
        ],
        scratch=[
            pltpu.VMEM((model, heads_cols + q_cols), BF),
            pltpu.VMEM((pack_size, rows), F32),
            pltpu.VMEM((q_cols, rows), BF),
            pltpu.VMEM((q_cols, rows), F32),
            pltpu.VMEM((rows, model), BF),
        ],
        flops=flops,
        moved=30 << 20,
        smem=3,
        args=args,
        name="attention_forward",
    )


def attention_backward(
    places, lengths, live, tokens, pieces, cosine, sine_part, query, kv, kvt, lse, mixed_t
):
    q_cols, pack_size = query.shape
    rows, model = tokens[0].shape
    n_heads = q_cols // HD
    heads_cols = q_cols + 2 * HD
    width = pieces[0].shape[0] - TOP

    def body(
        places_ref, lengths_ref, live_ref, cos_ref, sin_ref,
        query_ref, kv_ref, kvt_ref, lse_ref, mixed_t_ref, *refs
    ):
        token_refs, piece_refs, refs = refs[:4], refs[4 : 4 + len(pieces)], refs[4 + len(pieces) :]
        (
            grad_q_ref, grad_kv_ref, w_ref, bias_ref, grad_s, grad_q_s, key_acc, value_acc, inner_s,
            tokens_s,
        ) = refs
        live_count = live_ref[0]
        fill_weights(piece_refs, w_ref, TOP, width, slice(heads_cols, heads_cols + q_cols))
        key_acc[...] = jnp.zeros_like(key_acc)
        value_acc[...] = jnp.zeros_like(value_acc)
        for block in range(4):
            place = places_ref[block]
            at = slice(block * rows, (block + 1) * rows)
            keys = (block + 1) * rows
            to = pl.ds(pl.multiple_of(place * rows, rows), rows)
            pick(token_refs, place, tokens_s)
            grad_t = rounded(dot(tokens_s[...], w_ref[...]).T)
            grad_s[...] = grad_t.astype(BF)
            product = grad_t * mixed_t_ref[:, at]
            for h in range(n_heads):
                inner_s[h : h + 1, :] = jnp.sum(
                    product[h * HD : (h + 1) * HD], axis=0, keepdims=True
                )
            write_bias(bias_ref, lengths_ref, live_count, block, rows)

            def attend(h, _):
                mine = pl.ds(pl.multiple_of(h * HD, HD), HD)
                query_h = query_ref[mine, at]
                grad_h = grad_s[mine, :]
                scores = dot(kv_ref[:keys, :HD], query_h) + bias_ref[:keys, :]
                probs = jnp.exp(scores - lse_ref[pl.ds(h, 1), at])
                grad_probs = dot(kv_ref[:keys, HD:], grad_h)
                grad_scores = (probs * (grad_probs - inner_s[pl.ds(h, 1), :])).astype(BF)
                grad_q_s[mine, :] = dot(kvt_ref[:HD, :keys], grad_scores) * HD**-0.5
                key_acc[:keys, :] += against(grad_scores, query_h)
                value_acc[:keys, :] += against(probs.astype(BF), grad_h)
                return 0

            lax.fori_loop(0, n_heads, attend, 0, unroll=8)
            turned = turn(rounded(grad_q_s[...]), cos_ref[:, at], -sin_ref[:, at])
            grad_q_ref[to, :] = turned.T.astype(BF)
        for block in range(4):
            at = slice(block * rows, (block + 1) * rows)
            to = pl.ds(pl.multiple_of(places_ref[block] * rows, rows), rows)
            key_t = turn(rounded(key_acc[at, :]).T, cos_ref[:, at], -sin_ref[:, at])
            grad_kv_ref[to, :] = jnp.concatenate([key_t.T, value_acc[at, :]], axis=1).astype(BF)

    args = [
        places, lengths, live, cosine, sine_part, query, kv, kvt, lse, mixed_t, *tokens, *pieces
    ]
    return kernel_call(
        body,
        [((pack_size, q_cols), BF), ((pack_size, 2 * HD), BF)],
        scratch=[
            pltpu.VMEM((model, q_cols), BF),
            pltpu.VMEM((pack_size, rows), F32),
            pltpu.VMEM((q_cols, rows), BF),
            pltpu.VMEM((q_cols, rows), F32),
            pltpu.VMEM((pack_size, HD), F32),
            pltpu.VMEM((pack_size, HD), F32),
            pltpu.VMEM((n_heads, rows), F32),
            pltpu.VMEM((rows, model), BF),
        ],
        flops=2 * pack_size * model * q_cols + 10 * n_heads * pack_size**2 * HD * 3,
        moved=20 << 20,
        smem=3,
        args=args,
        name="attention_backward",
    )


def heads_back(grad_q, grad_kv, tokens, pieces):
    pack_size, q_cols = grad_q.shape
    rows, model = tokens[0].shape
    heads_cols = q_cols + 2 * HD
    width = pieces[0].shape[0] - TOP

    def body(grad_q_ref, grad_kv_ref, *refs):
        token_refs, piece_refs = refs[:4], refs[4 : 4 + len(pieces)]
        keep_ref, send_ref, gain_ref, w_ref, tokens_s = refs[4 + len(pieces) :]
        step = pl.program_id(0)

        @pl.when(step == 0)
        def _():
            fill_weights(piece_refs, w_ref, TOP, width, slice(0, heads_cols))
            gain_ref[...] = jnp.zeros_like(gain_ref)

        pick(token_refs, step, tokens_s)
        inputs = tokens_s[...].astype(F32)
        inverse = lax.rsqrt(jnp.mean(inputs * inputs, axis=1, keepdims=True) + EPS)
        grad = against(grad_q_ref[...], w_ref[:, :q_cols]) + against(
            grad_kv_ref[...], w_ref[:, q_cols:]
        )

        @pl.when(step < 2)
        def _():
            keep_ref[...] = grad.astype(BF)

        @pl.when(step >= 2)
        def _():
            send_ref[...] = grad.astype(BF)

        total = jnp.sum(grad * inputs * inverse, axis=0, keepdims=True)
        gain_ref[...] += jnp.broadcast_to(total, gain_ref.shape)

    first = pl.BlockSpec((rows, model), lambda i: (jnp.minimum(i, 1), 0))
    second = pl.BlockSpec((rows, model), lambda i: (jnp.maximum(i - 2, 0), 0))
    fixed = lambda a: pl.BlockSpec(memory_space=pltpu.VMEM)
    half = jax.ShapeDtypeStruct((pack_size // 2, model), BF)
    return pl.pallas_call(
        body,
        grid=(4,),
        out_shape=(half, half, jax.ShapeDtypeStruct((8, model), F32)),
        in_specs=[
            pl.BlockSpec((rows, q_cols), lambda i: (i, 0)),
            pl.BlockSpec((rows, 2 * HD), lambda i: (i, 0)),
        ]
        + [fixed(a) for a in (*tokens, *pieces)],
        out_specs=(first, second, pl.BlockSpec((8, model), lambda i: (0, 0))),
        scratch_shapes=[pltpu.VMEM((model, heads_cols), BF), pltpu.VMEM((rows, model), BF)],
        compiler_params=limits("heads_back"),
        cost_estimate=COST,
        name="heads_back",
    )(grad_q, grad_kv, *tokens, *pieces)


def mlp_chunk(tokens, cots, pieces, before, size, room):
    rows, model = tokens[0].shape
    pack_size = 4 * rows

    def body(*refs):
        token_refs, cot_refs, refs = refs[:4], refs[4:8], refs[8:]
        piece_refs, refs = refs[: len(pieces)], refs[len(pieces) :]
        before_refs, refs = refs[: len(before)], refs[len(before) :]
        down_keep, down_send, grad_keep, grad_send, both_ref, w_ref, tokens_s, cot_s = refs
        step = pl.program_id(0)

        @pl.when(step == 0)
        def _():
            fill_weights(piece_refs, w_ref, 0, model, slice(None))

        pick(token_refs, step, tokens_s)
        pick(cot_refs, step, cot_s)
        both = dot(tokens_s[...], w_ref[:, : 2 * size])
        grad_act = dot(cot_s[...], w_ref[:, 2 * size :])
        gate_pre, up_pre = both[:, :size], both[:, size:]
        sig = 1.0 / (1.0 + jnp.exp(-gate_pre))
        active = gate_pre * sig
        both_ref[:, 2 * size :] = (active * up_pre).astype(BF)
        both_ref[:, size : 2 * size] = (grad_act * active).astype(BF)
        both_ref[:, :size] = (grad_act * up_pre * (sig + active * (1.0 - sig))).astype(BF)
        down = against(both_ref[:, 2 * size :], w_ref[:, 2 * size :])
        grad = against(both_ref[:, : 2 * size], w_ref[:, : 2 * size])

        def put(keep, send, value, keep_before, send_before):
            @pl.when(step < 2)
            def _():
                extra = 0.0 if keep_before is None else keep_before[...].astype(F32)
                keep[...] = (value + extra).astype(BF)

            @pl.when(step >= 2)
            def _():
                extra = 0.0 if send_before is None else send_before[...].astype(F32)
                send[...] = (value + extra).astype(BF)

        old = before_refs or [None] * 4
        put(down_keep, down_send, down, old[0], old[1])
        put(grad_keep, grad_send, grad, old[2], old[3])

    first = pl.BlockSpec((rows, model), lambda i: (jnp.minimum(i, 1), 0))
    second = pl.BlockSpec((rows, model), lambda i: (jnp.maximum(i - 2, 0), 0))
    fixed = pl.BlockSpec(memory_space=pltpu.VMEM)
    half = jax.ShapeDtypeStruct((pack_size // 2, model), BF)
    return pl.pallas_call(
        body,
        grid=(4,),
        out_shape=(half, half, half, half, jax.ShapeDtypeStruct((pack_size, 3 * size), BF)),
        in_specs=[fixed] * (8 + len(pieces)) + [first, second] * (len(before) // 2),
        out_specs=(first, second, first, second, pl.BlockSpec((rows, 3 * size), lambda i: (i, 0))),
        scratch_shapes=[
            pltpu.VMEM((model, 3 * size), BF),
            pltpu.VMEM((rows, model), BF),
            pltpu.VMEM((rows, model), BF),
        ],
        compiler_params=limits(room),
        cost_estimate=COST,
        name="mlp_chunk",
    )(*tokens, *cots, *pieces, *before)


def weight_terms(pairs, width, n_slots, group, cut, tops=None):
    tokens = sum(x.shape[0] for x in pairs[0][0])
    total = sum(cols.stop - cols.start for _, _, cols in pairs)
    head = 0 if tops is None else TOP

    def distinct(lists):
        out = []
        for one in lists:
            if not any(one is other for other in out):
                out.append(one)
        return out

    x_lists = distinct(x for x, _, _ in pairs)
    g_lists = distinct(g for _, g, _ in pairs)
    while (width * group) % 128:
        group *= 2
    wide = width * group
    args, specs = [], []
    for x in [x for xs in x_lists for x in xs]:
        args.append(x)
        specs.append(pl.BlockSpec((x.shape[0], wide), lambda i: (0, i)))
    for g in [g for gs in g_lists for g in gs]:
        args.append(g)
        specs.append(pl.BlockSpec(memory_space=pltpu.VMEM))
    if head:
        args.append(tops)
        specs.append(pl.BlockSpec((group * TOP, total), lambda i: (i, 0)))

    def body(*refs):
        def take(lists):
            nonlocal refs
            out = []
            for one in lists:
                out.append((one, refs[: len(one)]))
                refs = refs[len(one) :]
            return out

        x_refs, g_refs = take(x_lists), take(g_lists)
        out_ref, up_ref, down_ref, x_s = refs[-4:]
        lane = 0
        filled = None
        for xs, gs, cols in pairs:
            parts = next(r for other, r in x_refs if other is xs)
            g_parts = next(r for other, r in g_refs if other is gs)
            if len(parts) > 1 and filled is not xs:
                at = 0
                for part in parts:
                    x_s[at : at + part.shape[0], :] = part[...]
                    at += part.shape[0]
                filled = xs
            product, at = None, 0
            for g in g_parts:
                rows = g.shape[0]
                x = (x_s if len(parts) > 1 else parts[0])[at : at + rows, :]
                at += rows
                more = cross(x, g[:, cols])
                product = more if product is None else product + more
            product = product.astype(BF)
            count = cols.stop - cols.start
            for j in range(group):
                at = j * (head + width) + head
                out_ref[at : at + width, lane : lane + count] = product[
                    j * width : (j + 1) * width
                ]
            lane += count
        if head:
            for j in range(group):
                at = j * (head + width)
                out_ref[at : at + head, :] = refs[0][j * TOP : (j + 1) * TOP, :]

        @pl.when(pl.program_id(0) == n_slots // group - 1)
        def _():
            begin = (group - 1) * (head + width)
            up_ref[...] = out_ref[begin : begin + cut, :]
            down_ref[...] = out_ref[begin + cut : begin + head + width, :]

    far = [(cut, total), (head + width - cut, total)]
    return pl.pallas_call(
        body,
        grid=(n_slots // group,),
        out_shape=(
            jax.ShapeDtypeStruct((n_slots * (head + width), total), BF),
            *[jax.ShapeDtypeStruct(shape, BF) for shape in far],
        ),
        in_specs=specs,
        out_specs=(
            pl.BlockSpec((group * (head + width), total), lambda i: (i, 0)),
            *[pl.BlockSpec(shape, lambda i: (0, 0)) for shape in far],
        ),
        scratch_shapes=[pltpu.VMEM((tokens, wide), BF)],
        compiler_params=limits("weight_terms"),
        cost_estimate=COST,
        name="weight_terms",
    )(*args)


def ring_add(terms, slots, up, down, full, cut, tile):
    total = terms.shape[1]

    def body(up_term, down_term, up_ref, down_ref, up_out, down_out):
        if up_ref.shape[0] == full:
            up_out[...] = (up_term[...].astype(F32) + up_ref[...].astype(F32)).astype(BF)
            down_out[...] = (down_term[...].astype(F32) + down_ref[...].astype(F32)).astype(BF)
        else:
            up_out[:cut, :] = (up_term[:cut, :].astype(F32) + up_ref[...].astype(F32)).astype(BF)
            up_out[cut:, :] = up_term[cut:, :]
            down_out[:cut, :] = down_term[:cut, :]
            down_out[cut:, :] = (
                down_term[cut:, :].astype(F32) + down_ref[...].astype(F32)
            ).astype(BF)

    columns = lambda array: pl.BlockSpec((array.shape[0], tile), lambda i: (0, i))
    out = jax.ShapeDtypeStruct((full, total), BF)
    return pl.pallas_call(
        body,
        grid=(total // tile,),
        out_shape=(out, out),
        in_specs=[
            pl.BlockSpec((full, tile), lambda i: (slots[0], i)),
            pl.BlockSpec((full, tile), lambda i: (slots[1], i)),
            columns(up),
            columns(down),
        ],
        out_specs=(columns(out), columns(out)),
        compiler_params=limits("ring_add"),
        cost_estimate=COST,
        name="ring_add",
    )(terms, terms, up, down)


def row_call(body, outs, row_args, fixed_args, steps, smem=(), name=None):
    rows = outs[0][0][0] if outs[0][2] else row_args[0][0].shape[0]
    tile = rows // steps
    n_smem = len(smem)
    by_rows = lambda cols, at: pl.BlockSpec((tile, cols), lambda i, *_: (i + at, 0))
    return pl.pallas_call(
        body,
        out_shape=tuple(jax.ShapeDtypeStruct(s, d) for s, d, _ in outs),
        grid_spec=pltpu.PrefetchScalarGridSpec(
            num_scalar_prefetch=n_smem,
            grid=(steps,),
            in_specs=[by_rows(a.shape[1], at * steps) for a, at in row_args]
            + [pl.BlockSpec(a.shape, lambda i, *_: (0, 0)) for a in fixed_args],
            out_specs=tuple(
                by_rows(s[1], 0) if split else pl.BlockSpec(s, lambda i, *_: (0, 0))
                for s, _, split in outs
            ),
        ),
        compiler_params=limits(name),
        cost_estimate=COST,
        name=name,
    )(*smem, *[a for a, _ in row_args], *fixed_args)


STEPS = 2


def second_norm(inputs, keep, came, last, gains):
    def body(inputs_ref, keep_ref, came_ref, last_ref, gains_ref, hidden_ref, normed_ref):
        branch = keep_ref[...].astype(F32) + came_ref[...].astype(F32) + last_ref[...].astype(F32)
        hidden = inputs_ref[...].astype(F32) + branch
        inverse = lax.rsqrt(jnp.mean(hidden * hidden, axis=1, keepdims=True) + EPS)
        hidden_ref[...] = hidden
        normed_ref[...] = (hidden * inverse * gains_ref[1:2, :]).astype(BF)

    return row_call(
        body,
        [(inputs.shape, F32, True), (inputs.shape, BF, True)],
        [(inputs, 0), (keep, 0), (came, 0), (last, 0)],
        [gains],
        STEPS,
        name="second_norm",
    )


def norm_back(grad, values, gain):
    inverse = lax.rsqrt(jnp.mean(values * values, axis=1, keepdims=True) + EPS)
    scaled = grad * gain
    mean = jnp.mean(scaled * values, axis=1, keepdims=True)
    return inverse, inverse * (scaled - values * (inverse * inverse * mean))


def second_norm_back(cot, hidden, keep, came, last, gains):
    rows, model = hidden.shape

    def body(cot_ref, hidden_ref, keep_ref, came_ref, last_ref, gains_ref, grad_ref, low_ref, gain_ref):
        @pl.when(pl.program_id(0) == 0)
        def _():
            gain_ref[...] = jnp.zeros_like(gain_ref)

        grad = keep_ref[...].astype(F32) + came_ref[...].astype(F32) + last_ref[...].astype(F32)
        hidden_v = hidden_ref[...]
        inverse, back = norm_back(grad, hidden_v, gains_ref[1:2, :])
        total = jnp.sum(grad * hidden_v * inverse, axis=0, keepdims=True)
        gain_ref[...] += jnp.broadcast_to(total, gain_ref.shape)
        out = cot_ref[...].astype(F32) + back
        grad_ref[...] = out
        low_ref[...] = out.astype(BF)

    return row_call(
        body,
        [((rows, model), F32, True), ((rows, model), BF, True), ((8, model), F32, False)],
        [(cot, 0), (hidden, 0), (keep, 0), (came, 0), (last, 0)],
        [gains],
        STEPS,
        name="second_norm_back",
    )


def first_norm_back(grad_hidden, inputs, keep, came, last, gains, order, n_slots):
    width = inputs.shape[1] // n_slots

    def body(order_ref, grad_ref, inputs_ref, keep_ref, came_ref, last_ref, gains_ref, out_ref):
        grad = keep_ref[...].astype(F32) + came_ref[...].astype(F32) + last_ref[...].astype(F32)
        _, back = norm_back(grad, inputs_ref[...].astype(F32), gains_ref[0:1, :])
        out = (grad_ref[...] + back).astype(BF)
        if width % 128:
            out_ref[...] = out
        else:
            put_features(out, order_ref, out_ref, n_slots, width)

    return row_call(
        body,
        [(inputs.shape, BF, True)],
        [(grad_hidden, 0), (inputs, 0), (keep, 0), (came, 0), (last, 0)],
        [gains],
        STEPS,
        smem=(order,),
        name="first_norm_back",
    )[0]


def layer_output(hidden, keep, came, last, order, n_slots):
    width = hidden.shape[1] // n_slots

    def body(order_ref, hidden_ref, keep_ref, came_ref, last_ref, out_ref):
        down = keep_ref[...].astype(F32) + came_ref[...].astype(F32) + last_ref[...].astype(F32)
        out = (hidden_ref[...] + down).astype(BF)
        if width % 128:
            out_ref[...] = out
        else:
            put_features(out, order_ref, out_ref, n_slots, width)

    return row_call(
        body,
        [(hidden.shape, BF, True)],
        [(hidden, 0), (keep, 0), (came, 0), (last, 0)],
        [],
        STEPS,
        smem=(order,),
        name="layer_output",
    )[0]


def unpack_mlp(places, chunks, bounds, width, ff):
    flat = [block for blocks in chunks for block in blocks]

    def body(places_ref, *refs):
        ins = refs[: len(flat)]
        gate_ref, up_ref, down_ref = refs[len(flat) : len(flat) + 3]
        scratches = refs[len(flat) + 3 :]
        place = places_ref[pl.program_id(0)]
        for c, (a, b) in enumerate(bounds):
            size = b - a
            block_s = scratches[c]
            pick(ins[4 * c : 4 * c + 4], place, block_s)
            gate_ref[:, a:b] = block_s[:, :size].astype(F32)
            up_ref[:, a:b] = block_s[:, size : 2 * size].astype(F32)
            down_ref[a:b, :] = block_s[:, 2 * size :].astype(F32).T

    columns = pl.BlockSpec((width, ff), lambda i, p: (0, i))
    return pl.pallas_call(
        body,
        out_shape=(
            jax.ShapeDtypeStruct((width, 4 * ff), F32),
            jax.ShapeDtypeStruct((width, 4 * ff), F32),
            jax.ShapeDtypeStruct((4 * ff, width), F32),
        ),
        grid_spec=pltpu.PrefetchScalarGridSpec(
            num_scalar_prefetch=1,
            grid=(4,),
            in_specs=[
                pl.BlockSpec(h.shape, lambda i, p: (0, 0), pipeline_mode=pl.Buffered(1))
                for h in flat
            ],
            out_specs=(columns, columns, pl.BlockSpec((ff, width), lambda i, p: (i, 0))),
            scratch_shapes=[pltpu.VMEM((width, 3 * (b - a)), BF) for a, b in bounds],
        ),
        compiler_params=limits("unpack_mlp"),
        cost_estimate=COST,
        name="unpack_mlp",
    )(places, *flat)


def unpack_heads(places, heads, width, q_cols):
    kv = q_cols + 2 * HD

    def body(places_ref, *refs):
        head_refs = refs[:4]
        query_ref, key_ref, value_ref, out_ref, gain_ref, head_s = refs[4:]
        gain = jnp.zeros((8, 2 * width), F32)
        for place in range(4):
            pick(head_refs, places_ref[place], head_s)
            gain = gain + head_s[:TOP, : 2 * width].astype(F32)[:8]
            at = slice(place * q_cols, (place + 1) * q_cols)
            query_ref[:, at] = head_s[TOP:, :q_cols].astype(F32)
            both = head_s[TOP:, q_cols:kv].astype(F32)
            key_ref[:, place * HD : (place + 1) * HD] = both[:, :HD]
            value_ref[:, place * HD : (place + 1) * HD] = both[:, HD:]
            out_ref[at, :] = head_s[TOP:, kv:].astype(F32).T
        gain_ref[...] = gain

    args = [places, *heads]
    return kernel_call(
        body,
        [
            ((width, 4 * q_cols), F32),
            ((width, 4 * HD), F32),
            ((width, 4 * HD), F32),
            ((4 * q_cols, width), F32),
            ((8, 2 * width), F32),
        ],
        scratch=[pltpu.VMEM(heads[0].shape, BF)],
        smem=1,
        args=args,
        name="unpack_heads",
    )


def doc_positions(lengths, pack_size):
    doc_starts = jnp.cumsum(lengths) - lengths
    places = jnp.arange(pack_size, dtype=jnp.int32)
    doc_first = jnp.max(
        jnp.where(places[:, None] >= doc_starts[None, :], doc_starts[None, :], 0), axis=1
    )
    return places - doc_first


def rotary_tables(positions):
    half_dim = HD // 2
    frequency = 10000.0 ** (-2.0 * jnp.arange(half_dim, dtype=F32) / HD)
    angle_table = frequency[:, None] * positions.astype(F32)[None, :]
    return (jnp.cos(angle_table), jnp.sin(angle_table))


def layer(
    hidden_in,
    cotangent,
    gain_attn,
    w_query,
    w_key,
    w_value,
    w_out,
    gain_mlp,
    w_gate,
    w_up,
    w_down,
    doc_lengths,
    valid_count,
):
    seq = lax.axis_size("seq")
    n_dp = lax.axis_size("dp")
    here = lax.axis_index("seq").astype(jnp.int32)
    ring = Ring(n_dp)
    rows, model = hidden_in.shape
    pack_size = rows * seq
    width = gain_attn.shape[0]
    q_cols = w_query.shape[1] // seq
    ff = w_gate.shape[1] // seq
    here_1 = here.reshape(1)
    lengths, live = doc_lengths[0], valid_count[:1]
    middle = width // 2

    offset = here ^ jnp.arange(4, dtype=jnp.int32)
    places = (offset % 2) * 2 + offset // 2

    first = (ff // 2 + 127) // 128 * 128
    bounds = [(0, first), (first, ff)]
    sizes = [b - a for a, b in bounds]

    def other_half(keep, came):
        return plus(keep[rows:], came[rows:])

    def far_memory(*arrays):
        return [pltpu.with_memory_space_constraint(a, pltpu.HBM) for a in arrays]

    def four(block, across, beside):
        return [block, across, beside, swap(across, 1)]

    clock = Clock()
    head_block = pack_heads(here_1, w_query, w_key, w_value, w_out, gain_attn, gain_mlp, seq)
    clock.done(head_block)
    heads = Gather(ring, head_block, TOP + middle)
    hidden_in, cotangent = clock.tie(hidden_in, cotangent)
    mine = permute_features(hidden_in, ring.slot_owners(), n_dp)
    clock.done(mine)
    across, beside = swap(mine, 2), swap(mine, 1)
    w_gate, w_up, w_down, cotangent = clock.tie(w_gate, w_up, w_down, cotangent)
    blocks = pack_mlp(here_1, w_gate, w_up, w_down, bounds, seq)
    clock.done(blocks[0])
    heads.relay(clock)
    cotangent = clock.tie(cotangent)
    my_cot = permute_features(cotangent, ring.slot_owners(), n_dp)
    cosine, sine_part = rotary_tables(doc_positions(lengths, pack_size))
    cosine, sine_part, my_cot = clock.tie(cosine, sine_part, my_cot)
    heads.relay(clock)
    across, my_cot = clock.tie(across, my_cot)
    tokens = four(mine, across, beside)
    cot_across, cot_beside = swap(my_cot, 2), swap(my_cot, 1)
    heads.relay(clock)
    head_pieces = heads.finish(clock)
    tokens = list(clock.tie(*tokens))
    blocks = clock.tie(*blocks)
    chunks = [Gather(ring, block, middle) for block in blocks]
    normed, query, kv, kvt, lse, mixed_t, mixed, keep, send, gains = attention_forward(
        places, lengths, live, tokens, head_pieces, cosine, sine_part, q_cols
    )
    normed, query, kv, kvt, mixed_t, mixed = far_memory(normed, query, kv, kvt, mixed_t, mixed)
    clock.done(lse)
    chunks[0].relay(clock)
    chunks[1].land(clock)
    cot_across, send = clock.tie(cot_across, send)
    came = clock.tie(swap(send, 1))
    last = swap(clock.tie(other_half(keep, came)), 2)
    cots = four(my_cot, cot_across, cot_beside)
    chunks[0].relay(clock)
    last = clock.tie(last)
    hidden, my_normed = second_norm(mine, keep, came, last, gains)
    clock.done(my_normed)
    across, beside = swap(my_normed, 2), swap(my_normed, 1)
    beside = clock.tie(beside)
    chunks[0].relay(clock)
    across = clock.tie(across)
    seconds = four(my_normed, across, beside)
    pieces = chunks[0].finish(clock)
    chunks[1].go(clock)
    seconds = list(clock.tie(*seconds))
    cots = list(clock.tie(*cots))

    def terms_of(both, size):
        return weight_terms(
            [(seconds, [both], slice(0, 2 * size)), (cots, [both], slice(2 * size, 3 * size))],
            width,
            n_dp,
            2,
            middle,
        )

    *before, both = far_memory(*mlp_chunk(seconds, cots, pieces, (), sizes[0], "mlp_chunk"))
    clock.done(both)
    chunks[1].relay(clock)
    terms = terms_of(clock.tie(both), sizes[0])
    clock.done(terms[0])
    sums = [Scatter(ring, terms, middle, sizes[0])]
    chunks[1].relay(clock)
    pieces = far_memory(*chunks[1].finish(clock))
    sums[0].relay(clock)
    down_keep, down_send, grad_keep, grad_send, both = mlp_chunk(
        seconds, cots, clock.tie(*pieces), before, sizes[1], "mlp_chunk_far"
    )
    both = far_memory(both)[0]
    clock.done(both)
    sums[0].relay(clock)
    grad_send, down_send = clock.tie(grad_send, down_send)
    came, down_came = swap(grad_send, 1), swap(down_send, 1)
    came = clock.tie(came)
    last = swap(clock.tie(other_half(grad_keep, came)), 2)
    terms = terms_of(clock.tie(both), sizes[1])
    clock.done(terms[0])
    sums.append(Scatter(ring, terms, middle, sizes[1]))
    down_came = clock.tie(down_came)
    sums[0].relay(clock)
    sums[1].relay(clock)
    last = clock.tie(last)
    grad_hidden, my_branch, gain_two_terms = second_norm_back(
        my_cot, hidden, grad_keep, came, last, gains
    )
    clock.done(my_branch)
    across, beside = swap(my_branch, 2), swap(my_branch, 1)
    down_other = clock.tie(other_half(down_keep, down_came))
    beside = clock.tie(beside)
    chunk_sum = sums[0].finish(clock)
    chunk_across, chunk_beside = swap(chunk_sum, 2), swap(chunk_sum, 1)
    across = clock.tie(across)
    branches = four(my_branch, across, beside)
    branches = list(clock.tie(*branches))
    grad_q, grad_kv = attention_backward(
        places, lengths, live, branches, head_pieces, cosine, sine_part,
        query, kv, kvt, lse, mixed_t
    )
    clock.done(grad_kv)
    sums[1].relay(clock)
    chunk_across, chunk_beside = clock.tie(chunk_across, chunk_beside)
    firsts = four(chunk_sum, chunk_across, chunk_beside)
    down_last = swap(clock.tie(down_other), 2)
    tokens = clock.tie(*tokens)
    grad_keep, grad_send, gain_one_terms = heads_back(grad_q, grad_kv, tokens, head_pieces)
    clock.done(gain_one_terms)
    columns = head_block.shape[1]
    tops = jnp.concatenate(
        [
            gain_one_terms[0].reshape(n_dp, width),
            gain_two_terms[0].reshape(n_dp, width),
            jnp.zeros((n_dp, columns - 2 * width), F32),
        ],
        axis=1,
    ).astype(BF)
    tops = jnp.pad(tops[:, None], ((0, 0), (0, TOP - 1), (0, 0))).reshape(n_dp * TOP, -1)
    normed, tops = clock.tie(normed, tops)
    normed = [normed]
    head_terms = weight_terms(
        [
            (normed, [grad_q], slice(0, q_cols)),
            (normed, [grad_kv], slice(0, 2 * HD)),
            (branches, [mixed], slice(0, q_cols)),
        ],
        width,
        n_dp,
        2,
        TOP + middle,
        tops,
    )
    clock.done(head_terms[0])
    head_ring = Scatter(ring, head_terms, TOP + middle, columns)
    sums[1].relay(clock)
    firsts = list(clock.tie(*firsts))
    head_ring.relay(clock)
    down_last = clock.tie(down_last)
    came = clock.tie(swap(clock.tie(grad_send), 1))
    last = swap(clock.tie(other_half(grad_keep, came)), 2)
    second_sum = sums[1].finish(clock)
    second_across, second_beside = swap(second_sum, 2), swap(second_sum, 1)
    head_ring.relay(clock)
    down_came = clock.tie(down_came)
    result = layer_output(hidden, down_keep, down_came, down_last, ring.slot_owners(), n_dp)
    clock.done(result)
    last, second_beside = clock.tie(last, second_beside)
    grad_input = first_norm_back(
        grad_hidden, mine, grad_keep, came, last, gains, ring.slot_owners(), n_dp
    )
    clock.done(grad_input)
    head_ring.relay(clock)
    second_across = clock.tie(second_across)
    others = four(second_sum, second_across, second_beside)
    head_sum = head_ring.finish(clock)
    head_across, head_beside = swap(head_sum, 2), swap(head_sum, 1)
    others = list(clock.tie(*others))
    grad_gate, grad_up, grad_down = unpack_mlp(places, [firsts, others], bounds, width, ff)
    clock.done(grad_gate)
    head_across = clock.tie(head_across)
    head_blocks = four(head_sum, head_across, head_beside)
    grad_query, grad_key, grad_value, grad_out, gain_sums = unpack_heads(
        places, list(clock.tie(*head_blocks)), width, q_cols
    )
    if width % 128:
        slots = ring.owner_slots()
        result = blocks_in_order(result, slots, n_dp)
        grad_input = blocks_in_order(grad_input, slots, n_dp)

    return (
        result,
        grad_input,
        gain_sums[0, :width],
        grad_query,
        grad_key,
        grad_value,
        grad_out,
        gain_sums[0, width:],
        grad_gate,
        grad_up,
        grad_down,
    )


def solution(mesh):
    return jax.shard_map(
        layer,
        mesh=mesh,
        in_specs=(
            P(("dp", "seq"), None),
            P(("dp", "seq"), None),
            P("dp"),
            P("dp", None),
            P("dp", None),
            P("dp", None),
            P(None, "dp"),
            P("dp"),
            P("dp", None),
            P("dp", None),
            P(None, "dp"),
            P("dp", None),
            P("dp"),
        ),
        out_specs=(
            P(("dp", "seq"), None),
            P(("dp", "seq"), None),
            P("dp"),
            P("dp", None),
            P("dp", None),
            P("dp", None),
            P(None, "dp"),
            P("dp"),
            P("dp", None),
            P("dp", None),
            P(None, "dp"),
        ),
        check_vma=False,
    )
```

```python
import functools

import jax
import jax.numpy as jnp
from jax import lax
from jax.experimental import pallas as pl
from jax.experimental.pallas import tpu as pltpu
from jax.sharding import PartitionSpec as P

HEADS = 32
HD = 64
KVH = 4
EPS = 1e-05
TOP = 16
BF = jnp.bfloat16
F32 = jnp.float32
NEG = -1e30
LIMITS = {
    "attention_forward": 23,
    "attention_backward": 18,
    "heads_back": 15,
    "mlp_chunk": 29,
    "mlp_chunk_far": 44,
    "weight_terms": 15,
    "unpack_mlp": 28,
    "unpack_heads": 12,
    "permute_features": 56,
    "pack_heads": 56,
    "pack_mlp": 56,
}


def limits(name):
    return pltpu.CompilerParams(vmem_limit_bytes=LIMITS.get(name, 12) << 20)


COST = pl.CostEstimate(flops=1000, transcendentals=0, bytes_accessed=1000)


def dot(left_side, right_side):
    return jnp.dot(left_side, right_side, preferred_element_type=F32)


def cross(left_side, right_side):
    return lax.dot_general(
        left_side, right_side, (((0,), (0,)), ((), ())), preferred_element_type=F32
    )


def against(left_side, right_side):
    return lax.dot_general(
        left_side, right_side, (((1,), (1,)), ((), ())), preferred_element_type=F32
    )


def kernel_call(body, outs, scratch=(), flops=0, moved=0, smem=0, args=(), name=None):
    vmem = pl.BlockSpec(memory_space=pltpu.VMEM)
    return pl.pallas_call(
        body,
        out_shape=tuple(jax.ShapeDtypeStruct(s, d) for s, d in outs),
        in_specs=[pl.BlockSpec(memory_space=pltpu.SMEM)] * smem + [vmem] * (len(args) - smem),
        out_specs=tuple(vmem for _ in outs),
        scratch_shapes=list(scratch),
        compiler_params=limits(name),
        cost_estimate=COST,
        name=name,
    )(*args)


class Ring:
    def __init__(self, size):
        self.size = size
        self.half = size // 2
        self.order = list(range(0, size, 2)) + list(range(size - 1, 0, -2))
        place = [0] * size
        for position, device in enumerate(self.order):
            place[device] = position
        self.place = place
        walk = [(self.order[i], self.order[(i + 1) % size]) for i in range(size)]
        self.up = walk
        self.down = [(b, a) for a, b in walk]
        self.steps = (
            [-t for t in range(self.half)] + [t for t in range(1, self.half)] + [self.half]
        )

    def slot_owners(self):
        mine = jnp.asarray(self.place, jnp.int32)[lax.axis_index("dp")]
        wanted = (mine + jnp.asarray(self.steps, jnp.int32)) % self.size
        return jnp.asarray(self.order, jnp.int32)[wanted]

    def owner_slots(self):
        mine = jnp.asarray(self.place, jnp.int32)[lax.axis_index("dp")]
        slot_of_step = [0] * self.size
        for slot, step in enumerate(self.steps):
            slot_of_step[step % self.size] = slot
        step = (jnp.asarray(self.place, jnp.int32) - mine) % self.size
        return jnp.asarray(slot_of_step, jnp.int32)[step]

    def go_up(self, block):
        return lax.ppermute(block, "dp", self.up)

    def go_down(self, block):
        return lax.ppermute(block, "dp", self.down)


class Clock:
    def __init__(self):
        self.last = None

    def tie(self, *arrays):
        if self.last is None:
            out = lax.optimization_barrier(arrays)
        else:
            out = lax.optimization_barrier((*arrays, self.last))[: len(arrays)]
        self.last = out[0]
        return out if len(out) > 1 else out[0]

    def done(self, array):
        self.last = array


class Gather:
    def __init__(self, ring, block, cut):
        self.ring, self.cut = ring, cut
        self.up, self.down = [block], [block]
        self.flying = (ring.go_up(block), ring.go_down(block))
        self.left = ring.half - 1

    def land(self, clock):
        up, down = clock.tie(*self.flying)
        self.flying = None
        self.up.append(up)
        self.down.append(down)

    def go(self, clock):
        up, down = clock.tie(self.up[-1], self.down[-1])
        self.left -= 1
        if self.left == 0:
            up, down = up[: self.cut], down[self.cut :]
        self.flying = (self.ring.go_up(up), self.ring.go_down(down))

    def relay(self, clock):
        if self.left == 0:
            return
        self.left -= 1
        up = clock.tie(self.flying[0])
        self.up.append(up)
        up = self.ring.go_up(up if self.left else up[: self.cut])
        down = clock.tie(self.flying[1])
        self.down.append(down)
        self.flying = (up, self.ring.go_down(down if self.left else down[self.cut :]))

    def finish(self, clock):
        while self.left:
            self.relay(clock)
        return self.up + self.down[1:] + list(clock.tie(*self.flying))


class Scatter:
    def __init__(self, ring, terms, cut, tile):
        self.ring, self.cut, self.tile = ring, cut, tile
        self.terms, up, down = terms
        self.full = self.terms.shape[0] // ring.size
        self.left = ring.half - 1
        self.flying = (ring.go_up(up), ring.go_down(down))

    def term(self, slot, begin=0, end=None):
        end = self.full if end is None else end
        return self.terms[slot * self.full + begin : slot * self.full + end]

    def land(self, clock):
        self.relay(clock, hold=True)

    def go(self, clock):
        up, down = clock.tie(*self.held)
        self.flying = (self.ring.go_up(up), self.ring.go_down(down))

    def relay(self, clock, hold=False):
        if self.left == 0:
            return
        above, below = self.ring.half - 1 + self.left, self.left
        self.left -= 1
        up, down = self.flying
        if up.shape[0] < self.full:
            up, down = clock.tie(up, down)
            self.held = ring_add(
                self.terms, (above, below), up, down, self.full, self.cut, self.tile
            )
            if not hold:
                self.go(clock)
            return
        up = self.ring.go_up(clock.tie(plus(self.term(above), clock.tie(up))))
        down = self.ring.go_down(clock.tie(plus(self.term(below), clock.tie(down))))
        self.flying = (up, down)

    def finish(self, clock):
        while self.left:
            self.relay(clock)
        up, down = clock.tie(*self.flying)
        return clock.tie(self.last(0, self.full, up, down))

    def last(self, begin, end, up, down):
        return (self.term(0, begin, end).astype(F32) + up.astype(F32) + down.astype(F32)).astype(BF)

    def fork(self, clock):
        while self.left > 2:
            self.relay(clock)
        up, down = clock.tie(*self.flying)
        self.rows = [(0, self.cut), (self.cut, self.full)]
        self.parts = []
        for begin, end in self.rows:
            self.parts.append(self.pass_on(2, begin, end, up[begin:end], down[begin:end], clock))

    def pass_on(self, left, begin, end, up, down, clock):
        up = plus(self.term(self.ring.half - 1 + left, begin, end), up)
        down = plus(self.term(left, begin, end), down)
        up, down = clock.tie(up, down)
        return self.ring.go_up(up), self.ring.go_down(down)

    def relay_part(self, part, clock):
        up, down = clock.tie(*self.parts[part])
        self.parts[part] = self.pass_on(1, *self.rows[part], up, down, clock)

    def finish_part(self, part, clock):
        up, down = clock.tie(*self.parts[part])
        return clock.tie(self.last(*self.rows[part], up, down))


def plus(one, two):
    return (one.astype(F32) + two.astype(F32)).astype(BF)


def swap(block, distance):
    return lax.ppermute(block, "seq", [(i, i ^ distance) for i in range(4)])


def fill_weights(pieces, scratch, top, width, columns):
    begin = 0
    for index, piece in enumerate(pieces):
        skip = top if index < len(pieces) - 1 else 0
        count = piece.shape[0] - skip
        scratch[begin : begin + count, :] = piece[skip:, columns]
        begin += count


def put_features(values, order_ref, target, slots, width):
    for j in range(slots):
        to = pl.ds(pl.multiple_of(order_ref[j] * width, 128), width)
        target[:, to] = values[:, j * width : (j + 1) * width]


def blocks_in_order(array, order, size):
    width = array.shape[1] // size
    return jnp.concatenate(
        [lax.dynamic_slice_in_dim(array, order[i] * width, width, 1) for i in range(size)],
        axis=1,
    )


def permute_features(array, order, size):
    width = array.shape[1] // size
    if width % 128:
        return blocks_in_order(array, order, size)

    def body(order_ref, source, target):
        for j in range(size):
            begin = pl.ds(pl.multiple_of(order_ref[j] * width, 128), width)
            target[:, j * width : (j + 1) * width] = source[:, begin]

    return kernel_call(
        body, [(array.shape, array.dtype)], smem=1, args=[order, array], name="permute_features"
    )[0]


def pack_heads(here, w_query, w_key, w_value, w_out, gain_attn, gain_mlp, seq):
    width = w_query.shape[0]
    q_cols, k_cols = w_query.shape[1] // seq, w_key.shape[1] // seq
    total = 2 * q_cols + 2 * k_cols

    def body(here_ref, query_ref, key_ref, value_ref, out_ref, one_ref, two_ref, block_ref):
        s = here_ref[0]
        block_ref[:TOP, :] = jnp.zeros((TOP, total), BF)
        block_ref[:1, :width] = one_ref[...].reshape(1, width)
        block_ref[:1, width : 2 * width] = two_ref[...].reshape(1, width)
        block_ref[TOP:, :q_cols] = query_ref[...]

        def mine(ref):
            part = jnp.zeros((width, k_cols), F32)
            for place in range(seq):
                piece = ref[:, place * k_cols : (place + 1) * k_cols].astype(F32)
                part = jnp.where(s == place, piece, part)
            return part

        both = jnp.concatenate([mine(key_ref), mine(value_ref)], axis=1)
        block_ref[TOP:, q_cols : q_cols + 2 * k_cols] = both.astype(BF)
        block_ref[TOP:, q_cols + 2 * k_cols :] = out_ref[...].astype(F32).T.astype(BF)

    whole = lambda shape: pl.BlockSpec(shape, lambda i, o: (0, 0))
    return pl.pallas_call(
        body,
        out_shape=jax.ShapeDtypeStruct((TOP + width, total), BF),
        grid_spec=pltpu.PrefetchScalarGridSpec(
            num_scalar_prefetch=1,
            grid=(1,),
            in_specs=[
                pl.BlockSpec((width, q_cols), lambda i, o: (0, o[0])),
                whole(w_key.shape),
                whole(w_value.shape),
                pl.BlockSpec((q_cols, width), lambda i, o: (o[0], 0)),
                pl.BlockSpec((width,), lambda i, o: (0,)),
                pl.BlockSpec((width,), lambda i, o: (0,)),
            ],
            out_specs=whole((TOP + width, total)),
        ),
        compiler_params=limits("pack_heads"),
        name="pack_heads",
    )(here, w_query, w_key, w_value, w_out, gain_attn, gain_mlp)


def pack_mlp(here, w_gate, w_up, w_down, bounds, seq):
    width, ff = w_gate.shape[0], w_gate.shape[1] // seq

    def body(here_ref, gate_ref, up_ref, down_ref, *blocks):
        for (a, b), block in zip(bounds, blocks):
            size = b - a
            block[:, :size] = gate_ref[:, a:b]
            block[:, size : 2 * size] = up_ref[:, a:b]
            block[:, 2 * size :] = down_ref[a:b, :].astype(F32).T.astype(BF)

    columns = pl.BlockSpec((width, ff), lambda i, o: (0, o[0]))
    return pl.pallas_call(
        body,
        out_shape=tuple(jax.ShapeDtypeStruct((width, 3 * (b - a)), BF) for a, b in bounds),
        grid_spec=pltpu.PrefetchScalarGridSpec(
            num_scalar_prefetch=1,
            grid=(1,),
            in_specs=[columns, columns, pl.BlockSpec((ff, width), lambda i, o: (o[0], 0))],
            out_specs=tuple(
                pl.BlockSpec((width, 3 * (b - a)), lambda i, o: (0, 0)) for a, b in bounds
            ),
        ),
        compiler_params=limits("pack_mlp"),
        name="pack_mlp",
    )(here, w_gate, w_up, w_down)


def turn(values, cosine, sine_part):
    half_dim = HD // 2
    pieces = []
    for h in range(values.shape[0] // HD):
        first = values[h * HD : h * HD + half_dim]
        second = values[h * HD + half_dim : (h + 1) * HD]
        pieces.append(first * cosine - second * sine_part)
        pieces.append(second * cosine + first * sine_part)
    return jnp.concatenate(pieces, axis=0)


def rounded(values):
    return values.astype(BF).astype(F32)


def pick(refs, place, target):
    rows = target.shape[0]
    at = 0
    for ref in refs:
        index, begin, count = at // rows, at % rows, ref.shape[0]
        at += count

        @pl.when(place == index)
        def _():
            target[begin : begin + count, :] = ref[...]


def write_bias(bias_ref, lengths_ref, live, block, rows):
    keys = (block + 1) * rows
    query = lax.broadcasted_iota(jnp.int32, (1, rows), 1) + block * rows
    low = jnp.zeros((1, rows), jnp.int32)
    start = 0
    for slot in range(lengths_ref.shape[0]):
        low = jnp.where(query >= start, jnp.maximum(low, start), low)
        start = start + lengths_ref[slot]
    high = jnp.minimum(query, live - 1)
    key = lax.broadcasted_iota(jnp.int32, (keys, rows), 0)
    allowed = ((key >= low) & (key <= high)) | (key == query)
    bias_ref[:keys, :] = jnp.where(allowed, 0.0, NEG)


def attention_forward(places, lengths, live, tokens, pieces, cosine, sine_part, q_cols):
    rows, model = tokens[0].shape
    pack_size = 4 * rows
    n_heads = q_cols // HD
    heads_cols = q_cols + 2 * HD
    width = pieces[0].shape[0] - TOP

    def body(places_ref, lengths_ref, live_ref, cos_ref, sin_ref, *refs):
        token_refs, piece_refs, refs = refs[:4], refs[4 : 4 + len(pieces)], refs[4 + len(pieces) :]
        (
            normed_ref, query_ref, kv_ref, kvt_ref, lse_ref, mixed_t_ref, mixed_ref, keep_ref,
            send_ref, gains_ref, w_ref, bias_ref, query_s, mixed_s, tokens_s,
        ) = refs
        live_count = live_ref[0]
        fill_weights(piece_refs, w_ref, TOP, width, slice(None))
        gains_ref[...] = jnp.zeros_like(gains_ref)
        for index, piece in enumerate(piece_refs[:-1]):
            at = slice(index * width, (index + 1) * width)
            gains_ref[0:1, at] = piece[0:1, :width].astype(F32)
            gains_ref[1:2, at] = piece[0:1, width : 2 * width].astype(F32)
        ones = jnp.ones((HD, rows), BF)
        for block in range(4):
            place = places_ref[block]
            at = slice(block * rows, (block + 1) * rows)
            keys = (block + 1) * rows
            to = pl.ds(pl.multiple_of(place * rows, rows), rows)
            pick(token_refs, place, tokens_s)
            inputs = tokens_s[...].astype(F32)
            inverse = lax.rsqrt(jnp.mean(inputs * inputs, axis=1, keepdims=True) + EPS)
            normed = (inputs * inverse * gains_ref[0:1, :]).astype(BF)
            normed_ref[to, :] = normed
            pre = dot(normed, w_ref[:, :heads_cols]).T
            cos_b, sin_b = cos_ref[:, at], sin_ref[:, at]
            query = (rounded(turn(pre[:q_cols], cos_b, sin_b)) * HD**-0.5).astype(BF)
            query_s[...] = query
            query_ref[:, at] = query
            key_t = rounded(turn(pre[q_cols : q_cols + HD], cos_b, sin_b))
            value_t = rounded(pre[q_cols + HD :])
            kv_t = jnp.concatenate([key_t, value_t], axis=0)
            kv_ref[at, :] = kv_t.T.astype(BF)
            kvt_ref[: 2 * HD, at] = kv_t.astype(BF)
            kvt_ref[2 * HD :, at] = ones
            write_bias(bias_ref, lengths_ref, live_count, block, rows)

            def attend(h, _):
                mine = pl.ds(pl.multiple_of(h * HD, HD), HD)
                scores = dot(kv_ref[:keys, :HD], query_s[mine, :]) + bias_ref[:keys, :]
                peak = jnp.max(scores, axis=0, keepdims=True)
                weights = jnp.exp(scores - peak).astype(BF)
                summed = dot(kvt_ref[HD:, :keys], weights)
                total = summed[HD : HD + 1]
                mixed = summed[:HD] * (1.0 / total)
                mixed_s[mine, :] = mixed
                lse_ref[pl.ds(h, 1), at] = peak + jnp.log(total)
                return 0

            lax.fori_loop(0, n_heads, attend, 0, unroll=2)
            mixed_t = mixed_s[...]
            mixed_t_ref[:, at] = mixed_t
            mixed = mixed_t.T.astype(BF)
            mixed_ref[to, :] = mixed
            branch = against(mixed, w_ref[:, heads_cols:]).astype(BF)
            half_to = pl.ds(pl.multiple_of((place % 2) * rows, rows), rows)

            @pl.when(place < 2)
            def _():
                keep_ref[half_to, :] = branch

            @pl.when(place >= 2)
            def _():
                send_ref[half_to, :] = branch

    args = [places, lengths, live, cosine, sine_part, *tokens, *pieces]
    flops = 2 * pack_size * model * (heads_cols + q_cols) + 4 * n_heads * pack_size**2 * HD * 3
    return kernel_call(
        body,
        [
            ((pack_size, model), BF),
            ((q_cols, pack_size), BF),
            ((pack_size, 2 * HD), BF),
            ((3 * HD, pack_size), BF),
            ((n_heads, pack_size), F32),
            ((q_cols, pack_size), F32),
            ((pack_size, q_cols), BF),
            ((pack_size // 2, model), BF),
            ((pack_size // 2, model), BF),
            ((8, model), F32),
        ],
        scratch=[
            pltpu.VMEM((model, heads_cols + q_cols), BF),
            pltpu.VMEM((pack_size, rows), F32),
            pltpu.VMEM((q_cols, rows), BF),
            pltpu.VMEM((q_cols, rows), F32),
            pltpu.VMEM((rows, model), BF),
        ],
        flops=flops,
        moved=30 << 20,
        smem=3,
        args=args,
        name="attention_forward",
    )


def attention_backward(
    places, lengths, live, tokens, pieces, cosine, sine_part, query, kv, kvt, lse, mixed_t
):
    q_cols, pack_size = query.shape
    rows, model = tokens[0].shape
    n_heads = q_cols // HD
    heads_cols = q_cols + 2 * HD
    width = pieces[0].shape[0] - TOP

    def body(
        places_ref, lengths_ref, live_ref, cos_ref, sin_ref,
        query_ref, kv_ref, kvt_ref, lse_ref, mixed_t_ref, *refs
    ):
        token_refs, piece_refs, refs = refs[:4], refs[4 : 4 + len(pieces)], refs[4 + len(pieces) :]
        (
            grad_q_ref, grad_kv_ref, w_ref, bias_ref, grad_s, grad_q_s, key_acc, value_acc, inner_s,
            tokens_s,
        ) = refs
        live_count = live_ref[0]
        fill_weights(piece_refs, w_ref, TOP, width, slice(heads_cols, heads_cols + q_cols))
        key_acc[...] = jnp.zeros_like(key_acc)
        value_acc[...] = jnp.zeros_like(value_acc)
        for block in range(4):
            place = places_ref[block]
            at = slice(block * rows, (block + 1) * rows)
            keys = (block + 1) * rows
            to = pl.ds(pl.multiple_of(place * rows, rows), rows)
            pick(token_refs, place, tokens_s)
            grad_t = rounded(dot(tokens_s[...], w_ref[...]).T)
            grad_s[...] = grad_t.astype(BF)
            product = grad_t * mixed_t_ref[:, at]
            for h in range(n_heads):
                inner_s[h : h + 1, :] = jnp.sum(
                    product[h * HD : (h + 1) * HD], axis=0, keepdims=True
                )
            write_bias(bias_ref, lengths_ref, live_count, block, rows)

            def attend(h, _):
                mine = pl.ds(pl.multiple_of(h * HD, HD), HD)
                query_h = query_ref[mine, at]
                grad_h = grad_s[mine, :]
                scores = dot(kv_ref[:keys, :HD], query_h) + bias_ref[:keys, :]
                probs = jnp.exp(scores - lse_ref[pl.ds(h, 1), at])
                grad_probs = dot(kv_ref[:keys, HD:], grad_h)
                grad_scores = (probs * (grad_probs - inner_s[pl.ds(h, 1), :])).astype(BF)
                grad_q_s[mine, :] = dot(kvt_ref[:HD, :keys], grad_scores) * HD**-0.5
                key_acc[:keys, :] += against(grad_scores, query_h)
                value_acc[:keys, :] += against(probs.astype(BF), grad_h)
                return 0

            lax.fori_loop(0, n_heads, attend, 0, unroll=8)
            turned = turn(rounded(grad_q_s[...]), cos_ref[:, at], -sin_ref[:, at])
            grad_q_ref[to, :] = turned.T.astype(BF)
        for block in range(4):
            at = slice(block * rows, (block + 1) * rows)
            to = pl.ds(pl.multiple_of(places_ref[block] * rows, rows), rows)
            key_t = turn(rounded(key_acc[at, :]).T, cos_ref[:, at], -sin_ref[:, at])
            grad_kv_ref[to, :] = jnp.concatenate([key_t.T, value_acc[at, :]], axis=1).astype(BF)

    args = [
        places, lengths, live, cosine, sine_part, query, kv, kvt, lse, mixed_t, *tokens, *pieces
    ]
    return kernel_call(
        body,
        [((pack_size, q_cols), BF), ((pack_size, 2 * HD), BF)],
        scratch=[
            pltpu.VMEM((model, q_cols), BF),
            pltpu.VMEM((pack_size, rows), F32),
            pltpu.VMEM((q_cols, rows), BF),
            pltpu.VMEM((q_cols, rows), F32),
            pltpu.VMEM((pack_size, HD), F32),
            pltpu.VMEM((pack_size, HD), F32),
            pltpu.VMEM((n_heads, rows), F32),
            pltpu.VMEM((rows, model), BF),
        ],
        flops=2 * pack_size * model * q_cols + 10 * n_heads * pack_size**2 * HD * 3,
        moved=20 << 20,
        smem=3,
        args=args,
        name="attention_backward",
    )


def heads_back(grad_q, grad_kv, tokens, pieces):
    pack_size, q_cols = grad_q.shape
    rows, model = tokens[0].shape
    heads_cols = q_cols + 2 * HD
    width = pieces[0].shape[0] - TOP

    def body(grad_q_ref, grad_kv_ref, *refs):
        token_refs, piece_refs = refs[:4], refs[4 : 4 + len(pieces)]
        keep_ref, send_ref, gain_ref, w_ref, tokens_s = refs[4 + len(pieces) :]
        step = pl.program_id(0)

        @pl.when(step == 0)
        def _():
            fill_weights(piece_refs, w_ref, TOP, width, slice(0, heads_cols))
            gain_ref[...] = jnp.zeros_like(gain_ref)

        pick(token_refs, step, tokens_s)
        inputs = tokens_s[...].astype(F32)
        inverse = lax.rsqrt(jnp.mean(inputs * inputs, axis=1, keepdims=True) + EPS)
        grad = against(grad_q_ref[...], w_ref[:, :q_cols]) + against(
            grad_kv_ref[...], w_ref[:, q_cols:]
        )

        @pl.when(step < 2)
        def _():
            keep_ref[...] = grad.astype(BF)

        @pl.when(step >= 2)
        def _():
            send_ref[...] = grad.astype(BF)

        total = jnp.sum(grad * inputs * inverse, axis=0, keepdims=True)
        gain_ref[...] += jnp.broadcast_to(total, gain_ref.shape)

    first = pl.BlockSpec((rows, model), lambda i: (jnp.minimum(i, 1), 0))
    second = pl.BlockSpec((rows, model), lambda i: (jnp.maximum(i - 2, 0), 0))
    fixed = lambda a: pl.BlockSpec(memory_space=pltpu.VMEM)
    half = jax.ShapeDtypeStruct((pack_size // 2, model), BF)
    return pl.pallas_call(
        body,
        grid=(4,),
        out_shape=(half, half, jax.ShapeDtypeStruct((8, model), F32)),
        in_specs=[
            pl.BlockSpec((rows, q_cols), lambda i: (i, 0)),
            pl.BlockSpec((rows, 2 * HD), lambda i: (i, 0)),
        ]
        + [fixed(a) for a in (*tokens, *pieces)],
        out_specs=(first, second, pl.BlockSpec((8, model), lambda i: (0, 0))),
        scratch_shapes=[pltpu.VMEM((model, heads_cols), BF), pltpu.VMEM((rows, model), BF)],
        compiler_params=limits("heads_back"),
        cost_estimate=COST,
        name="heads_back",
    )(grad_q, grad_kv, *tokens, *pieces)


def mlp_chunk(tokens, cots, pieces, before, size, room):
    rows, model = tokens[0].shape
    pack_size = 4 * rows

    def body(*refs):
        token_refs, cot_refs, refs = refs[:4], refs[4:8], refs[8:]
        piece_refs, refs = refs[: len(pieces)], refs[len(pieces) :]
        before_refs, refs = refs[: len(before)], refs[len(before) :]
        down_keep, down_send, grad_keep, grad_send, both_ref, w_ref, tokens_s, cot_s = refs
        step = pl.program_id(0)

        @pl.when(step == 0)
        def _():
            fill_weights(piece_refs, w_ref, 0, model, slice(None))

        pick(token_refs, step, tokens_s)
        pick(cot_refs, step, cot_s)
        both = dot(tokens_s[...], w_ref[:, : 2 * size])
        grad_act = dot(cot_s[...], w_ref[:, 2 * size :])
        gate_pre, up_pre = both[:, :size], both[:, size:]
        sig = 1.0 / (1.0 + jnp.exp(-gate_pre))
        active = gate_pre * sig
        both_ref[:, 2 * size :] = (active * up_pre).astype(BF)
        both_ref[:, size : 2 * size] = (grad_act * active).astype(BF)
        both_ref[:, :size] = (grad_act * up_pre * (sig + active * (1.0 - sig))).astype(BF)
        down = against(both_ref[:, 2 * size :], w_ref[:, 2 * size :])
        grad = against(both_ref[:, : 2 * size], w_ref[:, : 2 * size])

        def put(keep, send, value, keep_before, send_before):
            @pl.when(step < 2)
            def _():
                extra = 0.0 if keep_before is None else keep_before[...].astype(F32)
                keep[...] = (value + extra).astype(BF)

            @pl.when(step >= 2)
            def _():
                extra = 0.0 if send_before is None else send_before[...].astype(F32)
                send[...] = (value + extra).astype(BF)

        old = before_refs or [None] * 4
        put(down_keep, down_send, down, old[0], old[1])
        put(grad_keep, grad_send, grad, old[2], old[3])

    first = pl.BlockSpec((rows, model), lambda i: (jnp.minimum(i, 1), 0))
    second = pl.BlockSpec((rows, model), lambda i: (jnp.maximum(i - 2, 0), 0))
    fixed = pl.BlockSpec(memory_space=pltpu.VMEM)
    half = pltpu.HBM((pack_size // 2, model), BF)
    return pl.pallas_call(
        body,
        grid=(4,),
        out_shape=(half, half, half, half, pltpu.HBM((pack_size, 3 * size), BF)),
        in_specs=[fixed] * (8 + len(pieces)) + [first, second] * (len(before) // 2),
        out_specs=(first, second, first, second, pl.BlockSpec((rows, 3 * size), lambda i: (i, 0))),
        scratch_shapes=[
            pltpu.VMEM((model, 3 * size), BF),
            pltpu.VMEM((rows, model), BF),
            pltpu.VMEM((rows, model), BF),
        ],
        compiler_params=limits(room),
        cost_estimate=COST,
        name="mlp_chunk",
    )(*tokens, *cots, *pieces, *before)


def weight_terms(pairs, width, n_slots, group, cut, tops=None):
    tokens = sum(x.shape[0] for x in pairs[0][0])
    total = sum(cols.stop - cols.start for _, _, cols in pairs)
    head = 0 if tops is None else TOP

    def distinct(lists):
        out = []
        for one in lists:
            if not any(one is other for other in out):
                out.append(one)
        return out

    x_lists = distinct(x for x, _, _ in pairs)
    g_lists = distinct(g for _, g, _ in pairs)
    while (width * group) % 128:
        group *= 2
    wide = width * group
    args, specs = [], []
    for x in [x for xs in x_lists for x in xs]:
        args.append(x)
        specs.append(pl.BlockSpec((x.shape[0], wide), lambda i: (0, i)))
    for g in [g for gs in g_lists for g in gs]:
        args.append(g)
        specs.append(pl.BlockSpec(memory_space=pltpu.VMEM))
    if head:
        args.append(tops)
        specs.append(pl.BlockSpec((group * TOP, total), lambda i: (i, 0)))

    def body(*refs):
        def take(lists):
            nonlocal refs
            out = []
            for one in lists:
                out.append((one, refs[: len(one)]))
                refs = refs[len(one) :]
            return out

        x_refs, g_refs = take(x_lists), take(g_lists)
        out_ref, up_ref, down_ref, x_s = refs[-4:]
        lane = 0
        filled = None
        for xs, gs, cols in pairs:
            parts = next(r for other, r in x_refs if other is xs)
            g_parts = next(r for other, r in g_refs if other is gs)
            if len(parts) > 1 and filled is not xs:
                at = 0
                for part in parts:
                    x_s[at : at + part.shape[0], :] = part[...]
                    at += part.shape[0]
                filled = xs
            product, at = None, 0
            for g in g_parts:
                rows = g.shape[0]
                x = (x_s if len(parts) > 1 else parts[0])[at : at + rows, :]
                at += rows
                more = cross(x, g[:, cols])
                product = more if product is None else product + more
            product = product.astype(BF)
            count = cols.stop - cols.start
            for j in range(group):
                at = j * (head + width) + head
                out_ref[at : at + width, lane : lane + count] = product[
                    j * width : (j + 1) * width
                ]
            lane += count
        if head:
            for j in range(group):
                at = j * (head + width)
                out_ref[at : at + head, :] = refs[0][j * TOP : (j + 1) * TOP, :]

        @pl.when(pl.program_id(0) == n_slots // group - 1)
        def _():
            begin = (group - 1) * (head + width)
            up_ref[...] = out_ref[begin : begin + cut, :]
            down_ref[...] = out_ref[begin + cut : begin + head + width, :]

    far = [(cut, total), (head + width - cut, total)]
    return pl.pallas_call(
        body,
        grid=(n_slots // group,),
        out_shape=(
            jax.ShapeDtypeStruct((n_slots * (head + width), total), BF),
            *[jax.ShapeDtypeStruct(shape, BF) for shape in far],
        ),
        in_specs=specs,
        out_specs=(
            pl.BlockSpec((group * (head + width), total), lambda i: (i, 0)),
            *[pl.BlockSpec(shape, lambda i: (0, 0)) for shape in far],
        ),
        scratch_shapes=[pltpu.VMEM((tokens, wide), BF)],
        compiler_params=limits("weight_terms"),
        cost_estimate=COST,
        name="weight_terms",
    )(*args)


def ring_add(terms, slots, up, down, full, cut, tile):
    total = terms.shape[1]

    def body(up_term, down_term, up_ref, down_ref, up_out, down_out):
        if up_ref.shape[0] == full:
            up_out[...] = (up_term[...].astype(F32) + up_ref[...].astype(F32)).astype(BF)
            down_out[...] = (down_term[...].astype(F32) + down_ref[...].astype(F32)).astype(BF)
        else:
            up_out[:cut, :] = (up_term[:cut, :].astype(F32) + up_ref[...].astype(F32)).astype(BF)
            up_out[cut:, :] = up_term[cut:, :]
            down_out[:cut, :] = down_term[:cut, :]
            down_out[cut:, :] = (
                down_term[cut:, :].astype(F32) + down_ref[...].astype(F32)
            ).astype(BF)

    columns = lambda array: pl.BlockSpec((array.shape[0], tile), lambda i: (0, i))
    out = jax.ShapeDtypeStruct((full, total), BF)
    return pl.pallas_call(
        body,
        grid=(total // tile,),
        out_shape=(out, out),
        in_specs=[
            pl.BlockSpec((full, tile), lambda i: (slots[0], i)),
            pl.BlockSpec((full, tile), lambda i: (slots[1], i)),
            columns(up),
            columns(down),
        ],
        out_specs=(columns(out), columns(out)),
        compiler_params=limits("ring_add"),
        cost_estimate=COST,
        name="ring_add",
    )(terms, terms, up, down)


def row_call(body, outs, row_args, fixed_args, steps, smem=(), name=None):
    rows = outs[0][0][0] if outs[0][2] else row_args[0][0].shape[0]
    tile = rows // steps
    n_smem = len(smem)
    by_rows = lambda cols, at: pl.BlockSpec((tile, cols), lambda i, *_: (i + at, 0))
    return pl.pallas_call(
        body,
        out_shape=tuple(jax.ShapeDtypeStruct(s, d) for s, d, _ in outs),
        grid_spec=pltpu.PrefetchScalarGridSpec(
            num_scalar_prefetch=n_smem,
            grid=(steps,),
            in_specs=[by_rows(a.shape[1], at * steps) for a, at in row_args]
            + [pl.BlockSpec(a.shape, lambda i, *_: (0, 0)) for a in fixed_args],
            out_specs=tuple(
                by_rows(s[1], 0) if split else pl.BlockSpec(s, lambda i, *_: (0, 0))
                for s, _, split in outs
            ),
        ),
        compiler_params=limits(name),
        cost_estimate=COST,
        name=name,
    )(*smem, *[a for a, _ in row_args], *fixed_args)


STEPS = 2


def second_norm(inputs, keep, came, last, gains):
    def body(inputs_ref, keep_ref, came_ref, last_ref, gains_ref, hidden_ref, normed_ref):
        branch = keep_ref[...].astype(F32) + came_ref[...].astype(F32) + last_ref[...].astype(F32)
        hidden = inputs_ref[...].astype(F32) + branch
        inverse = lax.rsqrt(jnp.mean(hidden * hidden, axis=1, keepdims=True) + EPS)
        hidden_ref[...] = hidden
        normed_ref[...] = (hidden * inverse * gains_ref[1:2, :]).astype(BF)

    return row_call(
        body,
        [(inputs.shape, F32, True), (inputs.shape, BF, True)],
        [(inputs, 0), (keep, 0), (came, 0), (last, 0)],
        [gains],
        STEPS,
        name="second_norm",
    )


def norm_back(grad, values, gain):
    inverse = lax.rsqrt(jnp.mean(values * values, axis=1, keepdims=True) + EPS)
    scaled = grad * gain
    mean = jnp.mean(scaled * values, axis=1, keepdims=True)
    return inverse, inverse * (scaled - values * (inverse * inverse * mean))


def second_norm_back(cot, hidden, keep, came, last, gains):
    rows, model = hidden.shape

    def body(cot_ref, hidden_ref, keep_ref, came_ref, last_ref, gains_ref, grad_ref, low_ref, gain_ref):
        @pl.when(pl.program_id(0) == 0)
        def _():
            gain_ref[...] = jnp.zeros_like(gain_ref)

        grad = keep_ref[...].astype(F32) + came_ref[...].astype(F32) + last_ref[...].astype(F32)
        hidden_v = hidden_ref[...]
        inverse, back = norm_back(grad, hidden_v, gains_ref[1:2, :])
        total = jnp.sum(grad * hidden_v * inverse, axis=0, keepdims=True)
        gain_ref[...] += jnp.broadcast_to(total, gain_ref.shape)
        out = cot_ref[...].astype(F32) + back
        grad_ref[...] = out
        low_ref[...] = out.astype(BF)

    return row_call(
        body,
        [((rows, model), F32, True), ((rows, model), BF, True), ((8, model), F32, False)],
        [(cot, 0), (hidden, 0), (keep, 0), (came, 0), (last, 0)],
        [gains],
        STEPS,
        name="second_norm_back",
    )


def first_norm_back(grad_hidden, inputs, keep, came, last, gains, order, n_slots):
    width = inputs.shape[1] // n_slots

    def body(order_ref, grad_ref, inputs_ref, keep_ref, came_ref, last_ref, gains_ref, out_ref):
        grad = keep_ref[...].astype(F32) + came_ref[...].astype(F32) + last_ref[...].astype(F32)
        _, back = norm_back(grad, inputs_ref[...].astype(F32), gains_ref[0:1, :])
        out = (grad_ref[...] + back).astype(BF)
        if width % 128:
            out_ref[...] = out
        else:
            put_features(out, order_ref, out_ref, n_slots, width)

    return row_call(
        body,
        [(inputs.shape, BF, True)],
        [(grad_hidden, 0), (inputs, 0), (keep, 0), (came, 0), (last, 0)],
        [gains],
        STEPS,
        smem=(order,),
        name="first_norm_back",
    )[0]


def layer_output(hidden, keep, came, last, order, n_slots):
    width = hidden.shape[1] // n_slots

    def body(order_ref, hidden_ref, keep_ref, came_ref, last_ref, out_ref):
        down = keep_ref[...].astype(F32) + came_ref[...].astype(F32) + last_ref[...].astype(F32)
        out = (hidden_ref[...] + down).astype(BF)
        if width % 128:
            out_ref[...] = out
        else:
            put_features(out, order_ref, out_ref, n_slots, width)

    return row_call(
        body,
        [(hidden.shape, BF, True)],
        [(hidden, 0), (keep, 0), (came, 0), (last, 0)],
        [],
        STEPS,
        smem=(order,),
        name="layer_output",
    )[0]


def unpack_mlp(places, chunks, bounds, width, ff):
    flat = [block for blocks in chunks for block in blocks]

    def body(places_ref, *refs):
        ins = refs[: len(flat)]
        gate_ref, up_ref, down_ref = refs[len(flat) : len(flat) + 3]
        scratches = refs[len(flat) + 3 :]
        place = places_ref[pl.program_id(0)]
        for c, (a, b) in enumerate(bounds):
            size = b - a
            block_s = scratches[c]
            pick(ins[4 * c : 4 * c + 4], place, block_s)
            gate_ref[:, a:b] = block_s[:, :size].astype(F32)
            up_ref[:, a:b] = block_s[:, size : 2 * size].astype(F32)
            down_ref[a:b, :] = block_s[:, 2 * size :].astype(F32).T

    columns = pl.BlockSpec((width, ff), lambda i, p: (0, i))
    return pl.pallas_call(
        body,
        out_shape=(
            jax.ShapeDtypeStruct((width, 4 * ff), F32),
            jax.ShapeDtypeStruct((width, 4 * ff), F32),
            jax.ShapeDtypeStruct((4 * ff, width), F32),
        ),
        grid_spec=pltpu.PrefetchScalarGridSpec(
            num_scalar_prefetch=1,
            grid=(4,),
            in_specs=[
                pl.BlockSpec(h.shape, lambda i, p: (0, 0), pipeline_mode=pl.Buffered(1))
                for h in flat
            ],
            out_specs=(columns, columns, pl.BlockSpec((ff, width), lambda i, p: (i, 0))),
            scratch_shapes=[pltpu.VMEM((width, 3 * (b - a)), BF) for a, b in bounds],
        ),
        compiler_params=limits("unpack_mlp"),
        cost_estimate=COST,
        name="unpack_mlp",
    )(places, *flat)


def unpack_heads(places, heads, width, q_cols):
    kv = q_cols + 2 * HD

    def body(places_ref, *refs):
        head_refs = refs[: len(heads)]
        query_ref, key_ref, value_ref, out_ref, gain_ref, head_s = refs[len(heads) :]
        gain = jnp.zeros((8, 2 * width), F32)
        for place in range(4):
            pick(head_refs, places_ref[place], head_s)
            gain = gain + head_s[:TOP, : 2 * width].astype(F32)[:8]
            at = slice(place * q_cols, (place + 1) * q_cols)
            query_ref[:, at] = head_s[TOP:, :q_cols].astype(F32)
            both = head_s[TOP:, q_cols:kv].astype(F32)
            key_ref[:, place * HD : (place + 1) * HD] = both[:, :HD]
            value_ref[:, place * HD : (place + 1) * HD] = both[:, HD:]
            out_ref[at, :] = head_s[TOP:, kv:].astype(F32).T
        gain_ref[...] = gain

    args = [places, *heads]
    return kernel_call(
        body,
        [
            ((width, 4 * q_cols), F32),
            ((width, 4 * HD), F32),
            ((width, 4 * HD), F32),
            ((4 * q_cols, width), F32),
            ((8, 2 * width), F32),
        ],
        scratch=[pltpu.VMEM((TOP + width, heads[0].shape[1]), BF)],
        smem=1,
        args=args,
        name="unpack_heads",
    )


def doc_positions(lengths, pack_size):
    doc_starts = jnp.cumsum(lengths) - lengths
    places = jnp.arange(pack_size, dtype=jnp.int32)
    doc_first = jnp.max(
        jnp.where(places[:, None] >= doc_starts[None, :], doc_starts[None, :], 0), axis=1
    )
    return places - doc_first


def rotary_tables(positions):
    half_dim = HD // 2
    frequency = 10000.0 ** (-2.0 * jnp.arange(half_dim, dtype=F32) / HD)
    angle_table = frequency[:, None] * positions.astype(F32)[None, :]
    return (jnp.cos(angle_table), jnp.sin(angle_table))


def layer(
    hidden_in,
    cotangent,
    gain_attn,
    w_query,
    w_key,
    w_value,
    w_out,
    gain_mlp,
    w_gate,
    w_up,
    w_down,
    doc_lengths,
    valid_count,
):
    seq = lax.axis_size("seq")
    n_dp = lax.axis_size("dp")
    here = lax.axis_index("seq").astype(jnp.int32)
    ring = Ring(n_dp)
    rows, model = hidden_in.shape
    pack_size = rows * seq
    width = gain_attn.shape[0]
    q_cols = w_query.shape[1] // seq
    ff = w_gate.shape[1] // seq
    here_1 = here.reshape(1)
    lengths, live = doc_lengths[0], valid_count[:1]
    middle = width // 2

    offset = here ^ jnp.arange(4, dtype=jnp.int32)
    places = (offset % 2) * 2 + offset // 2

    first = (ff // 2 + 127) // 128 * 128
    bounds = [(0, first), (first, ff)]
    sizes = [b - a for a, b in bounds]

    def other_half(keep, came):
        return plus(keep[rows:], came[rows:])

    def far_memory(*arrays):
        return [pltpu.with_memory_space_constraint(a, pltpu.HBM) for a in arrays]

    def four(block, across, beside):
        return [block, across, beside, swap(across, 1)]

    clock = Clock()
    head_block = pack_heads(here_1, w_query, w_key, w_value, w_out, gain_attn, gain_mlp, seq)
    clock.done(head_block)
    heads = Gather(ring, head_block, TOP + middle)
    hidden_in, cotangent = clock.tie(hidden_in, cotangent)
    mine = permute_features(hidden_in, ring.slot_owners(), n_dp)
    clock.done(mine)
    across, beside = swap(mine, 2), swap(mine, 1)
    w_gate, w_up, w_down, cotangent = clock.tie(w_gate, w_up, w_down, cotangent)
    blocks = pack_mlp(here_1, w_gate, w_up, w_down, bounds, seq)
    clock.done(blocks[0])
    heads.relay(clock)
    cotangent = clock.tie(cotangent)
    my_cot = permute_features(cotangent, ring.slot_owners(), n_dp)
    cosine, sine_part = rotary_tables(doc_positions(lengths, pack_size))
    cosine, sine_part, my_cot = clock.tie(cosine, sine_part, my_cot)
    heads.relay(clock)
    across, my_cot = clock.tie(across, my_cot)
    tokens = four(mine, across, beside)
    cot_across, cot_beside = swap(my_cot, 2), swap(my_cot, 1)
    heads.relay(clock)
    head_pieces = heads.finish(clock)
    tokens = list(clock.tie(*tokens))
    blocks = clock.tie(*blocks)
    chunks = [Gather(ring, block, middle) for block in blocks]
    normed, query, kv, kvt, lse, mixed_t, mixed, keep, send, gains = attention_forward(
        places, lengths, live, tokens, head_pieces, cosine, sine_part, q_cols
    )
    normed, query, kv, kvt, mixed_t, mixed = far_memory(normed, query, kv, kvt, mixed_t, mixed)
    clock.done(lse)
    chunks[0].relay(clock)
    chunks[1].land(clock)
    cot_across, send = clock.tie(cot_across, send)
    came = clock.tie(swap(send, 1))
    last = swap(clock.tie(other_half(keep, came)), 2)
    cots = four(my_cot, cot_across, cot_beside)
    chunks[0].relay(clock)
    last = clock.tie(last)
    hidden, my_normed = second_norm(mine, keep, came, last, gains)
    clock.done(my_normed)
    across, beside = swap(my_normed, 2), swap(my_normed, 1)
    beside = clock.tie(beside)
    chunks[0].relay(clock)
    across = clock.tie(across)
    seconds = four(my_normed, across, beside)
    pieces = chunks[0].finish(clock)
    chunks[1].go(clock)
    seconds = list(clock.tie(*seconds))
    cots = list(clock.tie(*cots))

    def terms_of(both, size):
        return weight_terms(
            [(seconds, [both], slice(0, 2 * size)), (cots, [both], slice(2 * size, 3 * size))],
            width,
            n_dp,
            2,
            middle,
        )

    *before, both = mlp_chunk(seconds, cots, pieces, (), sizes[0], "mlp_chunk")
    clock.done(both)
    chunks[1].relay(clock)
    terms = terms_of(clock.tie(both), sizes[0])
    clock.done(terms[0])
    sums = [Scatter(ring, terms, middle, sizes[0])]
    chunks[1].relay(clock)
    sums[0].land(clock)
    pieces = far_memory(*chunks[1].finish(clock))
    sums[0].go(clock)
    down_keep, down_send, grad_keep, grad_send, both = mlp_chunk(
        seconds, cots, clock.tie(*pieces), before, sizes[1], "mlp_chunk_far"
    )
    clock.done(both)
    sums[0].relay(clock)
    grad_send, down_send = clock.tie(grad_send, down_send)
    came, down_came = swap(grad_send, 1), swap(down_send, 1)
    came = clock.tie(came)
    last = swap(clock.tie(other_half(grad_keep, came)), 2)
    terms = terms_of(clock.tie(both), sizes[1])
    clock.done(terms[0])
    sums.append(Scatter(ring, terms, middle, sizes[1]))
    down_came = clock.tie(down_came)
    sums[0].relay(clock)
    sums[1].relay(clock)
    last = clock.tie(last)
    grad_hidden, my_branch, gain_two_terms = second_norm_back(
        my_cot, hidden, grad_keep, came, last, gains
    )
    clock.done(my_branch)
    across, beside = swap(my_branch, 2), swap(my_branch, 1)
    down_other = clock.tie(other_half(down_keep, down_came))
    beside = clock.tie(beside)
    chunk_sum = sums[0].finish(clock)
    chunk_across, chunk_beside = swap(chunk_sum, 2), swap(chunk_sum, 1)
    across = clock.tie(across)
    branches = four(my_branch, across, beside)
    branches = list(clock.tie(*branches))
    grad_q, grad_kv = attention_backward(
        places, lengths, live, branches, head_pieces, cosine, sine_part,
        query, kv, kvt, lse, mixed_t
    )
    clock.done(grad_kv)
    sums[1].relay(clock)
    chunk_across, chunk_beside = clock.tie(chunk_across, chunk_beside)
    firsts = four(chunk_sum, chunk_across, chunk_beside)
    down_last = swap(clock.tie(down_other), 2)
    tokens = clock.tie(*tokens)
    grad_keep, grad_send, gain_one_terms = heads_back(grad_q, grad_kv, tokens, head_pieces)
    clock.done(gain_one_terms)
    columns = head_block.shape[1]
    tops = jnp.concatenate(
        [
            gain_one_terms[0].reshape(n_dp, width),
            gain_two_terms[0].reshape(n_dp, width),
            jnp.zeros((n_dp, columns - 2 * width), F32),
        ],
        axis=1,
    ).astype(BF)
    tops = jnp.pad(tops[:, None], ((0, 0), (0, TOP - 1), (0, 0))).reshape(n_dp * TOP, -1)
    normed, tops = clock.tie(normed, tops)
    normed = [normed]
    head_terms = weight_terms(
        [
            (normed, [grad_q], slice(0, q_cols)),
            (normed, [grad_kv], slice(0, 2 * HD)),
            (branches, [mixed], slice(0, q_cols)),
        ],
        width,
        n_dp,
        2,
        TOP + middle,
        tops,
    )
    clock.done(head_terms[0])
    head_ring = Scatter(ring, head_terms, TOP + middle, columns)
    sums[1].relay(clock)
    firsts = list(clock.tie(*firsts))
    head_ring.relay(clock)
    down_last = clock.tie(down_last)
    came = clock.tie(swap(clock.tie(grad_send), 1))
    last = swap(clock.tie(other_half(grad_keep, came)), 2)
    second_sum = sums[1].finish(clock)
    second_across, second_beside = swap(second_sum, 2), swap(second_sum, 1)
    head_ring.fork(clock)
    down_came = clock.tie(down_came)
    result = layer_output(hidden, down_keep, down_came, down_last, ring.slot_owners(), n_dp)
    clock.done(result)
    last, second_beside = clock.tie(last, second_beside)
    grad_input = first_norm_back(
        grad_hidden, mine, grad_keep, came, last, gains, ring.slot_owners(), n_dp
    )
    clock.done(grad_input)
    head_ring.relay_part(0, clock)
    head_ring.relay_part(1, clock)
    head_sums = [head_ring.finish_part(0, clock)]
    head_across = [swap(head_sums[0], 2)]
    second_across = clock.tie(second_across)
    others = four(second_sum, second_across, second_beside)
    head_sums.append(head_ring.finish_part(1, clock))
    head_across.append(swap(head_sums[1], 2))
    others = list(clock.tie(*others))
    grad_gate, grad_up, grad_down = unpack_mlp(places, [firsts, others], bounds, width, ff)
    clock.done(grad_gate)
    head_beside = [swap(part, 1) for part in head_sums]
    head_across = clock.tie(*head_across)
    head_blocks = [
        *head_sums, *head_across, *head_beside, *[swap(part, 1) for part in head_across]
    ]
    grad_query, grad_key, grad_value, grad_out, gain_sums = unpack_heads(
        places, list(clock.tie(*head_blocks)), width, q_cols
    )
    if width % 128:
        slots = ring.owner_slots()
        result = blocks_in_order(result, slots, n_dp)
        grad_input = blocks_in_order(grad_input, slots, n_dp)

    return (
        result,
        grad_input,
        gain_sums[0, :width],
        grad_query,
        grad_key,
        grad_value,
        grad_out,
        gain_sums[0, width:],
        grad_gate,
        grad_up,
        grad_down,
    )


def solution(mesh):
    return jax.shard_map(
        layer,
        mesh=mesh,
        in_specs=(
            P(("dp", "seq"), None),
            P(("dp", "seq"), None),
            P("dp"),
            P("dp", None),
            P("dp", None),
            P("dp", None),
            P(None, "dp"),
            P("dp"),
            P("dp", None),
            P("dp", None),
            P(None, "dp"),
            P("dp", None),
            P("dp"),
        ),
        out_specs=(
            P(("dp", "seq"), None),
            P(("dp", "seq"), None),
            P("dp"),
            P("dp", None),
            P("dp", None),
            P("dp", None),
            P(None, "dp"),
            P("dp"),
            P("dp", None),
            P("dp", None),
            P(None, "dp"),
        ),
        check_vma=False,
    )
```

```python
import functools

import jax
import jax.numpy as jnp
from jax import lax
from jax.experimental import pallas as pl
from jax.experimental.pallas import tpu as pltpu
from jax.sharding import PartitionSpec as P

HEADS = 32
HD = 64
KVH = 4
EPS = 1e-05
TOP = 8
BF = jnp.bfloat16
F32 = jnp.float32
NEG = -1e30
LIMITS = {
    "attention_forward": 23,
    "attention_backward": 18,
    "heads_back": 15,
    "mlp_chunk": 29,
    "mlp_chunk_far": 44,
    "weight_terms": 15,
    "unpack_mlp": 28,
    "unpack_heads": 12,
    "permute_features": 56,
    "pack_heads": 56,
    "pack_mlp": 56,
}


def limits(name):
    return pltpu.CompilerParams(vmem_limit_bytes=LIMITS.get(name, 12) << 20)


COST = pl.CostEstimate(flops=1000, transcendentals=0, bytes_accessed=1000)


def dot(left_side, right_side):
    return jnp.dot(left_side, right_side, preferred_element_type=F32)


def cross(left_side, right_side):
    return lax.dot_general(
        left_side, right_side, (((0,), (0,)), ((), ())), preferred_element_type=F32
    )


def against(left_side, right_side):
    return lax.dot_general(
        left_side, right_side, (((1,), (1,)), ((), ())), preferred_element_type=F32
    )


def kernel_call(body, outs, scratch=(), flops=0, moved=0, smem=0, args=(), name=None):
    vmem = pl.BlockSpec(memory_space=pltpu.VMEM)
    return pl.pallas_call(
        body,
        out_shape=tuple(jax.ShapeDtypeStruct(s, d) for s, d in outs),
        in_specs=[pl.BlockSpec(memory_space=pltpu.SMEM)] * smem + [vmem] * (len(args) - smem),
        out_specs=tuple(vmem for _ in outs),
        scratch_shapes=list(scratch),
        compiler_params=limits(name),
        cost_estimate=COST,
        name=name,
    )(*args)


class Ring:
    def __init__(self, size):
        self.size = size
        self.half = size // 2
        self.order = list(range(0, size, 2)) + list(range(size - 1, 0, -2))
        place = [0] * size
        for position, device in enumerate(self.order):
            place[device] = position
        self.place = place
        walk = [(self.order[i], self.order[(i + 1) % size]) for i in range(size)]
        self.up = walk
        self.down = [(b, a) for a, b in walk]
        self.steps = (
            [-t for t in range(self.half)] + [t for t in range(1, self.half)] + [self.half]
        )

    def slot_owners(self):
        mine = jnp.asarray(self.place, jnp.int32)[lax.axis_index("dp")]
        wanted = (mine + jnp.asarray(self.steps, jnp.int32)) % self.size
        return jnp.asarray(self.order, jnp.int32)[wanted]

    def owner_slots(self):
        mine = jnp.asarray(self.place, jnp.int32)[lax.axis_index("dp")]
        slot_of_step = [0] * self.size
        for slot, step in enumerate(self.steps):
            slot_of_step[step % self.size] = slot
        step = (jnp.asarray(self.place, jnp.int32) - mine) % self.size
        return jnp.asarray(slot_of_step, jnp.int32)[step]

    def go_up(self, block):
        return lax.ppermute(block, "dp", self.up)

    def go_down(self, block):
        return lax.ppermute(block, "dp", self.down)


class Clock:
    def __init__(self):
        self.last = None

    def tie(self, *arrays):
        if self.last is None:
            out = lax.optimization_barrier(arrays)
        else:
            out = lax.optimization_barrier((*arrays, self.last))[: len(arrays)]
        self.last = out[0]
        return out if len(out) > 1 else out[0]

    def done(self, array):
        self.last = array


class Gather:
    def __init__(self, ring, block, cut):
        self.ring, self.cut = ring, cut
        self.up, self.down = [block], [block]
        self.flying = (ring.go_up(block), ring.go_down(block))
        self.left = ring.half - 1

    def land(self, clock):
        up, down = clock.tie(*self.flying)
        self.flying = None
        self.up.append(up)
        self.down.append(down)

    def go(self, clock):
        up, down = clock.tie(self.up[-1], self.down[-1])
        self.left -= 1
        if self.left == 0:
            up, down = up[: self.cut], down[self.cut :]
        self.flying = (self.ring.go_up(up), self.ring.go_down(down))

    def relay(self, clock):
        if self.left == 0:
            return
        self.left -= 1
        up = clock.tie(self.flying[0])
        self.up.append(up)
        up = self.ring.go_up(up if self.left else up[: self.cut])
        down = clock.tie(self.flying[1])
        self.down.append(down)
        self.flying = (up, self.ring.go_down(down if self.left else down[self.cut :]))

    def finish(self, clock):
        while self.left:
            self.relay(clock)
        return self.up + self.down[1:] + list(clock.tie(*self.flying))


class Scatter:
    def __init__(self, ring, terms, cut, tile):
        self.ring, self.cut, self.tile = ring, cut, tile
        self.terms, up, down = terms
        self.full = self.terms.shape[0] // ring.size
        self.left = ring.half - 1
        self.flying = (ring.go_up(up), ring.go_down(down))

    def term(self, slot, begin=0, end=None):
        end = self.full if end is None else end
        return self.terms[slot * self.full + begin : slot * self.full + end]

    def land(self, clock):
        self.relay(clock, hold=True)

    def go(self, clock):
        up, down = clock.tie(*self.held)
        self.flying = (self.ring.go_up(up), self.ring.go_down(down))

    def relay(self, clock, hold=False):
        if self.left == 0:
            return
        above, below = self.ring.half - 1 + self.left, self.left
        self.left -= 1
        up, down = self.flying
        if up.shape[0] < self.full:
            up, down = clock.tie(up, down)
            self.held = ring_add(
                self.terms, (above, below), up, down, self.full, self.cut, self.tile
            )
            if not hold:
                self.go(clock)
            return
        up = self.ring.go_up(clock.tie(plus(self.term(above), clock.tie(up))))
        down = self.ring.go_down(clock.tie(plus(self.term(below), clock.tie(down))))
        self.flying = (up, down)

    def finish(self, clock):
        while self.left:
            self.relay(clock)
        up, down = clock.tie(*self.flying)
        return clock.tie(self.last(0, self.full, up, down))

    def last(self, begin, end, up, down):
        return (self.term(0, begin, end).astype(F32) + up.astype(F32) + down.astype(F32)).astype(BF)

    def fork(self, clock):
        while self.left > 2:
            self.relay(clock)
        up, down = clock.tie(*self.flying)
        self.rows = [(0, self.cut), (self.cut, self.full)]
        self.parts = []
        for begin, end in self.rows:
            self.parts.append(self.pass_on(2, begin, end, up[begin:end], down[begin:end], clock))

    def pass_on(self, left, begin, end, up, down, clock):
        up = plus(self.term(self.ring.half - 1 + left, begin, end), up)
        down = plus(self.term(left, begin, end), down)
        up, down = clock.tie(up, down)
        return self.ring.go_up(up), self.ring.go_down(down)

    def relay_part(self, part, clock):
        up, down = clock.tie(*self.parts[part])
        self.parts[part] = self.pass_on(1, *self.rows[part], up, down, clock)

    def finish_part(self, part, clock):
        up, down = clock.tie(*self.parts[part])
        return clock.tie(self.last(*self.rows[part], up, down))


def plus(one, two):
    return (one.astype(F32) + two.astype(F32)).astype(BF)


def swap(block, distance):
    return lax.ppermute(block, "seq", [(i, i ^ distance) for i in range(4)])


def fill_weights(pieces, scratch, top, width, columns):
    begin = 0
    for index, piece in enumerate(pieces):
        skip = top if index < len(pieces) - 1 else 0
        count = piece.shape[0] - skip
        scratch[begin : begin + count, :] = piece[skip:, columns]
        begin += count


def put_features(values, order_ref, target, slots, width):
    for j in range(slots):
        to = pl.ds(pl.multiple_of(order_ref[j] * width, 128), width)
        target[:, to] = values[:, j * width : (j + 1) * width]


def blocks_in_order(array, order, size):
    width = array.shape[1] // size
    return jnp.concatenate(
        [lax.dynamic_slice_in_dim(array, order[i] * width, width, 1) for i in range(size)],
        axis=1,
    )


def permute_features(array, order, size):
    width = array.shape[1] // size
    if width % 128:
        return blocks_in_order(array, order, size)

    def body(order_ref, source, target):
        for j in range(size):
            begin = pl.ds(pl.multiple_of(order_ref[j] * width, 128), width)
            target[:, j * width : (j + 1) * width] = source[:, begin]

    return kernel_call(
        body, [(array.shape, array.dtype)], smem=1, args=[order, array], name="permute_features"
    )[0]


def pack_heads(here, w_query, w_key, w_value, w_out, gain_attn, gain_mlp, seq):
    width = w_query.shape[0]
    q_cols, k_cols = w_query.shape[1] // seq, w_key.shape[1] // seq
    total = 2 * q_cols + 2 * k_cols

    def body(here_ref, query_ref, key_ref, value_ref, out_ref, one_ref, two_ref, block_ref):
        s = here_ref[0]
        block_ref[:TOP, :] = jnp.zeros((TOP, total), BF)
        block_ref[:1, :width] = one_ref[...].reshape(1, width)
        block_ref[:1, width : 2 * width] = two_ref[...].reshape(1, width)
        block_ref[TOP:, :q_cols] = query_ref[...]

        def mine(ref):
            part = jnp.zeros((width, k_cols), F32)
            for place in range(seq):
                piece = ref[:, place * k_cols : (place + 1) * k_cols].astype(F32)
                part = jnp.where(s == place, piece, part)
            return part

        both = jnp.concatenate([mine(key_ref), mine(value_ref)], axis=1)
        block_ref[TOP:, q_cols : q_cols + 2 * k_cols] = both.astype(BF)
        block_ref[TOP:, q_cols + 2 * k_cols :] = out_ref[...].astype(F32).T.astype(BF)

    whole = lambda shape: pl.BlockSpec(shape, lambda i, o: (0, 0))
    return pl.pallas_call(
        body,
        out_shape=jax.ShapeDtypeStruct((TOP + width, total), BF),
        grid_spec=pltpu.PrefetchScalarGridSpec(
            num_scalar_prefetch=1,
            grid=(1,),
            in_specs=[
                pl.BlockSpec((width, q_cols), lambda i, o: (0, o[0])),
                whole(w_key.shape),
                whole(w_value.shape),
                pl.BlockSpec((q_cols, width), lambda i, o: (o[0], 0)),
                pl.BlockSpec((width,), lambda i, o: (0,)),
                pl.BlockSpec((width,), lambda i, o: (0,)),
            ],
            out_specs=whole((TOP + width, total)),
        ),
        compiler_params=limits("pack_heads"),
        name="pack_heads",
    )(here, w_query, w_key, w_value, w_out, gain_attn, gain_mlp)


def pack_mlp(here, w_gate, w_up, w_down, bounds, seq):
    width, ff = w_gate.shape[0], w_gate.shape[1] // seq

    def body(here_ref, gate_ref, up_ref, down_ref, *blocks):
        for (a, b), block in zip(bounds, blocks):
            size = b - a
            block[:, :size] = gate_ref[:, a:b]
            block[:, size : 2 * size] = up_ref[:, a:b]
            block[:, 2 * size :] = down_ref[a:b, :].astype(F32).T.astype(BF)

    columns = pl.BlockSpec((width, ff), lambda i, o: (0, o[0]))
    return pl.pallas_call(
        body,
        out_shape=tuple(jax.ShapeDtypeStruct((width, 3 * (b - a)), BF) for a, b in bounds),
        grid_spec=pltpu.PrefetchScalarGridSpec(
            num_scalar_prefetch=1,
            grid=(1,),
            in_specs=[columns, columns, pl.BlockSpec((ff, width), lambda i, o: (o[0], 0))],
            out_specs=tuple(
                pl.BlockSpec((width, 3 * (b - a)), lambda i, o: (0, 0)) for a, b in bounds
            ),
        ),
        compiler_params=limits("pack_mlp"),
        name="pack_mlp",
    )(here, w_gate, w_up, w_down)


def turn(values, cosine, sine_part):
    half_dim = HD // 2
    pieces = []
    for h in range(values.shape[0] // HD):
        first = values[h * HD : h * HD + half_dim]
        second = values[h * HD + half_dim : (h + 1) * HD]
        pieces.append(first * cosine - second * sine_part)
        pieces.append(second * cosine + first * sine_part)
    return jnp.concatenate(pieces, axis=0)


def rounded(values):
    return values.astype(BF).astype(F32)


def pick(refs, place, target):
    rows = target.shape[0]
    at = 0
    for ref in refs:
        index, begin, count = at // rows, at % rows, ref.shape[0]
        at += count

        @pl.when(place == index)
        def _():
            target[begin : begin + count, :] = ref[...]


def write_bias(bias_ref, lengths_ref, live, block, rows):
    keys = (block + 1) * rows
    query = lax.broadcasted_iota(jnp.int32, (1, rows), 1) + block * rows
    low = jnp.zeros((1, rows), jnp.int32)
    start = 0
    for slot in range(lengths_ref.shape[0]):
        low = jnp.where(query >= start, jnp.maximum(low, start), low)
        start = start + lengths_ref[slot]
    high = jnp.minimum(query, live - 1)
    key = lax.broadcasted_iota(jnp.int32, (keys, rows), 0)
    allowed = ((key >= low) & (key <= high)) | (key == query)
    bias_ref[:keys, :] = jnp.where(allowed, 0.0, NEG)


def attention_forward(places, lengths, live, tokens, pieces, cosine, sine_part, q_cols):
    rows, model = tokens[0].shape
    pack_size = 4 * rows
    n_heads = q_cols // HD
    heads_cols = q_cols + 2 * HD
    width = pieces[0].shape[0] - TOP

    def body(places_ref, lengths_ref, live_ref, cos_ref, sin_ref, *refs):
        token_refs, piece_refs, refs = refs[:4], refs[4 : 4 + len(pieces)], refs[4 + len(pieces) :]
        (
            normed_ref, query_ref, kv_ref, kvt_ref, lse_ref, mixed_t_ref, mixed_ref, keep_ref,
            send_ref, gains_ref, w_ref, bias_ref, query_s, mixed_s, tokens_s,
        ) = refs
        live_count = live_ref[0]
        fill_weights(piece_refs, w_ref, TOP, width, slice(None))
        gains_ref[...] = jnp.zeros_like(gains_ref)
        for index, piece in enumerate(piece_refs[:-1]):
            at = slice(index * width, (index + 1) * width)
            gains_ref[0:1, at] = piece[0:1, :width].astype(F32)
            gains_ref[1:2, at] = piece[0:1, width : 2 * width].astype(F32)
        ones = jnp.ones((HD, rows), BF)
        for block in range(4):
            place = places_ref[block]
            at = slice(block * rows, (block + 1) * rows)
            keys = (block + 1) * rows
            to = pl.ds(pl.multiple_of(place * rows, rows), rows)
            pick(token_refs, place, tokens_s)
            inputs = tokens_s[...].astype(F32)
            inverse = lax.rsqrt(jnp.mean(inputs * inputs, axis=1, keepdims=True) + EPS)
            normed = (inputs * inverse * gains_ref[0:1, :]).astype(BF)
            normed_ref[to, :] = normed
            pre = dot(normed, w_ref[:, :heads_cols]).T
            cos_b, sin_b = cos_ref[:, at], sin_ref[:, at]
            query = (rounded(turn(pre[:q_cols], cos_b, sin_b)) * HD**-0.5).astype(BF)
            query_s[...] = query
            query_ref[:, at] = query
            key_t = rounded(turn(pre[q_cols : q_cols + HD], cos_b, sin_b))
            value_t = rounded(pre[q_cols + HD :])
            kv_t = jnp.concatenate([key_t, value_t], axis=0)
            kv_ref[at, :] = kv_t.T.astype(BF)
            kvt_ref[: 2 * HD, at] = kv_t.astype(BF)
            kvt_ref[2 * HD :, at] = ones
            write_bias(bias_ref, lengths_ref, live_count, block, rows)

            def attend(h, _):
                mine = pl.ds(pl.multiple_of(h * HD, HD), HD)
                scores = dot(kv_ref[:keys, :HD], query_s[mine, :]) + bias_ref[:keys, :]
                peak = jnp.max(scores, axis=0, keepdims=True)
                weights = jnp.exp(scores - peak).astype(BF)
                summed = dot(kvt_ref[HD:, :keys], weights)
                total = summed[HD : HD + 1]
                mixed = summed[:HD] * (1.0 / total)
                mixed_s[mine, :] = mixed
                lse_ref[pl.ds(h, 1), at] = peak + jnp.log(total)
                return 0

            lax.fori_loop(0, n_heads, attend, 0, unroll=2)
            mixed_t = mixed_s[...]
            mixed_t_ref[:, at] = mixed_t
            mixed = mixed_t.T.astype(BF)
            mixed_ref[to, :] = mixed
            branch = against(mixed, w_ref[:, heads_cols:]).astype(BF)
            half_to = pl.ds(pl.multiple_of((place % 2) * rows, rows), rows)

            @pl.when(place < 2)
            def _():
                keep_ref[half_to, :] = branch

            @pl.when(place >= 2)
            def _():
                send_ref[half_to, :] = branch

    args = [places, lengths, live, cosine, sine_part, *tokens, *pieces]
    flops = 2 * pack_size * model * (heads_cols + q_cols) + 4 * n_heads * pack_size**2 * HD * 3
    return kernel_call(
        body,
        [
            ((pack_size, model), BF),
            ((q_cols, pack_size), BF),
            ((pack_size, 2 * HD), BF),
            ((3 * HD, pack_size), BF),
            ((n_heads, pack_size), F32),
            ((q_cols, pack_size), F32),
            ((pack_size, q_cols), BF),
            ((pack_size // 2, model), BF),
            ((pack_size // 2, model), BF),
            ((8, model), F32),
        ],
        scratch=[
            pltpu.VMEM((model, heads_cols + q_cols), BF),
            pltpu.VMEM((pack_size, rows), F32),
            pltpu.VMEM((q_cols, rows), BF),
            pltpu.VMEM((q_cols, rows), F32),
            pltpu.VMEM((rows, model), BF),
        ],
        flops=flops,
        moved=30 << 20,
        smem=3,
        args=args,
        name="attention_forward",
    )


def attention_backward(
    places, lengths, live, tokens, pieces, cosine, sine_part, query, kv, kvt, lse, mixed_t
):
    q_cols, pack_size = query.shape
    rows, model = tokens[0].shape
    n_heads = q_cols // HD
    heads_cols = q_cols + 2 * HD
    width = pieces[0].shape[0] - TOP

    def body(
        places_ref, lengths_ref, live_ref, cos_ref, sin_ref,
        query_ref, kv_ref, kvt_ref, lse_ref, mixed_t_ref, *refs
    ):
        token_refs, piece_refs, refs = refs[:4], refs[4 : 4 + len(pieces)], refs[4 + len(pieces) :]
        (
            grad_q_ref, grad_kv_ref, w_ref, bias_ref, grad_s, grad_q_s, key_acc, value_acc, inner_s,
            tokens_s,
        ) = refs
        live_count = live_ref[0]
        fill_weights(piece_refs, w_ref, TOP, width, slice(heads_cols, heads_cols + q_cols))
        key_acc[...] = jnp.zeros_like(key_acc)
        value_acc[...] = jnp.zeros_like(value_acc)
        for block in range(4):
            place = places_ref[block]
            at = slice(block * rows, (block + 1) * rows)
            keys = (block + 1) * rows
            to = pl.ds(pl.multiple_of(place * rows, rows), rows)
            pick(token_refs, place, tokens_s)
            grad_t = rounded(dot(tokens_s[...], w_ref[...]).T)
            grad_s[...] = grad_t.astype(BF)
            product = grad_t * mixed_t_ref[:, at]
            for h in range(n_heads):
                inner_s[h : h + 1, :] = jnp.sum(
                    product[h * HD : (h + 1) * HD], axis=0, keepdims=True
                )
            write_bias(bias_ref, lengths_ref, live_count, block, rows)

            def attend(h, _):
                mine = pl.ds(pl.multiple_of(h * HD, HD), HD)
                query_h = query_ref[mine, at]
                grad_h = grad_s[mine, :]
                scores = dot(kv_ref[:keys, :HD], query_h) + bias_ref[:keys, :]
                probs = jnp.exp(scores - lse_ref[pl.ds(h, 1), at])
                grad_probs = dot(kv_ref[:keys, HD:], grad_h)
                grad_scores = (probs * (grad_probs - inner_s[pl.ds(h, 1), :])).astype(BF)
                grad_q_s[mine, :] = dot(kvt_ref[:HD, :keys], grad_scores) * HD**-0.5
                key_acc[:keys, :] += against(grad_scores, query_h)
                value_acc[:keys, :] += against(probs.astype(BF), grad_h)
                return 0

            lax.fori_loop(0, n_heads, attend, 0, unroll=8)
            turned = turn(rounded(grad_q_s[...]), cos_ref[:, at], -sin_ref[:, at])
            grad_q_ref[to, :] = turned.T.astype(BF)
        for block in range(4):
            at = slice(block * rows, (block + 1) * rows)
            to = pl.ds(pl.multiple_of(places_ref[block] * rows, rows), rows)
            key_t = turn(rounded(key_acc[at, :]).T, cos_ref[:, at], -sin_ref[:, at])
            grad_kv_ref[to, :] = jnp.concatenate([key_t.T, value_acc[at, :]], axis=1).astype(BF)

    args = [
        places, lengths, live, cosine, sine_part, query, kv, kvt, lse, mixed_t, *tokens, *pieces
    ]
    return kernel_call(
        body,
        [((pack_size, q_cols), BF), ((pack_size, 2 * HD), BF)],
        scratch=[
            pltpu.VMEM((model, q_cols), BF),
            pltpu.VMEM((pack_size, rows), F32),
            pltpu.VMEM((q_cols, rows), BF),
            pltpu.VMEM((q_cols, rows), F32),
            pltpu.VMEM((pack_size, HD), F32),
            pltpu.VMEM((pack_size, HD), F32),
            pltpu.VMEM((n_heads, rows), F32),
            pltpu.VMEM((rows, model), BF),
        ],
        flops=2 * pack_size * model * q_cols + 10 * n_heads * pack_size**2 * HD * 3,
        moved=20 << 20,
        smem=3,
        args=args,
        name="attention_backward",
    )


def heads_back(grad_q, grad_kv, tokens, pieces):
    pack_size, q_cols = grad_q.shape
    rows, model = tokens[0].shape
    heads_cols = q_cols + 2 * HD
    width = pieces[0].shape[0] - TOP

    def body(grad_q_ref, grad_kv_ref, *refs):
        token_refs, piece_refs = refs[:4], refs[4 : 4 + len(pieces)]
        keep_ref, send_ref, gain_ref, w_ref, tokens_s = refs[4 + len(pieces) :]
        step = pl.program_id(0)

        @pl.when(step == 0)
        def _():
            fill_weights(piece_refs, w_ref, TOP, width, slice(0, heads_cols))
            gain_ref[...] = jnp.zeros_like(gain_ref)

        pick(token_refs, step, tokens_s)
        inputs = tokens_s[...].astype(F32)
        inverse = lax.rsqrt(jnp.mean(inputs * inputs, axis=1, keepdims=True) + EPS)
        grad = against(grad_q_ref[...], w_ref[:, :q_cols]) + against(
            grad_kv_ref[...], w_ref[:, q_cols:]
        )

        @pl.when(step < 2)
        def _():
            keep_ref[...] = grad.astype(BF)

        @pl.when(step >= 2)
        def _():
            send_ref[...] = grad.astype(BF)

        total = jnp.sum(grad * inputs * inverse, axis=0, keepdims=True)
        gain_ref[...] += jnp.broadcast_to(total, gain_ref.shape)

    first = pl.BlockSpec((rows, model), lambda i: (jnp.minimum(i, 1), 0))
    second = pl.BlockSpec((rows, model), lambda i: (jnp.maximum(i - 2, 0), 0))
    fixed = lambda a: pl.BlockSpec(memory_space=pltpu.VMEM)
    half = jax.ShapeDtypeStruct((pack_size // 2, model), BF)
    return pl.pallas_call(
        body,
        grid=(4,),
        out_shape=(half, half, jax.ShapeDtypeStruct((8, model), F32)),
        in_specs=[
            pl.BlockSpec((rows, q_cols), lambda i: (i, 0)),
            pl.BlockSpec((rows, 2 * HD), lambda i: (i, 0)),
        ]
        + [fixed(a) for a in (*tokens, *pieces)],
        out_specs=(first, second, pl.BlockSpec((8, model), lambda i: (0, 0))),
        scratch_shapes=[pltpu.VMEM((model, heads_cols), BF), pltpu.VMEM((rows, model), BF)],
        compiler_params=limits("heads_back"),
        cost_estimate=COST,
        name="heads_back",
    )(grad_q, grad_kv, *tokens, *pieces)


def mlp_chunk(tokens, cots, pieces, before, size, room):
    rows, model = tokens[0].shape
    pack_size = 4 * rows

    def body(*refs):
        token_refs, cot_refs, refs = refs[:4], refs[4:8], refs[8:]
        piece_refs, refs = refs[: len(pieces)], refs[len(pieces) :]
        before_refs, refs = refs[: len(before)], refs[len(before) :]
        down_keep, down_send, grad_keep, grad_send, both_ref, w_ref, tokens_s, cot_s = refs
        step = pl.program_id(0)

        @pl.when(step == 0)
        def _():
            fill_weights(piece_refs, w_ref, 0, model, slice(None))

        pick(token_refs, step, tokens_s)
        pick(cot_refs, step, cot_s)
        both = dot(tokens_s[...], w_ref[:, : 2 * size])
        grad_act = dot(cot_s[...], w_ref[:, 2 * size :])
        gate_pre, up_pre = both[:, :size], both[:, size:]
        sig = 1.0 / (1.0 + jnp.exp(-gate_pre))
        active = gate_pre * sig
        both_ref[:, 2 * size :] = (active * up_pre).astype(BF)
        both_ref[:, size : 2 * size] = (grad_act * active).astype(BF)
        both_ref[:, :size] = (grad_act * up_pre * (sig + active * (1.0 - sig))).astype(BF)
        down = against(both_ref[:, 2 * size :], w_ref[:, 2 * size :])
        grad = against(both_ref[:, : 2 * size], w_ref[:, : 2 * size])

        def put(keep, send, value, keep_before, send_before):
            @pl.when(step < 2)
            def _():
                extra = 0.0 if keep_before is None else keep_before[...].astype(F32)
                keep[...] = (value + extra).astype(BF)

            @pl.when(step >= 2)
            def _():
                extra = 0.0 if send_before is None else send_before[...].astype(F32)
                send[...] = (value + extra).astype(BF)

        old = before_refs or [None] * 4
        put(down_keep, down_send, down, old[0], old[1])
        put(grad_keep, grad_send, grad, old[2], old[3])

    first = pl.BlockSpec((rows, model), lambda i: (jnp.minimum(i, 1), 0))
    second = pl.BlockSpec((rows, model), lambda i: (jnp.maximum(i - 2, 0), 0))
    fixed = pl.BlockSpec(memory_space=pltpu.VMEM)
    half = pltpu.HBM((pack_size // 2, model), BF)
    return pl.pallas_call(
        body,
        grid=(4,),
        out_shape=(half, half, half, half, pltpu.HBM((pack_size, 3 * size), BF)),
        in_specs=[fixed] * (8 + len(pieces)) + [first, second] * (len(before) // 2),
        out_specs=(first, second, first, second, pl.BlockSpec((rows, 3 * size), lambda i: (i, 0))),
        scratch_shapes=[
            pltpu.VMEM((model, 3 * size), BF),
            pltpu.VMEM((rows, model), BF),
            pltpu.VMEM((rows, model), BF),
        ],
        compiler_params=limits(room),
        cost_estimate=COST,
        name="mlp_chunk",
    )(*tokens, *cots, *pieces, *before)


def weight_terms(pairs, width, n_slots, group, cut, tops=None):
    tokens = sum(x.shape[0] for x in pairs[0][0])
    total = sum(cols.stop - cols.start for _, _, cols in pairs)
    head = 0 if tops is None else TOP

    def distinct(lists):
        out = []
        for one in lists:
            if not any(one is other for other in out):
                out.append(one)
        return out

    x_lists = distinct(x for x, _, _ in pairs)
    g_lists = distinct(g for _, g, _ in pairs)
    while (width * group) % 128:
        group *= 2
    wide = width * group
    args, specs = [], []
    for x in [x for xs in x_lists for x in xs]:
        args.append(x)
        specs.append(pl.BlockSpec((x.shape[0], wide), lambda i: (0, i)))
    for g in [g for gs in g_lists for g in gs]:
        args.append(g)
        specs.append(pl.BlockSpec(memory_space=pltpu.VMEM))
    if head:
        args.append(tops)
        specs.append(pl.BlockSpec((group * TOP, total), lambda i: (i, 0)))

    def body(*refs):
        def take(lists):
            nonlocal refs
            out = []
            for one in lists:
                out.append((one, refs[: len(one)]))
                refs = refs[len(one) :]
            return out

        x_refs, g_refs = take(x_lists), take(g_lists)
        out_ref, up_ref, down_ref, x_s = refs[-4:]
        lane = 0
        filled = None
        for xs, gs, cols in pairs:
            parts = next(r for other, r in x_refs if other is xs)
            g_parts = next(r for other, r in g_refs if other is gs)
            if len(parts) > 1 and filled is not xs:
                at = 0
                for part in parts:
                    x_s[at : at + part.shape[0], :] = part[...]
                    at += part.shape[0]
                filled = xs
            product, at = None, 0
            for g in g_parts:
                rows = g.shape[0]
                x = (x_s if len(parts) > 1 else parts[0])[at : at + rows, :]
                at += rows
                more = cross(x, g[:, cols])
                product = more if product is None else product + more
            product = product.astype(BF)
            count = cols.stop - cols.start
            for j in range(group):
                at = j * (head + width) + head
                out_ref[at : at + width, lane : lane + count] = product[
                    j * width : (j + 1) * width
                ]
            lane += count
        if head:
            for j in range(group):
                at = j * (head + width)
                out_ref[at : at + head, :] = refs[0][j * TOP : (j + 1) * TOP, :]

        @pl.when(pl.program_id(0) == n_slots // group - 1)
        def _():
            begin = (group - 1) * (head + width)
            up_ref[...] = out_ref[begin : begin + cut, :]
            down_ref[...] = out_ref[begin + cut : begin + head + width, :]

    far = [(cut, total), (head + width - cut, total)]
    return pl.pallas_call(
        body,
        grid=(n_slots // group,),
        out_shape=(
            jax.ShapeDtypeStruct((n_slots * (head + width), total), BF),
            *[jax.ShapeDtypeStruct(shape, BF) for shape in far],
        ),
        in_specs=specs,
        out_specs=(
            pl.BlockSpec((group * (head + width), total), lambda i: (i, 0)),
            *[pl.BlockSpec(shape, lambda i: (0, 0)) for shape in far],
        ),
        scratch_shapes=[pltpu.VMEM((tokens, wide), BF)],
        compiler_params=limits("weight_terms"),
        cost_estimate=COST,
        name="weight_terms",
    )(*args)


def ring_add(terms, slots, up, down, full, cut, tile):
    total = terms.shape[1]

    def body(up_term, down_term, up_ref, down_ref, up_out, down_out):
        if up_ref.shape[0] == full:
            up_out[...] = (up_term[...].astype(F32) + up_ref[...].astype(F32)).astype(BF)
            down_out[...] = (down_term[...].astype(F32) + down_ref[...].astype(F32)).astype(BF)
        else:
            up_out[:cut, :] = (up_term[:cut, :].astype(F32) + up_ref[...].astype(F32)).astype(BF)
            up_out[cut:, :] = up_term[cut:, :]
            down_out[:cut, :] = down_term[:cut, :]
            down_out[cut:, :] = (
                down_term[cut:, :].astype(F32) + down_ref[...].astype(F32)
            ).astype(BF)

    columns = lambda array: pl.BlockSpec((array.shape[0], tile), lambda i: (0, i))
    out = jax.ShapeDtypeStruct((full, total), BF)
    return pl.pallas_call(
        body,
        grid=(total // tile,),
        out_shape=(out, out),
        in_specs=[
            pl.BlockSpec((full, tile), lambda i: (slots[0], i)),
            pl.BlockSpec((full, tile), lambda i: (slots[1], i)),
            columns(up),
            columns(down),
        ],
        out_specs=(columns(out), columns(out)),
        compiler_params=limits("ring_add"),
        cost_estimate=COST,
        name="ring_add",
    )(terms, terms, up, down)


def row_call(body, outs, row_args, fixed_args, steps, smem=(), name=None):
    rows = outs[0][0][0] if outs[0][2] else row_args[0][0].shape[0]
    tile = rows // steps
    n_smem = len(smem)
    by_rows = lambda cols, at: pl.BlockSpec((tile, cols), lambda i, *_: (i + at, 0))
    return pl.pallas_call(
        body,
        out_shape=tuple(jax.ShapeDtypeStruct(s, d) for s, d, _ in outs),
        grid_spec=pltpu.PrefetchScalarGridSpec(
            num_scalar_prefetch=n_smem,
            grid=(steps,),
            in_specs=[by_rows(a.shape[1], at * steps) for a, at in row_args]
            + [pl.BlockSpec(a.shape, lambda i, *_: (0, 0)) for a in fixed_args],
            out_specs=tuple(
                by_rows(s[1], 0) if split else pl.BlockSpec(s, lambda i, *_: (0, 0))
                for s, _, split in outs
            ),
        ),
        compiler_params=limits(name),
        cost_estimate=COST,
        name=name,
    )(*smem, *[a for a, _ in row_args], *fixed_args)


STEPS = 2


def second_norm(inputs, keep, came, last, gains):
    def body(inputs_ref, keep_ref, came_ref, last_ref, gains_ref, hidden_ref, normed_ref):
        branch = keep_ref[...].astype(F32) + came_ref[...].astype(F32) + last_ref[...].astype(F32)
        hidden = inputs_ref[...].astype(F32) + branch
        inverse = lax.rsqrt(jnp.mean(hidden * hidden, axis=1, keepdims=True) + EPS)
        hidden_ref[...] = hidden
        normed_ref[...] = (hidden * inverse * gains_ref[1:2, :]).astype(BF)

    return row_call(
        body,
        [(inputs.shape, F32, True), (inputs.shape, BF, True)],
        [(inputs, 0), (keep, 0), (came, 0), (last, 0)],
        [gains],
        STEPS,
        name="second_norm",
    )


def norm_back(grad, values, gain):
    inverse = lax.rsqrt(jnp.mean(values * values, axis=1, keepdims=True) + EPS)
    scaled = grad * gain
    mean = jnp.mean(scaled * values, axis=1, keepdims=True)
    return inverse, inverse * (scaled - values * (inverse * inverse * mean))


def second_norm_back(cot, hidden, keep, came, last, gains):
    rows, model = hidden.shape

    def body(cot_ref, hidden_ref, keep_ref, came_ref, last_ref, gains_ref, grad_ref, low_ref, gain_ref):
        @pl.when(pl.program_id(0) == 0)
        def _():
            gain_ref[...] = jnp.zeros_like(gain_ref)

        grad = keep_ref[...].astype(F32) + came_ref[...].astype(F32) + last_ref[...].astype(F32)
        hidden_v = hidden_ref[...]
        inverse, back = norm_back(grad, hidden_v, gains_ref[1:2, :])
        total = jnp.sum(grad * hidden_v * inverse, axis=0, keepdims=True)
        gain_ref[...] += jnp.broadcast_to(total, gain_ref.shape)
        out = cot_ref[...].astype(F32) + back
        grad_ref[...] = out
        low_ref[...] = out.astype(BF)

    return row_call(
        body,
        [((rows, model), F32, True), ((rows, model), BF, True), ((8, model), F32, False)],
        [(cot, 0), (hidden, 0), (keep, 0), (came, 0), (last, 0)],
        [gains],
        STEPS,
        name="second_norm_back",
    )


def first_norm_back(grad_hidden, inputs, keep, came, last, gains, order, n_slots):
    width = inputs.shape[1] // n_slots

    def body(order_ref, grad_ref, inputs_ref, keep_ref, came_ref, last_ref, gains_ref, out_ref):
        grad = keep_ref[...].astype(F32) + came_ref[...].astype(F32) + last_ref[...].astype(F32)
        _, back = norm_back(grad, inputs_ref[...].astype(F32), gains_ref[0:1, :])
        out = (grad_ref[...] + back).astype(BF)
        if width % 128:
            out_ref[...] = out
        else:
            put_features(out, order_ref, out_ref, n_slots, width)

    return row_call(
        body,
        [(inputs.shape, BF, True)],
        [(grad_hidden, 0), (inputs, 0), (keep, 0), (came, 0), (last, 0)],
        [gains],
        STEPS,
        smem=(order,),
        name="first_norm_back",
    )[0]


def layer_output(hidden, keep, came, last, order, n_slots):
    width = hidden.shape[1] // n_slots

    def body(order_ref, hidden_ref, keep_ref, came_ref, last_ref, out_ref):
        down = keep_ref[...].astype(F32) + came_ref[...].astype(F32) + last_ref[...].astype(F32)
        out = (hidden_ref[...] + down).astype(BF)
        if width % 128:
            out_ref[...] = out
        else:
            put_features(out, order_ref, out_ref, n_slots, width)

    return row_call(
        body,
        [(hidden.shape, BF, True)],
        [(hidden, 0), (keep, 0), (came, 0), (last, 0)],
        [],
        STEPS,
        smem=(order,),
        name="layer_output",
    )[0]


def unpack_mlp(places, chunks, bounds, width, ff):
    flat = [block for blocks in chunks for block in blocks]

    def body(places_ref, *refs):
        ins = refs[: len(flat)]
        gate_ref, up_ref, down_ref = refs[len(flat) : len(flat) + 3]
        scratches = refs[len(flat) + 3 :]
        place = places_ref[pl.program_id(0)]
        for c, (a, b) in enumerate(bounds):
            size = b - a
            block_s = scratches[c]
            pick(ins[4 * c : 4 * c + 4], place, block_s)
            gate_ref[:, a:b] = block_s[:, :size].astype(F32)
            up_ref[:, a:b] = block_s[:, size : 2 * size].astype(F32)
            down_ref[a:b, :] = block_s[:, 2 * size :].astype(F32).T

    columns = pl.BlockSpec((width, ff), lambda i, p: (0, i))
    return pl.pallas_call(
        body,
        out_shape=(
            jax.ShapeDtypeStruct((width, 4 * ff), F32),
            jax.ShapeDtypeStruct((width, 4 * ff), F32),
            jax.ShapeDtypeStruct((4 * ff, width), F32),
        ),
        grid_spec=pltpu.PrefetchScalarGridSpec(
            num_scalar_prefetch=1,
            grid=(4,),
            in_specs=[
                pl.BlockSpec(h.shape, lambda i, p: (0, 0), pipeline_mode=pl.Buffered(1))
                for h in flat
            ],
            out_specs=(columns, columns, pl.BlockSpec((ff, width), lambda i, p: (i, 0))),
            scratch_shapes=[pltpu.VMEM((width, 3 * (b - a)), BF) for a, b in bounds],
        ),
        compiler_params=limits("unpack_mlp"),
        cost_estimate=COST,
        name="unpack_mlp",
    )(places, *flat)


def unpack_heads(places, heads, width, q_cols):
    kv = q_cols + 2 * HD

    def body(places_ref, *refs):
        head_refs = refs[: len(heads)]
        query_ref, key_ref, value_ref, out_ref, gain_ref, head_s = refs[len(heads) :]
        gain = jnp.zeros((8, 2 * width), F32)
        for place in range(4):
            pick(head_refs, places_ref[place], head_s)
            gain = gain + head_s[:TOP, : 2 * width].astype(F32)[:8]
            at = slice(place * q_cols, (place + 1) * q_cols)
            query_ref[:, at] = head_s[TOP:, :q_cols].astype(F32)
            both = head_s[TOP:, q_cols:kv].astype(F32)
            key_ref[:, place * HD : (place + 1) * HD] = both[:, :HD]
            value_ref[:, place * HD : (place + 1) * HD] = both[:, HD:]
            out_ref[at, :] = head_s[TOP:, kv:].astype(F32).T
        gain_ref[...] = gain

    args = [places, *heads]
    return kernel_call(
        body,
        [
            ((width, 4 * q_cols), F32),
            ((width, 4 * HD), F32),
            ((width, 4 * HD), F32),
            ((4 * q_cols, width), F32),
            ((8, 2 * width), F32),
        ],
        scratch=[pltpu.VMEM((TOP + width, heads[0].shape[1]), BF)],
        smem=1,
        args=args,
        name="unpack_heads",
    )


def doc_positions(lengths, pack_size):
    doc_starts = jnp.cumsum(lengths) - lengths
    places = jnp.arange(pack_size, dtype=jnp.int32)
    doc_first = jnp.max(
        jnp.where(places[:, None] >= doc_starts[None, :], doc_starts[None, :], 0), axis=1
    )
    return places - doc_first


def rotary_tables(positions):
    half_dim = HD // 2
    frequency = 10000.0 ** (-2.0 * jnp.arange(half_dim, dtype=F32) / HD)
    angle_table = frequency[:, None] * positions.astype(F32)[None, :]
    return (jnp.cos(angle_table), jnp.sin(angle_table))


def layer(
    hidden_in,
    cotangent,
    gain_attn,
    w_query,
    w_key,
    w_value,
    w_out,
    gain_mlp,
    w_gate,
    w_up,
    w_down,
    doc_lengths,
    valid_count,
):
    seq = lax.axis_size("seq")
    n_dp = lax.axis_size("dp")
    here = lax.axis_index("seq").astype(jnp.int32)
    ring = Ring(n_dp)
    rows, model = hidden_in.shape
    pack_size = rows * seq
    width = gain_attn.shape[0]
    q_cols = w_query.shape[1] // seq
    ff = w_gate.shape[1] // seq
    here_1 = here.reshape(1)
    lengths, live = doc_lengths[0], valid_count[:1]
    middle = width // 2

    offset = here ^ jnp.arange(4, dtype=jnp.int32)
    places = (offset % 2) * 2 + offset // 2

    first = (ff // 2 + 127) // 128 * 128
    bounds = [(0, first), (first, ff)]
    sizes = [b - a for a, b in bounds]

    def other_half(keep, came):
        return plus(keep[rows:], came[rows:])

    def far_memory(*arrays):
        return [pltpu.with_memory_space_constraint(a, pltpu.HBM) for a in arrays]

    def four(block, across, beside):
        return [block, across, beside, swap(across, 1)]

    clock = Clock()
    head_block = pack_heads(here_1, w_query, w_key, w_value, w_out, gain_attn, gain_mlp, seq)
    clock.done(head_block)
    heads = Gather(ring, head_block, TOP + middle)
    hidden_in, cotangent = clock.tie(hidden_in, cotangent)
    mine = permute_features(hidden_in, ring.slot_owners(), n_dp)
    clock.done(mine)
    across, beside = swap(mine, 2), swap(mine, 1)
    w_gate, w_up, w_down, cotangent = clock.tie(w_gate, w_up, w_down, cotangent)
    blocks = pack_mlp(here_1, w_gate, w_up, w_down, bounds, seq)
    clock.done(blocks[0])
    heads.relay(clock)
    cotangent = clock.tie(cotangent)
    my_cot = permute_features(cotangent, ring.slot_owners(), n_dp)
    cosine, sine_part = rotary_tables(doc_positions(lengths, pack_size))
    cosine, sine_part, my_cot = clock.tie(cosine, sine_part, my_cot)
    heads.relay(clock)
    across, my_cot = clock.tie(across, my_cot)
    tokens = four(mine, across, beside)
    cot_across, cot_beside = swap(my_cot, 2), swap(my_cot, 1)
    heads.relay(clock)
    head_pieces = heads.finish(clock)
    tokens = list(clock.tie(*tokens))
    blocks = clock.tie(*blocks)
    chunks = [Gather(ring, block, middle) for block in blocks]
    normed, query, kv, kvt, lse, mixed_t, mixed, keep, send, gains = attention_forward(
        places, lengths, live, tokens, head_pieces, cosine, sine_part, q_cols
    )
    normed, query, kv, kvt, mixed_t, mixed = far_memory(normed, query, kv, kvt, mixed_t, mixed)
    clock.done(lse)
    chunks[0].relay(clock)
    chunks[1].land(clock)
    cot_across, send = clock.tie(cot_across, send)
    came = clock.tie(swap(send, 1))
    last = swap(clock.tie(other_half(keep, came)), 2)
    cots = four(my_cot, cot_across, cot_beside)
    chunks[0].relay(clock)
    last = clock.tie(last)
    hidden, my_normed = second_norm(mine, keep, came, last, gains)
    clock.done(my_normed)
    across, beside = swap(my_normed, 2), swap(my_normed, 1)
    beside = clock.tie(beside)
    chunks[0].relay(clock)
    across = clock.tie(across)
    seconds = four(my_normed, across, beside)
    pieces = chunks[0].finish(clock)
    chunks[1].go(clock)
    seconds = list(clock.tie(*seconds))
    cots = list(clock.tie(*cots))

    def terms_of(both, size):
        return weight_terms(
            [(seconds, [both], slice(0, 2 * size)), (cots, [both], slice(2 * size, 3 * size))],
            width,
            n_dp,
            2,
            middle,
        )

    *before, both = mlp_chunk(seconds, cots, pieces, (), sizes[0], "mlp_chunk")
    clock.done(both)
    chunks[1].relay(clock)
    terms = terms_of(clock.tie(both), sizes[0])
    clock.done(terms[0])
    sums = [Scatter(ring, terms, middle, sizes[0])]
    chunks[1].relay(clock)
    sums[0].land(clock)
    pieces = far_memory(*chunks[1].finish(clock))
    sums[0].go(clock)
    down_keep, down_send, grad_keep, grad_send, both = mlp_chunk(
        seconds, cots, clock.tie(*pieces), before, sizes[1], "mlp_chunk_far"
    )
    clock.done(both)
    sums[0].relay(clock)
    grad_send, down_send = clock.tie(grad_send, down_send)
    came, down_came = swap(grad_send, 1), swap(down_send, 1)
    came = clock.tie(came)
    last = swap(clock.tie(other_half(grad_keep, came)), 2)
    terms = terms_of(clock.tie(both), sizes[1])
    clock.done(terms[0])
    sums.append(Scatter(ring, terms, middle, sizes[1]))
    down_came = clock.tie(down_came)
    sums[0].relay(clock)
    sums[1].relay(clock)
    last = clock.tie(last)
    grad_hidden, my_branch, gain_two_terms = second_norm_back(
        my_cot, hidden, grad_keep, came, last, gains
    )
    clock.done(my_branch)
    across, beside = swap(my_branch, 2), swap(my_branch, 1)
    down_other = clock.tie(other_half(down_keep, down_came))
    beside = clock.tie(beside)
    chunk_sum = sums[0].finish(clock)
    chunk_across, chunk_beside = swap(chunk_sum, 2), swap(chunk_sum, 1)
    across = clock.tie(across)
    branches = four(my_branch, across, beside)
    branches = list(clock.tie(*branches))
    grad_q, grad_kv = attention_backward(
        places, lengths, live, branches, head_pieces, cosine, sine_part,
        query, kv, kvt, lse, mixed_t
    )
    clock.done(grad_kv)
    sums[1].relay(clock)
    chunk_across, chunk_beside = clock.tie(chunk_across, chunk_beside)
    firsts = four(chunk_sum, chunk_across, chunk_beside)
    down_last = swap(clock.tie(down_other), 2)
    tokens = clock.tie(*tokens)
    grad_keep, grad_send, gain_one_terms = heads_back(grad_q, grad_kv, tokens, head_pieces)
    clock.done(gain_one_terms)
    columns = head_block.shape[1]
    tops = jnp.concatenate(
        [
            gain_one_terms[0].reshape(n_dp, width),
            gain_two_terms[0].reshape(n_dp, width),
            jnp.zeros((n_dp, columns - 2 * width), F32),
        ],
        axis=1,
    ).astype(BF)
    tops = jnp.pad(tops[:, None], ((0, 0), (0, TOP - 1), (0, 0))).reshape(n_dp * TOP, -1)
    normed, tops = clock.tie(normed, tops)
    normed = [normed]
    head_terms = weight_terms(
        [
            (normed, [grad_q], slice(0, q_cols)),
            (normed, [grad_kv], slice(0, 2 * HD)),
            (branches, [mixed], slice(0, q_cols)),
        ],
        width,
        n_dp,
        2,
        TOP + middle,
        tops,
    )
    clock.done(head_terms[0])
    head_ring = Scatter(ring, head_terms, TOP + middle, columns)
    sums[1].relay(clock)
    firsts = list(clock.tie(*firsts))
    head_ring.relay(clock)
    down_last = clock.tie(down_last)
    came = clock.tie(swap(clock.tie(grad_send), 1))
    last = swap(clock.tie(other_half(grad_keep, came)), 2)
    second_sum = sums[1].finish(clock)
    second_across, second_beside = swap(second_sum, 2), swap(second_sum, 1)
    head_ring.fork(clock)
    down_came = clock.tie(down_came)
    result = layer_output(hidden, down_keep, down_came, down_last, ring.slot_owners(), n_dp)
    clock.done(result)
    last, second_beside = clock.tie(last, second_beside)
    grad_input = first_norm_back(
        grad_hidden, mine, grad_keep, came, last, gains, ring.slot_owners(), n_dp
    )
    clock.done(grad_input)
    head_ring.relay_part(0, clock)
    head_ring.relay_part(1, clock)
    head_sums = [head_ring.finish_part(0, clock)]
    head_across = [swap(head_sums[0], 2)]
    second_across = clock.tie(second_across)
    others = four(second_sum, second_across, second_beside)
    head_sums.append(head_ring.finish_part(1, clock))
    head_across.append(swap(head_sums[1], 2))
    others = list(clock.tie(*others))
    grad_gate, grad_up, grad_down = unpack_mlp(places, [firsts, others], bounds, width, ff)
    clock.done(grad_gate)
    head_beside = [swap(part, 1) for part in head_sums]
    head_across = clock.tie(*head_across)
    head_blocks = [
        *head_sums, *head_across, *head_beside, *[swap(part, 1) for part in head_across]
    ]
    grad_query, grad_key, grad_value, grad_out, gain_sums = unpack_heads(
        places, list(clock.tie(*head_blocks)), width, q_cols
    )
    if width % 128:
        slots = ring.owner_slots()
        result = blocks_in_order(result, slots, n_dp)
        grad_input = blocks_in_order(grad_input, slots, n_dp)

    return (
        result,
        grad_input,
        gain_sums[0, :width],
        grad_query,
        grad_key,
        grad_value,
        grad_out,
        gain_sums[0, width:],
        grad_gate,
        grad_up,
        grad_down,
    )


def solution(mesh):
    return jax.shard_map(
        layer,
        mesh=mesh,
        in_specs=(
            P(("dp", "seq"), None),
            P(("dp", "seq"), None),
            P("dp"),
            P("dp", None),
            P("dp", None),
            P("dp", None),
            P(None, "dp"),
            P("dp"),
            P("dp", None),
            P("dp", None),
            P(None, "dp"),
            P("dp", None),
            P("dp"),
        ),
        out_specs=(
            P(("dp", "seq"), None),
            P(("dp", "seq"), None),
            P("dp"),
            P("dp", None),
            P("dp", None),
            P("dp", None),
            P(None, "dp"),
            P("dp"),
            P("dp", None),
            P("dp", None),
            P(None, "dp"),
        ),
        check_vma=False,
    )
```

```python
import functools

import jax
import jax.numpy as jnp
from jax import lax
from jax.experimental import pallas as pl
from jax.experimental.pallas import tpu as pltpu
from jax.sharding import PartitionSpec as P

HEADS = 32
HD = 64
KVH = 4
EPS = 1e-05
TOP = 8
BF = jnp.bfloat16
F32 = jnp.float32
NEG = -1e30
LIMITS = {
    "attention_forward": 23,
    "attention_backward": 18,
    "heads_back": 15,
    "mlp_chunk": 29,
    "mlp_chunk_far": 44,
    "weight_terms": 15,
    "unpack_mlp": 28,
    "unpack_heads": 12,
    "permute_features": 56,
    "pack_heads": 56,
    "pack_mlp": 56,
}


def limits(name):
    return pltpu.CompilerParams(vmem_limit_bytes=LIMITS.get(name, 12) << 20)


COST = pl.CostEstimate(flops=1000, transcendentals=0, bytes_accessed=1000)


def dot(left_side, right_side):
    return jnp.dot(left_side, right_side, preferred_element_type=F32)


def cross(left_side, right_side):
    return lax.dot_general(
        left_side, right_side, (((0,), (0,)), ((), ())), preferred_element_type=F32
    )


def against(left_side, right_side):
    return lax.dot_general(
        left_side, right_side, (((1,), (1,)), ((), ())), preferred_element_type=F32
    )


def kernel_call(body, outs, scratch=(), flops=0, moved=0, smem=0, args=(), name=None):
    vmem = pl.BlockSpec(memory_space=pltpu.VMEM)
    return pl.pallas_call(
        body,
        out_shape=tuple(jax.ShapeDtypeStruct(s, d) for s, d in outs),
        in_specs=[pl.BlockSpec(memory_space=pltpu.SMEM)] * smem + [vmem] * (len(args) - smem),
        out_specs=tuple(vmem for _ in outs),
        scratch_shapes=list(scratch),
        compiler_params=limits(name),
        cost_estimate=COST,
        name=name,
    )(*args)


class Ring:
    def __init__(self, size):
        self.size = size
        self.half = size // 2
        self.order = list(range(0, size, 2)) + list(range(size - 1, 0, -2))
        place = [0] * size
        for position, device in enumerate(self.order):
            place[device] = position
        self.place = place
        walk = [(self.order[i], self.order[(i + 1) % size]) for i in range(size)]
        self.up = walk
        self.down = [(b, a) for a, b in walk]
        self.steps = (
            [-t for t in range(self.half)] + [t for t in range(1, self.half)] + [self.half]
        )

    def slot_owners(self):
        mine = jnp.asarray(self.place, jnp.int32)[lax.axis_index("dp")]
        wanted = (mine + jnp.asarray(self.steps, jnp.int32)) % self.size
        return jnp.asarray(self.order, jnp.int32)[wanted]

    def owner_slots(self):
        mine = jnp.asarray(self.place, jnp.int32)[lax.axis_index("dp")]
        slot_of_step = [0] * self.size
        for slot, step in enumerate(self.steps):
            slot_of_step[step % self.size] = slot
        step = (jnp.asarray(self.place, jnp.int32) - mine) % self.size
        return jnp.asarray(slot_of_step, jnp.int32)[step]

    def go_up(self, block):
        return lax.ppermute(block, "dp", self.up)

    def go_down(self, block):
        return lax.ppermute(block, "dp", self.down)


class Clock:
    def __init__(self):
        self.last = None

    def tie(self, *arrays):
        if self.last is None:
            out = lax.optimization_barrier(arrays)
        else:
            out = lax.optimization_barrier((*arrays, self.last))[: len(arrays)]
        self.last = out[0]
        return out if len(out) > 1 else out[0]

    def done(self, array):
        self.last = array


class Gather:
    def __init__(self, ring, block, cut):
        self.ring, self.cut = ring, cut
        self.up, self.down = [block], [block]
        self.flying = (ring.go_up(block), ring.go_down(block))
        self.left = ring.half - 1

    def land(self, clock):
        up, down = clock.tie(*self.flying)
        self.flying = None
        self.up.append(up)
        self.down.append(down)

    def go(self, clock):
        up, down = clock.tie(self.up[-1], self.down[-1])
        self.left -= 1
        if self.left == 0:
            up, down = up[: self.cut], down[self.cut :]
        self.flying = (self.ring.go_up(up), self.ring.go_down(down))

    def relay(self, clock):
        if self.left == 0:
            return
        self.left -= 1
        up = clock.tie(self.flying[0])
        self.up.append(up)
        up = self.ring.go_up(up if self.left else up[: self.cut])
        down = clock.tie(self.flying[1])
        self.down.append(down)
        self.flying = (up, self.ring.go_down(down if self.left else down[self.cut :]))

    def finish(self, clock):
        while self.left:
            self.relay(clock)
        return self.up + self.down[1:] + list(clock.tie(*self.flying))


class Scatter:
    def __init__(self, ring, terms, cut, tile):
        self.ring, self.cut, self.tile = ring, cut, tile
        self.terms, up, down = terms
        self.full = self.terms.shape[0] // ring.size
        self.left = ring.half - 1
        self.flying = (ring.go_up(up), ring.go_down(down))

    def term(self, slot, begin=0, end=None):
        end = self.full if end is None else end
        return self.terms[slot * self.full + begin : slot * self.full + end]

    def land(self, clock):
        self.relay(clock, hold=True)

    def go(self, clock):
        up, down = clock.tie(*self.held)
        self.flying = (self.ring.go_up(up), self.ring.go_down(down))

    def relay(self, clock, hold=False):
        if self.left == 0:
            return
        above, below = self.ring.half - 1 + self.left, self.left
        self.left -= 1
        up, down = self.flying
        if up.shape[0] < self.full:
            up, down = clock.tie(up, down)
            self.held = ring_add(
                self.terms, (above, below), up, down, self.full, self.cut, self.tile
            )
            if not hold:
                self.go(clock)
            return
        up = self.ring.go_up(clock.tie(plus(self.term(above), clock.tie(up))))
        down = self.ring.go_down(clock.tie(plus(self.term(below), clock.tie(down))))
        self.flying = (up, down)

    def finish(self, clock):
        while self.left:
            self.relay(clock)
        up, down = clock.tie(*self.flying)
        return clock.tie(self.last(0, self.full, up, down))

    def last(self, begin, end, up, down):
        return (self.term(0, begin, end).astype(F32) + up.astype(F32) + down.astype(F32)).astype(BF)

    def fork(self, clock):
        while self.left > 2:
            self.relay(clock)
        up, down = clock.tie(*self.flying)
        self.rows = [(0, self.cut), (self.cut, self.full)]
        self.parts = []
        for begin, end in self.rows:
            self.parts.append(self.pass_on(2, begin, end, up[begin:end], down[begin:end], clock))

    def pass_on(self, left, begin, end, up, down, clock):
        up = plus(self.term(self.ring.half - 1 + left, begin, end), up)
        down = plus(self.term(left, begin, end), down)
        up, down = clock.tie(up, down)
        return self.ring.go_up(up), self.ring.go_down(down)

    def relay_part(self, part, clock):
        up, down = clock.tie(*self.parts[part])
        self.parts[part] = self.pass_on(1, *self.rows[part], up, down, clock)

    def finish_part(self, part, clock):
        up, down = clock.tie(*self.parts[part])
        return clock.tie(self.last(*self.rows[part], up, down))


def plus(one, two):
    return (one.astype(F32) + two.astype(F32)).astype(BF)


def swap(block, distance):
    return lax.ppermute(block, "seq", [(i, i ^ distance) for i in range(4)])


def fill_weights(pieces, scratch, top, width, columns):
    begin = 0
    for index, piece in enumerate(pieces):
        skip = top if index < len(pieces) - 1 else 0
        count = piece.shape[0] - skip
        scratch[begin : begin + count, :] = piece[skip:, columns]
        begin += count


def put_features(values, order_ref, target, slots, width):
    for j in range(slots):
        to = pl.ds(pl.multiple_of(order_ref[j] * width, 128), width)
        target[:, to] = values[:, j * width : (j + 1) * width]


def blocks_in_order(array, order, size):
    width = array.shape[1] // size
    return jnp.concatenate(
        [lax.dynamic_slice_in_dim(array, order[i] * width, width, 1) for i in range(size)],
        axis=1,
    )


def permute_features(array, order, size):
    width = array.shape[1] // size
    if width % 128:
        return blocks_in_order(array, order, size)

    def body(order_ref, source, target):
        for j in range(size):
            begin = pl.ds(pl.multiple_of(order_ref[j] * width, 128), width)
            target[:, j * width : (j + 1) * width] = source[:, begin]

    return kernel_call(
        body, [(array.shape, array.dtype)], smem=1, args=[order, array], name="permute_features"
    )[0]


def pack_heads(here, w_query, w_key, w_value, w_out, gain_attn, gain_mlp, seq):
    width = w_query.shape[0]
    q_cols, k_cols = w_query.shape[1] // seq, w_key.shape[1] // seq
    total = 2 * q_cols + 2 * k_cols

    def body(here_ref, query_ref, key_ref, value_ref, out_ref, one_ref, two_ref, block_ref):
        s = here_ref[0]
        block_ref[:TOP, :] = jnp.zeros((TOP, total), BF)
        block_ref[:1, :width] = one_ref[...].reshape(1, width)
        block_ref[:1, width : 2 * width] = two_ref[...].reshape(1, width)
        block_ref[TOP:, :q_cols] = query_ref[...]

        def mine(ref):
            part = jnp.zeros((width, k_cols), F32)
            for place in range(seq):
                piece = ref[:, place * k_cols : (place + 1) * k_cols].astype(F32)
                part = jnp.where(s == place, piece, part)
            return part

        both = jnp.concatenate([mine(key_ref), mine(value_ref)], axis=1)
        block_ref[TOP:, q_cols : q_cols + 2 * k_cols] = both.astype(BF)
        block_ref[TOP:, q_cols + 2 * k_cols :] = out_ref[...].astype(F32).T.astype(BF)

    whole = lambda shape: pl.BlockSpec(shape, lambda i, o: (0, 0))
    return pl.pallas_call(
        body,
        out_shape=jax.ShapeDtypeStruct((TOP + width, total), BF),
        grid_spec=pltpu.PrefetchScalarGridSpec(
            num_scalar_prefetch=1,
            grid=(1,),
            in_specs=[
                pl.BlockSpec((width, q_cols), lambda i, o: (0, o[0])),
                whole(w_key.shape),
                whole(w_value.shape),
                pl.BlockSpec((q_cols, width), lambda i, o: (o[0], 0)),
                pl.BlockSpec((width,), lambda i, o: (0,)),
                pl.BlockSpec((width,), lambda i, o: (0,)),
            ],
            out_specs=whole((TOP + width, total)),
        ),
        compiler_params=limits("pack_heads"),
        name="pack_heads",
    )(here, w_query, w_key, w_value, w_out, gain_attn, gain_mlp)


def pack_mlp(here, w_gate, w_up, w_down, bounds, seq):
    width, ff = w_gate.shape[0], w_gate.shape[1] // seq

    def body(here_ref, gate_ref, up_ref, down_ref, *blocks):
        for (a, b), block in zip(bounds, blocks):
            size = b - a
            block[:, :size] = gate_ref[:, a:b]
            block[:, size : 2 * size] = up_ref[:, a:b]
            block[:, 2 * size :] = down_ref[a:b, :].astype(F32).T.astype(BF)

    columns = pl.BlockSpec((width, ff), lambda i, o: (0, o[0]))
    return pl.pallas_call(
        body,
        out_shape=tuple(jax.ShapeDtypeStruct((width, 3 * (b - a)), BF) for a, b in bounds),
        grid_spec=pltpu.PrefetchScalarGridSpec(
            num_scalar_prefetch=1,
            grid=(1,),
            in_specs=[columns, columns, pl.BlockSpec((ff, width), lambda i, o: (o[0], 0))],
            out_specs=tuple(
                pl.BlockSpec((width, 3 * (b - a)), lambda i, o: (0, 0)) for a, b in bounds
            ),
        ),
        compiler_params=limits("pack_mlp"),
        name="pack_mlp",
    )(here, w_gate, w_up, w_down)


def turn(values, cosine, sine_part):
    half_dim = HD // 2
    pieces = []
    for h in range(values.shape[0] // HD):
        first = values[h * HD : h * HD + half_dim]
        second = values[h * HD + half_dim : (h + 1) * HD]
        pieces.append(first * cosine - second * sine_part)
        pieces.append(second * cosine + first * sine_part)
    return jnp.concatenate(pieces, axis=0)


def rounded(values):
    return values.astype(BF).astype(F32)


def pick(refs, place, target):
    rows = target.shape[0]
    at = 0
    for ref in refs:
        index, begin, count = at // rows, at % rows, ref.shape[0]
        at += count

        @pl.when(place == index)
        def _():
            target[begin : begin + count, :] = ref[...]


def write_bias(bias_ref, lengths_ref, live, block, rows):
    keys = (block + 1) * rows
    query = lax.broadcasted_iota(jnp.int32, (1, rows), 1) + block * rows
    low = jnp.zeros((1, rows), jnp.int32)
    start = 0
    for slot in range(lengths_ref.shape[0]):
        low = jnp.where(query >= start, jnp.maximum(low, start), low)
        start = start + lengths_ref[slot]
    high = jnp.minimum(query, live - 1)
    key = lax.broadcasted_iota(jnp.int32, (keys, rows), 0)
    allowed = ((key >= low) & (key <= high)) | (key == query)
    bias_ref[:keys, :] = jnp.where(allowed, 0.0, NEG)


def attention_forward(places, lengths, live, tokens, pieces, cosine, sine_part, q_cols):
    rows, model = tokens[0].shape
    pack_size = 4 * rows
    n_heads = q_cols // HD
    heads_cols = q_cols + 2 * HD
    width = pieces[0].shape[0] - TOP

    def body(places_ref, lengths_ref, live_ref, cos_ref, sin_ref, *refs):
        token_refs, piece_refs, refs = refs[:4], refs[4 : 4 + len(pieces)], refs[4 + len(pieces) :]
        (
            normed_ref, query_ref, kv_ref, kvt_ref, lse_ref, mixed_t_ref, mixed_ref, keep_ref,
            send_ref, gains_ref, w_ref, bias_ref, query_s, mixed_s, tokens_s,
        ) = refs
        live_count = live_ref[0]
        fill_weights(piece_refs, w_ref, TOP, width, slice(None))
        gains_ref[...] = jnp.zeros_like(gains_ref)
        for index, piece in enumerate(piece_refs[:-1]):
            at = slice(index * width, (index + 1) * width)
            gains_ref[0:1, at] = piece[0:1, :width].astype(F32)
            gains_ref[1:2, at] = piece[0:1, width : 2 * width].astype(F32)
        ones = jnp.ones((HD, rows), BF)
        for block in range(4):
            place = places_ref[block]
            at = slice(block * rows, (block + 1) * rows)
            keys = (block + 1) * rows
            to = pl.ds(pl.multiple_of(place * rows, rows), rows)
            pick(token_refs, place, tokens_s)
            inputs = tokens_s[...].astype(F32)
            inverse = lax.rsqrt(jnp.mean(inputs * inputs, axis=1, keepdims=True) + EPS)
            normed = (inputs * inverse * gains_ref[0:1, :]).astype(BF)
            normed_ref[to, :] = normed
            pre = dot(normed, w_ref[:, :heads_cols]).T
            cos_b, sin_b = cos_ref[:, at], sin_ref[:, at]
            query = (rounded(turn(pre[:q_cols], cos_b, sin_b)) * HD**-0.5).astype(BF)
            query_s[...] = query
            query_ref[:, at] = query
            key_t = rounded(turn(pre[q_cols : q_cols + HD], cos_b, sin_b))
            value_t = rounded(pre[q_cols + HD :])
            kv_t = jnp.concatenate([key_t, value_t], axis=0)
            kv_ref[at, :] = kv_t.T.astype(BF)
            kvt_ref[: 2 * HD, at] = kv_t.astype(BF)
            kvt_ref[2 * HD :, at] = ones
            write_bias(bias_ref, lengths_ref, live_count, block, rows)

            def attend(h, _):
                mine = pl.ds(pl.multiple_of(h * HD, HD), HD)
                scores = dot(kv_ref[:keys, :HD], query_s[mine, :]) + bias_ref[:keys, :]
                peak = jnp.max(scores, axis=0, keepdims=True)
                weights = jnp.exp(scores - peak).astype(BF)
                summed = dot(kvt_ref[HD:, :keys], weights)
                total = summed[HD : HD + 1]
                mixed = summed[:HD] * (1.0 / total)
                mixed_s[mine, :] = mixed
                lse_ref[pl.ds(h, 1), at] = peak + jnp.log(total)
                return 0

            lax.fori_loop(0, n_heads, attend, 0, unroll=2)
            mixed_t = mixed_s[...]
            mixed_t_ref[:, at] = mixed_t
            mixed = mixed_t.T.astype(BF)
            mixed_ref[to, :] = mixed
            branch = against(mixed, w_ref[:, heads_cols:]).astype(BF)
            half_to = pl.ds(pl.multiple_of((place % 2) * rows, rows), rows)

            @pl.when(place < 2)
            def _():
                keep_ref[half_to, :] = branch

            @pl.when(place >= 2)
            def _():
                send_ref[half_to, :] = branch

    args = [places, lengths, live, cosine, sine_part, *tokens, *pieces]
    flops = 2 * pack_size * model * (heads_cols + q_cols) + 4 * n_heads * pack_size**2 * HD * 3
    return kernel_call(
        body,
        [
            ((pack_size, model), BF),
            ((q_cols, pack_size), BF),
            ((pack_size, 2 * HD), BF),
            ((3 * HD, pack_size), BF),
            ((n_heads, pack_size), F32),
            ((q_cols, pack_size), F32),
            ((pack_size, q_cols), BF),
            ((pack_size // 2, model), BF),
            ((pack_size // 2, model), BF),
            ((8, model), F32),
        ],
        scratch=[
            pltpu.VMEM((model, heads_cols + q_cols), BF),
            pltpu.VMEM((pack_size, rows), F32),
            pltpu.VMEM((q_cols, rows), BF),
            pltpu.VMEM((q_cols, rows), F32),
            pltpu.VMEM((rows, model), BF),
        ],
        flops=flops,
        moved=30 << 20,
        smem=3,
        args=args,
        name="attention_forward",
    )


def attention_backward(
    places, lengths, live, tokens, pieces, cosine, sine_part, query, kv, kvt, lse, mixed_t
):
    q_cols, pack_size = query.shape
    rows, model = tokens[0].shape
    n_heads = q_cols // HD
    heads_cols = q_cols + 2 * HD
    width = pieces[0].shape[0] - TOP

    def body(
        places_ref, lengths_ref, live_ref, cos_ref, sin_ref,
        query_ref, kv_ref, kvt_ref, lse_ref, mixed_t_ref, *refs
    ):
        token_refs, piece_refs, refs = refs[:4], refs[4 : 4 + len(pieces)], refs[4 + len(pieces) :]
        (
            grad_q_ref, grad_kv_ref, w_ref, bias_ref, grad_s, grad_q_s, key_acc, value_acc, inner_s,
            tokens_s,
        ) = refs
        live_count = live_ref[0]
        fill_weights(piece_refs, w_ref, TOP, width, slice(heads_cols, heads_cols + q_cols))
        key_acc[...] = jnp.zeros_like(key_acc)
        value_acc[...] = jnp.zeros_like(value_acc)
        for block in range(4):
            place = places_ref[block]
            at = slice(block * rows, (block + 1) * rows)
            keys = (block + 1) * rows
            to = pl.ds(pl.multiple_of(place * rows, rows), rows)
            pick(token_refs, place, tokens_s)
            grad_t = rounded(dot(tokens_s[...], w_ref[...]).T)
            grad_s[...] = grad_t.astype(BF)
            product = grad_t * mixed_t_ref[:, at]
            for h in range(n_heads):
                inner_s[h : h + 1, :] = jnp.sum(
                    product[h * HD : (h + 1) * HD], axis=0, keepdims=True
                )
            write_bias(bias_ref, lengths_ref, live_count, block, rows)

            def attend(h, _):
                mine = pl.ds(pl.multiple_of(h * HD, HD), HD)
                query_h = query_ref[mine, at]
                grad_h = grad_s[mine, :]
                scores = dot(kv_ref[:keys, :HD], query_h) + bias_ref[:keys, :]
                probs = jnp.exp(scores - lse_ref[pl.ds(h, 1), at])
                grad_probs = dot(kv_ref[:keys, HD:], grad_h)
                grad_scores = (probs * (grad_probs - inner_s[pl.ds(h, 1), :])).astype(BF)
                grad_q_s[mine, :] = dot(kvt_ref[:HD, :keys], grad_scores) * HD**-0.5
                key_acc[:keys, :] += against(grad_scores, query_h)
                value_acc[:keys, :] += against(probs.astype(BF), grad_h)
                return 0

            lax.fori_loop(0, n_heads, attend, 0, unroll=8)
            turned = turn(rounded(grad_q_s[...]), cos_ref[:, at], -sin_ref[:, at])
            grad_q_ref[to, :] = turned.T.astype(BF)
        for block in range(4):
            at = slice(block * rows, (block + 1) * rows)
            to = pl.ds(pl.multiple_of(places_ref[block] * rows, rows), rows)
            key_t = turn(rounded(key_acc[at, :]).T, cos_ref[:, at], -sin_ref[:, at])
            grad_kv_ref[to, :] = jnp.concatenate([key_t.T, value_acc[at, :]], axis=1).astype(BF)

    args = [
        places, lengths, live, cosine, sine_part, query, kv, kvt, lse, mixed_t, *tokens, *pieces
    ]
    return kernel_call(
        body,
        [((pack_size, q_cols), BF), ((pack_size, 2 * HD), BF)],
        scratch=[
            pltpu.VMEM((model, q_cols), BF),
            pltpu.VMEM((pack_size, rows), F32),
            pltpu.VMEM((q_cols, rows), BF),
            pltpu.VMEM((q_cols, rows), F32),
            pltpu.VMEM((pack_size, HD), F32),
            pltpu.VMEM((pack_size, HD), F32),
            pltpu.VMEM((n_heads, rows), F32),
            pltpu.VMEM((rows, model), BF),
        ],
        flops=2 * pack_size * model * q_cols + 10 * n_heads * pack_size**2 * HD * 3,
        moved=20 << 20,
        smem=3,
        args=args,
        name="attention_backward",
    )


def heads_back(grad_q, grad_kv, tokens, pieces):
    pack_size, q_cols = grad_q.shape
    rows, model = tokens[0].shape
    heads_cols = q_cols + 2 * HD
    width = pieces[0].shape[0] - TOP

    def body(grad_q_ref, grad_kv_ref, *refs):
        token_refs, piece_refs = refs[:4], refs[4 : 4 + len(pieces)]
        keep_ref, send_ref, gain_ref, w_ref, tokens_s = refs[4 + len(pieces) :]
        step = pl.program_id(0)

        @pl.when(step == 0)
        def _():
            fill_weights(piece_refs, w_ref, TOP, width, slice(0, heads_cols))
            gain_ref[...] = jnp.zeros_like(gain_ref)

        pick(token_refs, step, tokens_s)
        inputs = tokens_s[...].astype(F32)
        inverse = lax.rsqrt(jnp.mean(inputs * inputs, axis=1, keepdims=True) + EPS)
        grad = against(grad_q_ref[...], w_ref[:, :q_cols]) + against(
            grad_kv_ref[...], w_ref[:, q_cols:]
        )

        @pl.when(step < 2)
        def _():
            keep_ref[...] = grad.astype(BF)

        @pl.when(step >= 2)
        def _():
            send_ref[...] = grad.astype(BF)

        total = jnp.sum(grad * inputs * inverse, axis=0, keepdims=True)
        gain_ref[...] += jnp.broadcast_to(total, gain_ref.shape)

    first = pl.BlockSpec((rows, model), lambda i: (jnp.minimum(i, 1), 0))
    second = pl.BlockSpec((rows, model), lambda i: (jnp.maximum(i - 2, 0), 0))
    fixed = lambda a: pl.BlockSpec(memory_space=pltpu.VMEM)
    half = jax.ShapeDtypeStruct((pack_size // 2, model), BF)
    return pl.pallas_call(
        body,
        grid=(4,),
        out_shape=(half, half, jax.ShapeDtypeStruct((8, model), F32)),
        in_specs=[
            pl.BlockSpec((rows, q_cols), lambda i: (i, 0)),
            pl.BlockSpec((rows, 2 * HD), lambda i: (i, 0)),
        ]
        + [fixed(a) for a in (*tokens, *pieces)],
        out_specs=(first, second, pl.BlockSpec((8, model), lambda i: (0, 0))),
        scratch_shapes=[pltpu.VMEM((model, heads_cols), BF), pltpu.VMEM((rows, model), BF)],
        compiler_params=limits("heads_back"),
        cost_estimate=COST,
        name="heads_back",
    )(grad_q, grad_kv, *tokens, *pieces)


def mlp_chunk(tokens, cots, pieces, before, size, room):
    rows, model = tokens[0].shape
    pack_size = 4 * rows

    def body(*refs):
        token_refs, cot_refs, refs = refs[:4], refs[4:8], refs[8:]
        piece_refs, refs = refs[: len(pieces)], refs[len(pieces) :]
        before_refs, refs = refs[: len(before)], refs[len(before) :]
        down_keep, down_send, grad_keep, grad_send, both_ref, w_ref, tokens_s, cot_s = refs
        step = pl.program_id(0)

        @pl.when(step == 0)
        def _():
            fill_weights(piece_refs, w_ref, 0, model, slice(None))

        pick(token_refs, step, tokens_s)
        pick(cot_refs, step, cot_s)
        both = dot(tokens_s[...], w_ref[:, : 2 * size])
        grad_act = dot(cot_s[...], w_ref[:, 2 * size :])
        gate_pre, up_pre = both[:, :size], both[:, size:]
        sig = 1.0 / (1.0 + jnp.exp(-gate_pre))
        active = gate_pre * sig
        both_ref[:, 2 * size :] = (active * up_pre).astype(BF)
        both_ref[:, size : 2 * size] = (grad_act * active).astype(BF)
        both_ref[:, :size] = (grad_act * up_pre * (sig + active * (1.0 - sig))).astype(BF)
        down = against(both_ref[:, 2 * size :], w_ref[:, 2 * size :])
        grad = against(both_ref[:, : 2 * size], w_ref[:, : 2 * size])

        def put(keep, send, value, keep_before, send_before):
            @pl.when(step < 2)
            def _():
                extra = 0.0 if keep_before is None else keep_before[...].astype(F32)
                keep[...] = (value + extra).astype(BF)

            @pl.when(step >= 2)
            def _():
                extra = 0.0 if send_before is None else send_before[...].astype(F32)
                send[...] = (value + extra).astype(BF)

        old = before_refs or [None] * 4
        put(down_keep, down_send, down, old[0], old[1])
        put(grad_keep, grad_send, grad, old[2], old[3])

    first = pl.BlockSpec((rows, model), lambda i: (jnp.minimum(i, 1), 0))
    second = pl.BlockSpec((rows, model), lambda i: (jnp.maximum(i - 2, 0), 0))
    fixed = pl.BlockSpec(memory_space=pltpu.VMEM)
    half = pltpu.HBM((pack_size // 2, model), BF)
    return pl.pallas_call(
        body,
        grid=(4,),
        out_shape=(half, half, half, half, pltpu.HBM((pack_size, 3 * size), BF)),
        in_specs=[fixed] * (8 + len(pieces)) + [first, second] * (len(before) // 2),
        out_specs=(first, second, first, second, pl.BlockSpec((rows, 3 * size), lambda i: (i, 0))),
        scratch_shapes=[
            pltpu.VMEM((model, 3 * size), BF),
            pltpu.VMEM((rows, model), BF),
            pltpu.VMEM((rows, model), BF),
        ],
        compiler_params=limits(room),
        cost_estimate=COST,
        name="mlp_chunk",
    )(*tokens, *cots, *pieces, *before)


def weight_terms(pairs, width, n_slots, group, cut, tops=None):
    tokens = sum(x.shape[0] for x in pairs[0][0])
    total = sum(cols.stop - cols.start for _, _, cols in pairs)
    head = 0 if tops is None else TOP

    def distinct(lists):
        out = []
        for one in lists:
            if not any(one is other for other in out):
                out.append(one)
        return out

    x_lists = distinct(x for x, _, _ in pairs)
    g_lists = distinct(g for _, g, _ in pairs)
    while (width * group) % 128:
        group *= 2
    wide = width * group
    args, specs = [], []
    for x in [x for xs in x_lists for x in xs]:
        args.append(x)
        specs.append(pl.BlockSpec((x.shape[0], wide), lambda i: (0, i)))
    for g in [g for gs in g_lists for g in gs]:
        args.append(g)
        specs.append(pl.BlockSpec(memory_space=pltpu.VMEM))
    if head:
        args.append(tops)
        specs.append(pl.BlockSpec((group * TOP, total), lambda i: (i, 0)))

    def body(*refs):
        def take(lists):
            nonlocal refs
            out = []
            for one in lists:
                out.append((one, refs[: len(one)]))
                refs = refs[len(one) :]
            return out

        x_refs, g_refs = take(x_lists), take(g_lists)
        out_ref, up_ref, down_ref, x_s = refs[-4:]
        lane = 0
        filled = None
        for xs, gs, cols in pairs:
            parts = next(r for other, r in x_refs if other is xs)
            g_parts = next(r for other, r in g_refs if other is gs)
            if len(parts) > 1 and filled is not xs:
                at = 0
                for part in parts:
                    x_s[at : at + part.shape[0], :] = part[...]
                    at += part.shape[0]
                filled = xs
            product, at = None, 0
            for g in g_parts:
                rows = g.shape[0]
                x = (x_s if len(parts) > 1 else parts[0])[at : at + rows, :]
                at += rows
                more = cross(x, g[:, cols])
                product = more if product is None else product + more
            product = product.astype(BF)
            count = cols.stop - cols.start
            for j in range(group):
                at = j * (head + width) + head
                out_ref[at : at + width, lane : lane + count] = product[
                    j * width : (j + 1) * width
                ]
            lane += count
        if head:
            for j in range(group):
                at = j * (head + width)
                out_ref[at : at + head, :] = refs[0][j * TOP : (j + 1) * TOP, :]

        @pl.when(pl.program_id(0) == n_slots // group - 1)
        def _():
            begin = (group - 1) * (head + width)
            up_ref[...] = out_ref[begin : begin + cut, :]
            down_ref[...] = out_ref[begin + cut : begin + head + width, :]

    far = [(cut, total), (head + width - cut, total)]
    return pl.pallas_call(
        body,
        grid=(n_slots // group,),
        out_shape=(
            jax.ShapeDtypeStruct((n_slots * (head + width), total), BF),
            *[jax.ShapeDtypeStruct(shape, BF) for shape in far],
        ),
        in_specs=specs,
        out_specs=(
            pl.BlockSpec((group * (head + width), total), lambda i: (i, 0)),
            *[pl.BlockSpec(shape, lambda i: (0, 0)) for shape in far],
        ),
        scratch_shapes=[pltpu.VMEM((tokens, wide), BF)],
        compiler_params=limits("weight_terms"),
        cost_estimate=COST,
        name="weight_terms",
    )(*args)


def ring_add(terms, slots, up, down, full, cut, tile):
    total = terms.shape[1]

    def body(up_term, down_term, up_ref, down_ref, up_out, down_out):
        if up_ref.shape[0] == full:
            up_out[...] = (up_term[...].astype(F32) + up_ref[...].astype(F32)).astype(BF)
            down_out[...] = (down_term[...].astype(F32) + down_ref[...].astype(F32)).astype(BF)
        else:
            up_out[:cut, :] = (up_term[:cut, :].astype(F32) + up_ref[...].astype(F32)).astype(BF)
            up_out[cut:, :] = up_term[cut:, :]
            down_out[:cut, :] = down_term[:cut, :]
            down_out[cut:, :] = (
                down_term[cut:, :].astype(F32) + down_ref[...].astype(F32)
            ).astype(BF)

    columns = lambda array: pl.BlockSpec((array.shape[0], tile), lambda i: (0, i))
    out = jax.ShapeDtypeStruct((full, total), BF)
    return pl.pallas_call(
        body,
        grid=(total // tile,),
        out_shape=(out, out),
        in_specs=[
            pl.BlockSpec((full, tile), lambda i: (slots[0], i)),
            pl.BlockSpec((full, tile), lambda i: (slots[1], i)),
            columns(up),
            columns(down),
        ],
        out_specs=(columns(out), columns(out)),
        compiler_params=limits("ring_add"),
        cost_estimate=COST,
        name="ring_add",
    )(terms, terms, up, down)


def row_call(body, outs, row_args, fixed_args, steps, smem=(), name=None):
    rows = outs[0][0][0] if outs[0][2] else row_args[0][0].shape[0]
    tile = rows // steps
    n_smem = len(smem)
    by_rows = lambda cols, at: pl.BlockSpec((tile, cols), lambda i, *_: (i + at, 0))
    return pl.pallas_call(
        body,
        out_shape=tuple(jax.ShapeDtypeStruct(s, d) for s, d, _ in outs),
        grid_spec=pltpu.PrefetchScalarGridSpec(
            num_scalar_prefetch=n_smem,
            grid=(steps,),
            in_specs=[by_rows(a.shape[1], at * steps) for a, at in row_args]
            + [pl.BlockSpec(a.shape, lambda i, *_: (0, 0)) for a in fixed_args],
            out_specs=tuple(
                by_rows(s[1], 0) if split else pl.BlockSpec(s, lambda i, *_: (0, 0))
                for s, _, split in outs
            ),
        ),
        compiler_params=limits(name),
        cost_estimate=COST,
        name=name,
    )(*smem, *[a for a, _ in row_args], *fixed_args)


STEPS = 2


def second_norm(inputs, keep, came, last, gains):
    def body(inputs_ref, keep_ref, came_ref, last_ref, gains_ref, hidden_ref, normed_ref):
        branch = keep_ref[...].astype(F32) + came_ref[...].astype(F32) + last_ref[...].astype(F32)
        hidden = inputs_ref[...].astype(F32) + branch
        inverse = lax.rsqrt(jnp.mean(hidden * hidden, axis=1, keepdims=True) + EPS)
        hidden_ref[...] = hidden
        normed_ref[...] = (hidden * inverse * gains_ref[1:2, :]).astype(BF)

    return row_call(
        body,
        [(inputs.shape, F32, True), (inputs.shape, BF, True)],
        [(inputs, 0), (keep, 0), (came, 0), (last, 0)],
        [gains],
        STEPS,
        name="second_norm",
    )


def norm_back(grad, values, gain):
    inverse = lax.rsqrt(jnp.mean(values * values, axis=1, keepdims=True) + EPS)
    scaled = grad * gain
    mean = jnp.mean(scaled * values, axis=1, keepdims=True)
    return inverse, inverse * (scaled - values * (inverse * inverse * mean))


def second_norm_back(cot, hidden, keep, came, last, gains):
    rows, model = hidden.shape

    def body(cot_ref, hidden_ref, keep_ref, came_ref, last_ref, gains_ref, grad_ref, low_ref, gain_ref):
        @pl.when(pl.program_id(0) == 0)
        def _():
            gain_ref[...] = jnp.zeros_like(gain_ref)

        grad = keep_ref[...].astype(F32) + came_ref[...].astype(F32) + last_ref[...].astype(F32)
        hidden_v = hidden_ref[...]
        inverse, back = norm_back(grad, hidden_v, gains_ref[1:2, :])
        total = jnp.sum(grad * hidden_v * inverse, axis=0, keepdims=True)
        gain_ref[...] += jnp.broadcast_to(total, gain_ref.shape)
        out = cot_ref[...].astype(F32) + back
        grad_ref[...] = out
        low_ref[...] = out.astype(BF)

    return row_call(
        body,
        [((rows, model), F32, True), ((rows, model), BF, True), ((8, model), F32, False)],
        [(cot, 0), (hidden, 0), (keep, 0), (came, 0), (last, 0)],
        [gains],
        STEPS,
        name="second_norm_back",
    )


def first_norm_back(grad_hidden, inputs, keep, came, last, gains, order, n_slots):
    width = inputs.shape[1] // n_slots

    def body(order_ref, grad_ref, inputs_ref, keep_ref, came_ref, last_ref, gains_ref, out_ref):
        grad = keep_ref[...].astype(F32) + came_ref[...].astype(F32) + last_ref[...].astype(F32)
        _, back = norm_back(grad, inputs_ref[...].astype(F32), gains_ref[0:1, :])
        out = (grad_ref[...] + back).astype(BF)
        if width % 128:
            out_ref[...] = out
        else:
            put_features(out, order_ref, out_ref, n_slots, width)

    return row_call(
        body,
        [(inputs.shape, BF, True)],
        [(grad_hidden, 0), (inputs, 0), (keep, 0), (came, 0), (last, 0)],
        [gains],
        STEPS,
        smem=(order,),
        name="first_norm_back",
    )[0]


def layer_output(hidden, keep, came, last, order, n_slots):
    width = hidden.shape[1] // n_slots

    def body(order_ref, hidden_ref, keep_ref, came_ref, last_ref, out_ref):
        down = keep_ref[...].astype(F32) + came_ref[...].astype(F32) + last_ref[...].astype(F32)
        out = (hidden_ref[...] + down).astype(BF)
        if width % 128:
            out_ref[...] = out
        else:
            put_features(out, order_ref, out_ref, n_slots, width)

    return row_call(
        body,
        [(hidden.shape, BF, True)],
        [(hidden, 0), (keep, 0), (came, 0), (last, 0)],
        [],
        STEPS,
        smem=(order,),
        name="layer_output",
    )[0]


def unpack_mlp(places, chunks, bounds, width, ff):
    flat = [block for blocks in chunks for block in blocks]

    def body(places_ref, *refs):
        ins = refs[: len(flat)]
        gate_ref, up_ref, down_ref = refs[len(flat) : len(flat) + 3]
        scratches = refs[len(flat) + 3 :]
        place = places_ref[pl.program_id(0)]
        for c, (a, b) in enumerate(bounds):
            size = b - a
            block_s = scratches[c]
            pick(ins[4 * c : 4 * c + 4], place, block_s)
            gate_ref[:, a:b] = block_s[:, :size].astype(F32)
            up_ref[:, a:b] = block_s[:, size : 2 * size].astype(F32)
            down_ref[a:b, :] = block_s[:, 2 * size :].astype(F32).T

    columns = pl.BlockSpec((width, ff), lambda i, p: (0, i))
    return pl.pallas_call(
        body,
        out_shape=(
            jax.ShapeDtypeStruct((width, 4 * ff), F32),
            jax.ShapeDtypeStruct((width, 4 * ff), F32),
            jax.ShapeDtypeStruct((4 * ff, width), F32),
        ),
        grid_spec=pltpu.PrefetchScalarGridSpec(
            num_scalar_prefetch=1,
            grid=(4,),
            in_specs=[
                pl.BlockSpec(h.shape, lambda i, p: (0, 0), pipeline_mode=pl.Buffered(1))
                for h in flat
            ],
            out_specs=(columns, columns, pl.BlockSpec((ff, width), lambda i, p: (i, 0))),
            scratch_shapes=[pltpu.VMEM((width, 3 * (b - a)), BF) for a, b in bounds],
        ),
        compiler_params=limits("unpack_mlp"),
        cost_estimate=COST,
        name="unpack_mlp",
    )(places, *flat)


def unpack_heads(places, heads, width, q_cols):
    kv = q_cols + 2 * HD

    def body(places_ref, *refs):
        head_refs = refs[: len(heads)]
        query_ref, key_ref, value_ref, out_ref, gain_ref, head_s = refs[len(heads) :]
        gain = jnp.zeros((8, 2 * width), F32)
        for place in range(4):
            pick(head_refs, places_ref[place], head_s)
            gain = gain + head_s[:TOP, : 2 * width].astype(F32)[:8]
            at = slice(place * q_cols, (place + 1) * q_cols)
            query_ref[:, at] = head_s[TOP:, :q_cols].astype(F32)
            both = head_s[TOP:, q_cols:kv].astype(F32)
            key_ref[:, place * HD : (place + 1) * HD] = both[:, :HD]
            value_ref[:, place * HD : (place + 1) * HD] = both[:, HD:]
            out_ref[at, :] = head_s[TOP:, kv:].astype(F32).T
        gain_ref[...] = gain

    args = [places, *heads]
    return kernel_call(
        body,
        [
            ((width, 4 * q_cols), F32),
            ((width, 4 * HD), F32),
            ((width, 4 * HD), F32),
            ((4 * q_cols, width), F32),
            ((8, 2 * width), F32),
        ],
        scratch=[pltpu.VMEM((TOP + width, heads[0].shape[1]), BF)],
        smem=1,
        args=args,
        name="unpack_heads",
    )


def doc_positions(lengths, pack_size):
    doc_starts = jnp.cumsum(lengths) - lengths
    places = jnp.arange(pack_size, dtype=jnp.int32)
    doc_first = jnp.max(
        jnp.where(places[:, None] >= doc_starts[None, :], doc_starts[None, :], 0), axis=1
    )
    return places - doc_first


def rotary_tables(positions):
    half_dim = HD // 2
    frequency = 10000.0 ** (-2.0 * jnp.arange(half_dim, dtype=F32) / HD)
    angle_table = frequency[:, None] * positions.astype(F32)[None, :]
    return (jnp.cos(angle_table), jnp.sin(angle_table))


def layer(
    hidden_in,
    cotangent,
    gain_attn,
    w_query,
    w_key,
    w_value,
    w_out,
    gain_mlp,
    w_gate,
    w_up,
    w_down,
    doc_lengths,
    valid_count,
):
    seq = lax.axis_size("seq")
    n_dp = lax.axis_size("dp")
    here = lax.axis_index("seq").astype(jnp.int32)
    ring = Ring(n_dp)
    rows, model = hidden_in.shape
    pack_size = rows * seq
    width = gain_attn.shape[0]
    q_cols = w_query.shape[1] // seq
    ff = w_gate.shape[1] // seq
    here_1 = here.reshape(1)
    lengths, live = doc_lengths[0], valid_count[:1]
    middle = width // 2

    offset = here ^ jnp.arange(4, dtype=jnp.int32)
    places = (offset % 2) * 2 + offset // 2

    first = (ff // 2 + 127) // 128 * 128
    bounds = [(0, first), (first, ff)]
    sizes = [b - a for a, b in bounds]

    def other_half(keep, came):
        return plus(keep[rows:], came[rows:])

    def far_memory(*arrays):
        return [pltpu.with_memory_space_constraint(a, pltpu.HBM) for a in arrays]

    def four(block, across, beside):
        return [block, across, beside, swap(across, 1)]

    clock = Clock()
    head_block = pack_heads(here_1, w_query, w_key, w_value, w_out, gain_attn, gain_mlp, seq)
    clock.done(head_block)
    heads = Gather(ring, head_block, TOP + middle)
    hidden_in, cotangent = clock.tie(hidden_in, cotangent)
    mine = permute_features(hidden_in, ring.slot_owners(), n_dp)
    clock.done(mine)
    across, beside = swap(mine, 2), swap(mine, 1)
    w_gate, w_up, w_down, cotangent = clock.tie(w_gate, w_up, w_down, cotangent)
    blocks = pack_mlp(here_1, w_gate, w_up, w_down, bounds, seq)
    clock.done(blocks[0])
    heads.relay(clock)
    cotangent = clock.tie(cotangent)
    my_cot = permute_features(cotangent, ring.slot_owners(), n_dp)
    cosine, sine_part = rotary_tables(doc_positions(lengths, pack_size))
    cosine, sine_part, my_cot = clock.tie(cosine, sine_part, my_cot)
    heads.relay(clock)
    across, my_cot = clock.tie(across, my_cot)
    tokens = four(mine, across, beside)
    cot_across, cot_beside = swap(my_cot, 2), swap(my_cot, 1)
    heads.relay(clock)
    head_pieces = heads.finish(clock)
    tokens = list(clock.tie(*tokens))
    blocks = clock.tie(*blocks)
    chunks = [Gather(ring, block, middle) for block in blocks]
    normed, query, kv, kvt, lse, mixed_t, mixed, keep, send, gains = attention_forward(
        places, lengths, live, tokens, head_pieces, cosine, sine_part, q_cols
    )
    normed, query, kv, kvt, mixed_t, mixed = far_memory(normed, query, kv, kvt, mixed_t, mixed)
    clock.done(lse)
    chunks[0].relay(clock)
    chunks[1].land(clock)
    cot_across, send = clock.tie(cot_across, send)
    came = clock.tie(swap(send, 1))
    last = swap(clock.tie(other_half(keep, came)), 2)
    cots = four(my_cot, cot_across, cot_beside)
    chunks[0].relay(clock)
    last = clock.tie(last)
    hidden, my_normed = second_norm(mine, keep, came, last, gains)
    clock.done(my_normed)
    across, beside = swap(my_normed, 2), swap(my_normed, 1)
    beside = clock.tie(beside)
    chunks[0].relay(clock)
    across = clock.tie(across)
    seconds = four(my_normed, across, beside)
    pieces = chunks[0].finish(clock)
    chunks[1].go(clock)
    seconds = list(clock.tie(*seconds))
    cots = list(clock.tie(*cots))

    def terms_of(both, size):
        return weight_terms(
            [(seconds, [both], slice(0, 2 * size)), (cots, [both], slice(2 * size, 3 * size))],
            width,
            n_dp,
            2,
            middle,
        )

    *before, both = mlp_chunk(seconds, cots, pieces, (), sizes[0], "mlp_chunk")
    clock.done(both)
    chunks[1].relay(clock)
    terms = terms_of(clock.tie(both), sizes[0])
    clock.done(terms[0])
    sums = [Scatter(ring, terms, middle, sizes[0])]
    chunks[1].relay(clock)
    sums[0].land(clock)
    pieces = far_memory(*chunks[1].finish(clock))
    sums[0].go(clock)
    down_keep, down_send, grad_keep, grad_send, both = mlp_chunk(
        seconds, cots, clock.tie(*pieces), before, sizes[1], "mlp_chunk_far"
    )
    clock.done(both)
    sums[0].relay(clock)
    grad_send, down_send = clock.tie(grad_send, down_send)
    came, down_came = swap(grad_send, 1), swap(down_send, 1)
    came = clock.tie(came)
    last = swap(clock.tie(other_half(grad_keep, came)), 2)
    terms = terms_of(clock.tie(both), sizes[1])
    clock.done(terms[0])
    sums.append(Scatter(ring, terms, middle, sizes[1]))
    down_came = clock.tie(down_came)
    sums[0].relay(clock)
    sums[1].relay(clock)
    last = clock.tie(last)
    grad_hidden, my_branch, gain_two_terms = second_norm_back(
        my_cot, hidden, grad_keep, came, last, gains
    )
    clock.done(my_branch)
    across, beside = swap(my_branch, 2), swap(my_branch, 1)
    down_other = clock.tie(other_half(down_keep, down_came))
    beside = clock.tie(beside)
    chunk_sum = sums[0].finish(clock)
    chunk_across, chunk_beside = swap(chunk_sum, 2), swap(chunk_sum, 1)
    across = clock.tie(across)
    branches = four(my_branch, across, beside)
    branches = list(clock.tie(*branches))
    grad_q, grad_kv = attention_backward(
        places, lengths, live, branches, head_pieces, cosine, sine_part,
        query, kv, kvt, lse, mixed_t
    )
    clock.done(grad_kv)
    sums[1].relay(clock)
    chunk_across, chunk_beside = clock.tie(chunk_across, chunk_beside)
    firsts = four(chunk_sum, chunk_across, chunk_beside)
    down_last = swap(clock.tie(down_other), 2)
    tokens = clock.tie(*tokens)
    grad_keep, grad_send, gain_one_terms = heads_back(grad_q, grad_kv, tokens, head_pieces)
    clock.done(gain_one_terms)
    columns = head_block.shape[1]
    tops = jnp.concatenate(
        [
            gain_one_terms[0].reshape(n_dp, width),
            gain_two_terms[0].reshape(n_dp, width),
            jnp.zeros((n_dp, columns - 2 * width), F32),
        ],
        axis=1,
    ).astype(BF)
    tops = jnp.pad(tops[:, None], ((0, 0), (0, TOP - 1), (0, 0))).reshape(n_dp * TOP, -1)
    normed, tops = clock.tie(normed, tops)
    normed = [normed]
    head_terms = weight_terms(
        [
            (normed, [grad_q], slice(0, q_cols)),
            (normed, [grad_kv], slice(0, 2 * HD)),
            (branches, [mixed], slice(0, q_cols)),
        ],
        width,
        n_dp,
        2,
        TOP + middle,
        tops,
    )
    clock.done(head_terms[0])
    head_ring = Scatter(ring, head_terms, TOP + middle, columns)
    sums[1].relay(clock)
    firsts = list(clock.tie(*firsts))
    head_ring.relay(clock)
    down_last = clock.tie(down_last)
    came = clock.tie(swap(clock.tie(grad_send), 1))
    last = swap(clock.tie(other_half(grad_keep, came)), 2)
    second_sum = sums[1].finish(clock)
    second_across, second_beside = swap(second_sum, 2), swap(second_sum, 1)
    down_came = clock.tie(down_came)
    result = layer_output(hidden, down_keep, down_came, down_last, ring.slot_owners(), n_dp)
    clock.done(result)
    head_ring.fork(clock)
    last, second_beside = clock.tie(last, second_beside)
    grad_input = first_norm_back(
        grad_hidden, mine, grad_keep, came, last, gains, ring.slot_owners(), n_dp
    )
    clock.done(grad_input)
    head_ring.relay_part(0, clock)
    head_ring.relay_part(1, clock)
    head_sums = [head_ring.finish_part(0, clock)]
    head_across = [swap(head_sums[0], 2)]
    second_across = clock.tie(second_across)
    others = four(second_sum, second_across, second_beside)
    head_sums.append(head_ring.finish_part(1, clock))
    head_across.append(swap(head_sums[1], 2))
    others = list(clock.tie(*others))
    grad_gate, grad_up, grad_down = unpack_mlp(places, [firsts, others], bounds, width, ff)
    clock.done(grad_gate)
    head_beside = [swap(part, 1) for part in head_sums]
    head_across = clock.tie(*head_across)
    head_blocks = [
        *head_sums, *head_across, *head_beside, *[swap(part, 1) for part in head_across]
    ]
    grad_query, grad_key, grad_value, grad_out, gain_sums = unpack_heads(
        places, list(clock.tie(*head_blocks)), width, q_cols
    )
    if width % 128:
        slots = ring.owner_slots()
        result = blocks_in_order(result, slots, n_dp)
        grad_input = blocks_in_order(grad_input, slots, n_dp)

    return (
        result,
        grad_input,
        gain_sums[0, :width],
        grad_query,
        grad_key,
        grad_value,
        grad_out,
        gain_sums[0, width:],
        grad_gate,
        grad_up,
        grad_down,
    )


def solution(mesh):
    return jax.shard_map(
        layer,
        mesh=mesh,
        in_specs=(
            P(("dp", "seq"), None),
            P(("dp", "seq"), None),
            P("dp"),
            P("dp", None),
            P("dp", None),
            P("dp", None),
            P(None, "dp"),
            P("dp"),
            P("dp", None),
            P("dp", None),
            P(None, "dp"),
            P("dp", None),
            P("dp"),
        ),
        out_specs=(
            P(("dp", "seq"), None),
            P(("dp", "seq"), None),
            P("dp"),
            P("dp", None),
            P("dp", None),
            P("dp", None),
            P(None, "dp"),
            P("dp"),
            P("dp", None),
            P("dp", None),
            P(None, "dp"),
        ),
        check_vma=False,
    )
```
